32 devices in a mesh: seq: 8 (over y, x, core), wshard: 4 (over z).
Axes of the slice: x: 2, y: 2, z: 4, core: 2. Of those that a mesh axis runs over, the one named last changes fastest.
Arguments:
- tokens: bfloat16 [8, 1024, 2048], P('wshard', 'seq')
- starts: int32 [8, 1024], P('wshard'), may hold values 0 or 1
- layer_index: int32 [1], replicated, may hold values from 0 to 23
- gain_mix: float32 [2048], replicated, may hold values from 0.5 to 1.5
- w_in: bfloat16 [2048, 2048], P('wshard'), may hold values from -0.125 to 0.125
- w_forget: bfloat16 [2048, 1024], P('wshard'), may hold values from -0.125 to 0.125
- bias_forget: float32 [1024], replicated, may hold values from 2 to 9
- theta: float32 [1024], replicated, may hold values from -1 to 1
- w_gate_out: bfloat16 [2048, 2048], P('wshard'), may hold values from -0.125 to 0.125
- gain_out: float32 [2048], replicated, may hold values from 0.5 to 1.5
- w_out: bfloat16 [2048, 2048], P('wshard'), may hold values from -0.1875 to 0.1875
- gain_ffn: float32 [2048], replicated, may hold values from 0.5 to 1.5
- w_ffgate: bfloat16 [2048, 5632], P('wshard'), may hold values from -0.125 to 0.125
- w_ffup: bfloat16 [2048, 5632], P('wshard'), may hold values from -0.125 to 0.125
- w_down: bfloat16 [5632, 2048], P('wshard'), may hold values from -0.15625 to 0.15625
- out_grad: bfloat16 [8, 1024, 2048], P('wshard', 'seq'), may hold values from -6 to 6
Outputs:
- result: bfloat16 [8, 1024, 2048], P('wshard', 'seq')
- grad_tokens: bfloat16 [8, 1024, 2048], P('wshard', 'seq')
- grad_gain_mix: float32 [2048], replicated
- grad_w_in: float32 [2048, 2048], P(('seq', 'wshard'))
- grad_w_forget: float32 [2048, 1024], P(('seq', 'wshard'))
- grad_bias_forget: float32 [1024], replicated
- grad_theta: float32 [1024], replicated
- grad_w_gate_out: float32 [2048, 2048], P(('seq', 'wshard'))
- grad_gain_out: float32 [2048], replicated
- grad_w_out: float32 [2048, 2048], P(('seq', 'wshard'))
- grad_gain_ffn: float32 [2048], replicated
- grad_w_ffgate: float32 [2048, 5632], P(('seq', 'wshard'))
- grad_w_ffup: float32 [2048, 5632], P(('seq', 'wshard'))
- grad_w_down: float32 [5632, 2048], P(('seq', 'wshard'))
- rms_values: float32 [3], replicated
The draws below stay inside these ranges and needn't reach their ends.
Inputs may be any that keep to these rules, and one draw needn't show every extreme that they name: 1 marks the first token of a document inside a sequence; the state starts afresh there. `layer_index`: the layer's place among 24.
All inputs are finite; a program needn't handle non-finite values. No bound on the sum of `starts` on one device may be relied on, other than what follows from the above.
Results may differ from the reference program's by a relative error of at most 0.014.
Values may be sent and summed in bfloat16 or wider, within the bound.
No kernel may reach another device: no remote copies, remote signals or barrier semaphores. Data moves between devices by JAX's collectives and lax.ppermute only.
A program may use at most 512 MiB of HBM per device.

```python
import math
import jax
import jax.numpy as jnp
from jax import lax

D = 2048
FF = 5632
CHANNELS = 1024
LAYERS = 24
SEQUENCES = 8
LENGTH = 1024


def draw_tokens(key, part):
    first = jax.random.fold_in(key, 0)
    base = jax.random.normal(first, (SEQUENCES, LENGTH, D), jnp.float32)
    place = jnp.arange(LENGTH, dtype=jnp.float32) / LENGTH
    rising = 0.6 + 1.2 * place
    value = base * rising[None, :, None]
    return jnp.clip(value, -8.0, 8.0).astype(jnp.bfloat16)


def place_ends(values, stream_key, least, high):
    extent = values.shape
    index_at = [jax.random.randint(jax.random.fold_in(stream_key, axis), (), 0, extent[axis]) for axis in range(len(extent))]
    values = values.at[tuple(index_at)].set(least)
    longest = extent.index(max(extent))
    index_at[longest] = (index_at[longest] + 1) % extent[longest]
    return values.at[tuple(index_at)].set(high)


def level_of(rng, extent, cuts, least, high):
    def one(axis_at, shards_of):
        steps = jax.random.uniform(jax.random.fold_in(jax.random.fold_in(rng, 6), axis_at), (shards_of,), jnp.float32, least / len(cuts), high / len(cuts))
        return jnp.repeat(jnp.exp(steps), extent[axis_at] // shards_of).reshape((-1,) + (1,) * (len(extent) - axis_at - 1))

    loudness = one(*cuts[0])
    for cut in cuts[1:]:
        loudness = loudness * one(*cut)
    return loudness


def bell_draw(rng, dims, scale, bound, pieces=(), held_as=jnp.bfloat16):
    values = jax.random.normal(rng, dims, jnp.float32) * scale
    if len(pieces) > 0:
        values = level_of(rng, dims, pieces, -0.22, 0.18) * values
    return jnp.clip(values, min=-bound, max=bound).astype(held_as)


def setup_inputs(seed: int = 0) -> dict:
    splits = jax.random.split(jax.random.key(seed), 17)
    return {
        "tokens": draw_tokens(jax.random.fold_in(splits[16], 71), 0),
        "starts": place_ends((jax.random.randint(splits[1], (SEQUENCES, LENGTH), 0, 300) < 1).astype(jnp.int32), jax.random.fold_in(splits[1], 1), 0, 1),
        "layer_index": jax.random.randint(splits[2], (1,), 0, LAYERS).astype(jnp.int32),
        "gain_mix": jnp.clip(1.0 + 0.1 * jax.random.normal(splits[3], (D,), jnp.float32), 0.5, 1.5),
        "w_in": bell_draw(splits[4], (D, D), D ** -0.5, 0.125, ((0, 4),)),
        "w_forget": bell_draw(splits[5], (D, CHANNELS), D ** -0.5, 0.125, ((0, 4),)),
        "bias_forget": jnp.clip(jax.random.uniform(splits[6], (CHANNELS,), jnp.float32, 2.0, 9.0), 2.0, 9.0),
        "theta": jnp.clip(jax.random.uniform(splits[7], (CHANNELS,), jnp.float32, -1.0, 1.0), -1.0, 1.0),
        "w_gate_out": bell_draw(splits[8], (D, D), D ** -0.5, 0.125, ((0, 4),)),
        "gain_out": jnp.clip(1.0 + 0.1 * jax.random.normal(splits[9], (D,), jnp.float32), 0.5, 1.5),
        "w_out": bell_draw(splits[10], (D, D), (D // 2) ** -0.5, 0.1875, ((0, 4),)),
        "gain_ffn": jnp.clip(1.0 + 0.1 * jax.random.normal(splits[11], (D,), jnp.float32), 0.5, 1.5),
        "w_ffgate": bell_draw(splits[12], (D, FF), D ** -0.5, 0.125, ((0, 4),)),
        "w_ffup": bell_draw(splits[13], (D, FF), D ** -0.5, 0.125, ((0, 4),)),
        "w_down": bell_draw(splits[14], (FF, D), (FF // 4) ** -0.5, 0.15625, ((0, 4),)),
        "out_grad": bell_draw(splits[15], (SEQUENCES, LENGTH, D), 1.0, 6.0, ((0, 4), (1, 8))),
    }


EPS = 1e-06

@jax.custom_vjp
def low(v):
    return lax.optimization_barrier(v.astype(jnp.bfloat16)).astype(jnp.float32)

@jax.custom_vjp
def low_back(v):
    return v

def low_keep(v):
    return (low(v), None)

def low_pass(kept, grad):
    return (grad,)

def back_keep(v):
    return (v, None)

def back_low(kept, grad):
    return (low(grad),)
low.defvjp(low_keep, low_pass)
low_back.defvjp(back_keep, back_low)

def combine(first, second):
    left_re, left_im, base_re, base_im = first
    right_re, right_im, add_re, add_im = second
    return (left_re * right_re - left_im * right_im, left_re * right_im + left_im * right_re, right_re * base_re - right_im * base_im + add_re, right_re * base_im + right_im * base_re + add_im)

def product(left, right):
    return jnp.einsum('...i,ij->...j', left, right, precision=lax.Precision.HIGHEST, preferred_element_type=jnp.float32)

def normalize(value, gain):
    return value * lax.rsqrt(lax.optimization_barrier(jnp.mean(value * value, axis=-1, keepdims=True)) + EPS) * gain

def block(resid_in, weights, floor, flags):
    gain_mix, w_in, w_forget, bias_forget, theta, w_gate_out, gain_out, w_out, gain_ffn, w_ffgate, w_ffup, w_down = weights
    normed_in = low(normalize(resid_in, gain_mix))
    pre_input = low_back(product(normed_in, w_in))
    cand = low(low_back(jax.nn.silu(pre_input)))
    forget_logit = low(low_back(product(normed_in, w_forget) + bias_forget))
    pre_gate = low_back(product(normed_in, w_gate_out))
    keep = (floor + (1.0 - floor) * jax.nn.sigmoid(forget_logit)) * (1.0 - flags)[..., None]
    elements = (keep * jnp.cos(theta), keep * jnp.sin(theta), (1.0 - keep) * cand[..., :CHANNELS], (1.0 - keep) * cand[..., CHANNELS:])
    _, _, state_re, state_im = lax.associative_scan(combine, elements, axis=1)
    mixed_state = low(low_back(jnp.concatenate([state_re, state_im], axis=-1)))
    gated = low(normalize(mixed_state, gain_out) * jax.nn.sigmoid(pre_gate))
    branch_mix = low_back(product(gated, w_out))
    resid = resid_in + branch_mix
    normed_ffn = low(normalize(resid, gain_ffn))
    ffn_gate = low_back(product(normed_ffn, w_ffgate))
    ffn_up = low_back(product(normed_ffn, w_ffup))
    ffn_hidden = low(jax.nn.silu(ffn_gate) * ffn_up)
    branch_ffn = low_back(product(ffn_hidden, w_down))
    return (resid + branch_ffn, (branch_mix, branch_ffn))

def reference(tokens, starts, layer_index, gain_mix, w_in, w_forget, bias_forget, theta, w_gate_out, gain_out, w_out, gain_ffn, w_ffgate, w_ffup, w_down, out_grad):
    floor = layer_index[0].astype(jnp.float32) / LAYERS
    weights = tuple((item.astype(jnp.float32) for item in (gain_mix, w_in, w_forget, bias_forget, theta, w_gate_out, gain_out, w_out, gain_ffn, w_ffgate, w_ffup, w_down)))
    group = math.gcd(SEQUENCES, max(1, 4096 // LENGTH))
    blocks = SEQUENCES // group
    inputs = tokens.astype(jnp.float32).reshape(blocks, group, LENGTH, D)
    flag_all = starts.astype(jnp.float32).reshape(blocks, group, LENGTH)
    cotangent = out_grad.astype(jnp.float32).reshape(blocks, group, LENGTH, D)

    def step(carry, item):
        totals, squares = carry
        resid_in, flags, upstream = item

        def forward(value, params):
            return block(value, params, floor, flags)
        result, pull, branches = jax.vjp(forward, resid_in, weights, has_aux=True)
        grad_in, grad_weights = pull(upstream)
        totals = jax.tree.map(lambda left, right: left + right, totals, grad_weights)
        squares = squares + jnp.stack([jnp.sum(resid_in * resid_in), jnp.sum(branches[0] * branches[0]), jnp.sum(branches[1] * branches[1])])
        return ((totals, squares), (result.astype(jnp.bfloat16), grad_in.astype(jnp.bfloat16)))
    start_totals = tuple((jnp.zeros_like(item) for item in weights))
    (totals, squares), (result, grad_in) = lax.scan(step, (start_totals, jnp.zeros((3,), jnp.float32)), (inputs, flag_all, cotangent))
    rms_values = jnp.sqrt(squares / (SEQUENCES * LENGTH * D))
    return (result.reshape(SEQUENCES, LENGTH, D), grad_in.reshape(SEQUENCES, LENGTH, D), totals[0], totals[1], totals[2], totals[3], totals[4], totals[5], totals[6], totals[7], totals[8], totals[9], totals[10], totals[11], rms_values)
```

```python
import functools

import jax
import jax.numpy as jnp
from jax import lax
from jax.experimental import pallas as pl
from jax.experimental.pallas import tpu as pltpu
from jax.sharding import PartitionSpec as P

LAYERS = 24
EPS = 1e-06
BF = jnp.bfloat16
F32 = jnp.float32


def dot(left, right, form):
    return jnp.einsum(form, left, right, preferred_element_type=F32)


def gather_seq(value):
    return lax.all_gather(value, "seq", axis=0, tiled=True)


def scatter_seq(value):
    return lax.psum_scatter(value, "seq", scatter_dimension=0, tiled=True)


def gather_shard(value):
    return lax.all_gather(value, "wshard", axis=0, tiled=True)


def scatter_shard(value):
    return lax.psum_scatter(value, "wshard", scatter_dimension=0, tiled=True)


def column_parts(array, count):
    width = array.shape[-1] // count
    if width % 128 == 0:
        return [(array, width, index) for index in range(count)]
    return [
        (array[..., index * width : (index + 1) * width], width, 0) for index in range(count)
    ]


def part_spec(groups, tokens, width, index):
    mode = pl.Buffered(1) if groups * tokens > 2048 else None
    return pl.BlockSpec(
        (groups, 1, tokens, width), lambda b, index=index: (0, b, 0, index), pipeline_mode=mode
    )


def row_spec(width, index):
    return pl.BlockSpec((1, width), lambda b, index=index: (0, index))


def flat(ref):
    groups, _, tokens, width = ref.shape
    return ref[...].reshape(groups * tokens, width)


def forward_kernel(
    floor_ref,
    pre_re,
    pre_im,
    pre_forget,
    gate_re,
    gate_im,
    flag_ref,
    bias_ref,
    theta_ref,
    gain_re,
    gain_im,
    state_re,
    state_im,
    gated_re,
    gated_im,
    square_ref,
    keep_s,
    val_re,
    val_im,
    prod_re,
    prod_im,
    carry_re,
    carry_im,
):
    groups, _, tokens, width = pre_re.shape
    floor = floor_ref[0]
    cosine = jnp.cos(theta_ref[...])
    sine = jnp.sin(theta_ref[...])
    logit = (flat(pre_forget) + bias_ref[...]).astype(BF).astype(F32)
    keep = (floor + (1.0 - floor) * jax.nn.sigmoid(logit)) * (1.0 - flat(flag_ref))
    keep_s[...] = keep
    fresh = 1.0 - keep
    value = flat(pre_re)
    val_re[...] = fresh * (value * jax.nn.sigmoid(value)).astype(BF).astype(F32)
    value = flat(pre_im)
    val_im[...] = fresh * (value * jax.nn.sigmoid(value)).astype(BF).astype(F32)

    def step(t, carry):
        h_re, h_im, p_re, p_im = carry
        rows = pl.ds(t, groups, stride=tokens)
        held = keep_s[rows, :]
        a_re = held * cosine
        a_im = held * sine
        n_re = a_re * h_re - a_im * h_im + val_re[rows, :]
        n_im = a_re * h_im + a_im * h_re + val_im[rows, :]
        q_re = a_re * p_re - a_im * p_im
        q_im = a_re * p_im + a_im * p_re
        val_re[rows, :] = n_re
        val_im[rows, :] = n_im
        prod_re[rows, :] = q_re
        prod_im[rows, :] = q_im
        return n_re, n_im, q_re, q_im

    zero = jnp.zeros((groups, width), F32)
    lax.fori_loop(0, tokens, step, (zero, zero, zero + 1.0, zero), unroll=8)
    c_re = jnp.zeros((1, width), F32)
    c_im = jnp.zeros((1, width), F32)
    for group in range(groups):
        carry_re[group : group + 1, :] = c_re
        carry_im[group : group + 1, :] = c_im
        last = (group + 1) * tokens - 1
        p_re = prod_re[last : last + 1, :]
        p_im = prod_im[last : last + 1, :]
        c_re, c_im = (
            p_re * c_re - p_im * c_im + val_re[last : last + 1, :],
            p_re * c_im + p_im * c_re + val_im[last : last + 1, :],
        )
    for group in range(groups):
        rows = slice(group * tokens, (group + 1) * tokens)
        c_re = carry_re[group : group + 1, :]
        c_im = carry_im[group : group + 1, :]
        p_re = prod_re[rows, :]
        p_im = prod_im[rows, :]
        h_re = val_re[rows, :] + p_re * c_re - p_im * c_im
        h_im = val_im[rows, :] + p_re * c_im + p_im * c_re
        state_re[group, 0] = h_re
        state_im[group, 0] = h_im
        m_re = h_re.astype(BF).astype(F32)
        m_im = h_im.astype(BF).astype(F32)
        gated_re[group, 0] = (m_re * gain_re[...] * jax.nn.sigmoid(gate_re[group, 0])).astype(BF)
        gated_im[group, 0] = (m_im * gain_im[...] * jax.nn.sigmoid(gate_im[group, 0])).astype(BF)
        square_ref[group, 0] = jnp.sum(m_re * m_re + m_im * m_im, axis=1, keepdims=True)


def backward_kernel(
    floor_ref,
    pre_re,
    pre_im,
    pre_forget,
    gate_re,
    gate_im,
    flag_ref,
    bias_ref,
    theta_ref,
    gain_re,
    gain_im,
    state_re,
    state_im,
    up_re,
    up_im,
    scale_ref,
    term_ref,
    out_re,
    out_im,
    out_forget,
    out_gate_re,
    out_gate_im,
    sum_bias,
    sum_theta,
    sum_gain_re,
    sum_gain_im,
    keep_s,
    adj_re,
    adj_im,
    prod_re,
    prod_im,
    carry_re,
    carry_im,
):
    groups, _, tokens, width = pre_re.shape
    rows_all = groups * tokens
    floor = floor_ref[0]
    cosine = jnp.cos(theta_ref[...])
    sine = jnp.sin(theta_ref[...])
    open_ = 1.0 - flat(flag_ref)
    logit = (flat(pre_forget) + bias_ref[...]).astype(BF).astype(F32)
    sig_forget = jax.nn.sigmoid(logit)
    keep = (floor + (1.0 - floor) * sig_forget) * open_
    keep_s[0:rows_all, :] = keep
    keep_s[rows_all : rows_all + tokens, :] = jnp.zeros((tokens, width), F32)
    scale = flat(scale_ref)
    term = flat(term_ref)

    @pl.when(pl.program_id(0) == 0)
    def _():
        sum_bias[...] = jnp.zeros_like(sum_bias)
        sum_theta[...] = jnp.zeros_like(sum_theta)
        sum_gain_re[...] = jnp.zeros_like(sum_gain_re)
        sum_gain_im[...] = jnp.zeros_like(sum_gain_im)

    for state, up, gate, gain, sum_gain, out_gate, adj in (
        (state_re, up_re, gate_re, gain_re, sum_gain_re, out_gate_re, adj_re),
        (state_im, up_im, gate_im, gain_im, sum_gain_im, out_gate_im, adj_im),
    ):
        mixed = flat(state).astype(BF).astype(F32)
        grad = flat(up)
        sig = jax.nn.sigmoid(flat(gate))
        inner = grad * sig
        normed = inner * mixed * scale
        sum_gain[...] += jnp.sum(normed, axis=0, keepdims=True)
        gate_grad = (normed * gain[...] * (1.0 - sig)).astype(BF)
        out_gate[...] = gate_grad.reshape(out_gate.shape)
        adj[...] = (scale * (inner * gain[...]) - mixed * term).astype(BF).astype(F32)

    def step(index, carry):
        g_re, g_im, p_re, p_im = carry
        t = tokens - 1 - index
        rows = pl.ds(t, groups, stride=tokens)
        held = keep_s[pl.ds(t + 1, groups, stride=tokens), :]
        a_re = held * cosine
        a_im = held * sine
        n_re = a_re * g_re + a_im * g_im + adj_re[rows, :]
        n_im = a_re * g_im - a_im * g_re + adj_im[rows, :]
        q_re = a_re * p_re + a_im * p_im
        q_im = a_re * p_im - a_im * p_re
        adj_re[rows, :] = n_re
        adj_im[rows, :] = n_im
        prod_re[rows, :] = q_re
        prod_im[rows, :] = q_im
        return n_re, n_im, q_re, q_im

    zero = jnp.zeros((groups, width), F32)
    lax.fori_loop(0, tokens, step, (zero, zero, zero + 1.0, zero), unroll=8)
    c_re = jnp.zeros((1, width), F32)
    c_im = jnp.zeros((1, width), F32)
    for group in reversed(range(groups)):
        carry_re[group : group + 1, :] = c_re
        carry_im[group : group + 1, :] = c_im
        first = group * tokens
        p_re = prod_re[first : first + 1, :]
        p_im = prod_im[first : first + 1, :]
        c_re, c_im = (
            p_re * c_re - p_im * c_im + adj_re[first : first + 1, :],
            p_re * c_im + p_im * c_re + adj_im[first : first + 1, :],
        )
    row_index = lax.broadcasted_iota(jnp.int32, (tokens, width), 0)
    tail_re = jnp.zeros((1, width), F32)
    tail_im = jnp.zeros((1, width), F32)
    total_theta = jnp.zeros((1, width), F32)
    total_bias = jnp.zeros((1, width), F32)
    for group in range(groups):
        rows = slice(group * tokens, (group + 1) * tokens)
        c_re = carry_re[group : group + 1, :]
        c_im = carry_im[group : group + 1, :]
        p_re = prod_re[rows, :]
        p_im = prod_im[rows, :]
        g_re = adj_re[rows, :] + p_re * c_re - p_im * c_im
        g_im = adj_im[rows, :] + p_re * c_im + p_im * c_re
        h_re = state_re[group, 0]
        h_im = state_im[group, 0]
        prev_re = jnp.where(row_index == 0, tail_re, pltpu.roll(h_re, 1, 0))
        prev_im = jnp.where(row_index == 0, tail_im, pltpu.roll(h_im, 1, 0))
        tail_re = h_re[tokens - 1 :, :]
        tail_im = h_im[tokens - 1 :, :]
        turn_re = cosine * prev_re - sine * prev_im
        turn_im = sine * prev_re + cosine * prev_im
        held = keep_s[rows, :]
        fresh = 1.0 - held
        x_re = pre_re[group, 0]
        x_im = pre_im[group, 0]
        s_re = jax.nn.sigmoid(x_re)
        s_im = jax.nn.sigmoid(x_im)
        cand_re = (x_re * s_re).astype(BF).astype(F32)
        cand_im = (x_im * s_im).astype(BF).astype(F32)
        grad_keep = g_re * (turn_re - cand_re) + g_im * (turn_im - cand_im)
        total_theta -= jnp.sum(
            held * (g_re * turn_im - g_im * turn_re), axis=0, keepdims=True
        )
        logit = (pre_forget[group, 0] + bias_ref[...]).astype(BF).astype(F32)
        sig = jax.nn.sigmoid(logit)
        grad_forget = (
            grad_keep * (1.0 - flag_ref[group, 0]) * ((1.0 - floor) * (sig * (1.0 - sig)))
        ).astype(BF)
        total_bias += jnp.sum(grad_forget.astype(F32), axis=0, keepdims=True)
        out_forget[group, 0] = grad_forget
        cand_grad = (fresh * g_re).astype(BF).astype(F32)
        out_re[group, 0] = (cand_grad * s_re * (1.0 + x_re * (1.0 - s_re))).astype(BF)
        cand_grad = (fresh * g_im).astype(BF).astype(F32)
        out_im[group, 0] = (cand_grad * s_im * (1.0 + x_im * (1.0 - s_im))).astype(BF)
    sum_theta[...] += total_theta
    sum_bias[...] += total_bias


def recur_forward(floor, pre, flags, bias, theta, gain):
    groups, seqs, tokens, _ = pre.shape
    parts = column_parts(pre, 5)
    width = parts[0][1]
    gains = column_parts(gain, 2)
    operands = [floor] + [p[0] for p in parts] + [flags, bias, theta] + [g[0] for g in gains]
    in_specs = (
        [pl.BlockSpec(memory_space=pltpu.SMEM)]
        + [part_spec(groups, tokens, width, p[2]) for p in parts]
        + [part_spec(groups, tokens, 1, 0), row_spec(width, 0), row_spec(width, 0)]
        + [row_spec(width, g[2]) for g in gains]
    )
    whole = pltpu.VMEM((groups * tokens, width), F32)
    shape = (groups, seqs, tokens, width)
    return pl.pallas_call(
        forward_kernel,
        grid=(seqs,),
        in_specs=in_specs,
        out_specs=[part_spec(groups, tokens, width, 0)] * 4 + [part_spec(groups, tokens, 1, 0)],
        out_shape=[
            jax.ShapeDtypeStruct(shape, F32),
            jax.ShapeDtypeStruct(shape, F32),
            jax.ShapeDtypeStruct(shape, BF),
            jax.ShapeDtypeStruct(shape, BF),
            jax.ShapeDtypeStruct((groups, seqs, tokens, 1), F32),
        ],
        scratch_shapes=[whole] * 5 + [pltpu.VMEM((groups, width), F32)] * 2,
        compiler_params=pltpu.CompilerParams(vmem_limit_bytes=56 * 2**20),
        cost_estimate=pl.CostEstimate(
            flops=60 * groups * seqs * tokens * width,
            bytes_accessed=32 * groups * seqs * tokens * width,
            transcendentals=5 * groups * seqs * tokens * width,
        ),
        name="recur_forward",
    )(*operands)


def recur_backward(floor, pre, flags, bias, theta, gain, state_re, state_im, up, scale, term):
    groups, seqs, tokens, _ = pre.shape
    parts = column_parts(pre, 5)
    width = parts[0][1]
    gains = column_parts(gain, 2)
    ups = column_parts(up, 2)
    operands = (
        [floor]
        + [p[0] for p in parts]
        + [flags, bias, theta]
        + [g[0] for g in gains]
        + [state_re, state_im]
        + [u[0] for u in ups]
        + [scale, term]
    )
    one = part_spec(groups, tokens, 1, 0)
    in_specs = (
        [pl.BlockSpec(memory_space=pltpu.SMEM)]
        + [part_spec(groups, tokens, width, p[2]) for p in parts]
        + [one, row_spec(width, 0), row_spec(width, 0)]
        + [row_spec(width, g[2]) for g in gains]
        + [part_spec(groups, tokens, width, 0)] * 2
        + [part_spec(groups, tokens, width, u[2]) for u in ups]
        + [one, one]
    )
    whole = pltpu.VMEM((groups * tokens, width), F32)
    shape = (groups, seqs, tokens, width)
    return pl.pallas_call(
        backward_kernel,
        grid=(seqs,),
        in_specs=in_specs,
        out_specs=[part_spec(groups, tokens, width, 0)] * 5 + [row_spec(width, 0)] * 4,
        out_shape=[jax.ShapeDtypeStruct(shape, BF)] * 5
        + [jax.ShapeDtypeStruct((1, width), F32)] * 4,
        scratch_shapes=[pltpu.VMEM(((groups + 1) * tokens, width), F32)]
        + [whole] * 4
        + [pltpu.VMEM((groups, width), F32)] * 2,
        compiler_params=pltpu.CompilerParams(vmem_limit_bytes=56 * 2**20),
        cost_estimate=pl.CostEstimate(
            flops=100 * groups * seqs * tokens * width,
            bytes_accessed=50 * groups * seqs * tokens * width,
            transcendentals=8 * groups * seqs * tokens * width,
        ),
        name="recur_backward",
    )(*operands)


def body(
    tokens,
    starts,
    layer_index,
    gain_mix,
    w_in,
    w_forget,
    bias_forget,
    theta,
    w_gate_out,
    gain_out,
    w_out,
    gain_ffn,
    w_ffgate,
    w_ffup,
    w_down,
    out_grad,
):
    seqs, seq_dev, width = tokens.shape
    rows = seqs * seq_dev
    groups = lax.axis_size("seq")
    planes = lax.axis_size("wshard")
    devices = groups * planes
    place = lax.axis_index("seq")
    total = groups * rows
    floor = layer_index.astype(F32) / LAYERS

    def own_columns(array):
        block = w_out.shape[0] if array.shape[-1] % w_down.shape[0] else w_down.shape[0]
        run = block // groups
        split = array.reshape(array.shape[:-1] + (array.shape[-1] // block, block))
        part = lax.dynamic_slice_in_dim(split, place * run, run, split.ndim - 1)
        return part.reshape(array.shape[:-1] + (-1,))

    def own_rows(array):
        run = array.shape[0] // groups
        return lax.dynamic_slice_in_dim(array, place * run, run, 0)

    rec_w = gather_shard(
        jnp.concatenate(
            [own_columns(w_in), own_columns(w_forget), own_columns(w_gate_out)], axis=1
        )
    )
    out_w = gather_shard(own_rows(w_out))
    ff_w = gather_shard(jnp.concatenate([own_columns(w_ffgate), own_columns(w_ffup)], axis=1))
    down_w = gather_shard(own_rows(w_down))
    hidden = down_w.shape[0]
    mixw = out_w.shape[0]
    chan = mixw // 2

    resid_in = tokens.reshape(rows, width).astype(F32)
    scale_in = lax.rsqrt(jnp.mean(resid_in * resid_in, axis=1, keepdims=True) + EPS)
    normed_in_own = (resid_in * scale_in * gain_mix).astype(BF)
    normed_in = gather_seq(normed_in_own)
    upstream_own = out_grad.reshape(rows, width)
    upstream = gather_seq(upstream_own)

    flags = starts.astype(F32).reshape(seqs, groups, seq_dev).transpose(1, 0, 2)[..., None]
    bias_own = own_columns(bias_forget[None])
    theta_own = own_columns(theta[None])
    gain_own = own_columns(gain_out[None])

    pre = dot(normed_in, rec_w, "td,dc->tc").reshape(groups, seqs, seq_dev, 5 * chan)
    state_re, state_im, gated_re, gated_im, square = recur_forward(
        floor, pre, flags, bias_own, theta_own, gain_own
    )
    gated = jnp.concatenate([gated_re, gated_im], axis=-1).reshape(total, mixw)
    mean_square = lax.psum(square.reshape(groups, rows), "seq") / width
    scale_all = lax.rsqrt(mean_square + EPS)
    scale_out = lax.dynamic_index_in_dim(scale_all, place, 0, keepdims=False)[:, None]
    branch_mix = scale_out * scatter_seq(dot(gated, out_w, "tc,cd->td").astype(BF)).astype(F32)
    resid = resid_in + branch_mix
    scale_ffn = lax.rsqrt(jnp.mean(resid * resid, axis=1, keepdims=True) + EPS)
    normed_ffn = gather_seq((resid * scale_ffn * gain_ffn).astype(BF))

    ff = dot(normed_ffn, ff_w, "td,df->tf")
    ffn_gate, ffn_up = ff[:, :hidden], ff[:, hidden:]
    sig_ffn = jax.nn.sigmoid(ffn_gate)
    silu_ffn = ffn_gate * sig_ffn
    ffn_hidden = (silu_ffn * ffn_up).astype(BF)
    grad_hidden = dot(upstream, down_w, "td,fd->tf")
    grad_gate = (grad_hidden * ffn_up * sig_ffn * (1.0 + ffn_gate * (1.0 - sig_ffn))).astype(BF)
    grad_up = (grad_hidden * silu_ffn).astype(BF)
    grad_ff = jnp.concatenate([grad_gate, grad_up], axis=1)
    grad_normed_ffn = scatter_seq(dot(grad_ff, ff_w, "tf,df->td").astype(BF)).astype(F32)
    branch_ffn = scatter_seq(dot(ffn_hidden, down_w, "tf,fd->td").astype(BF)).astype(F32)
    result = (resid + branch_ffn).astype(BF)

    scaled_ffn = grad_normed_ffn * gain_ffn
    grad_resid = (
        upstream_own.astype(F32)
        + scale_ffn * scaled_ffn
        - resid * scale_ffn**3 * jnp.mean(scaled_ffn * resid, axis=1, keepdims=True)
    )
    grad_gain_ffn = jnp.sum(grad_normed_ffn * resid * scale_ffn, axis=0)
    grad_branch_own = grad_resid.astype(BF)
    overlap = jnp.sum(grad_branch_own.astype(F32) * branch_mix, axis=1)
    term_own = scale_out[:, 0] ** 2 * overlap / width
    term_all = lax.all_gather(term_own, "seq", axis=0, tiled=True)
    grad_branch = gather_seq(grad_branch_own)
    grad_gated = dot(grad_branch, out_w, "td,cd->tc").reshape(groups, seqs, seq_dev, mixw)

    shape_one = (groups, seqs, seq_dev, 1)
    *grad_parts, sum_bias, sum_theta, sum_gain_re, sum_gain_im = recur_backward(
        floor,
        pre,
        flags,
        bias_own,
        theta_own,
        gain_own,
        state_re,
        state_im,
        grad_gated,
        scale_all.reshape(shape_one),
        term_all.reshape(shape_one),
    )
    grad_pre = jnp.concatenate(grad_parts, axis=-1).reshape(total, 5 * chan)
    grad_normed_in = scatter_seq(dot(grad_pre, rec_w, "tc,dc->td").astype(BF)).astype(F32)
    scaled_in = grad_normed_in * gain_mix
    grad_tokens = (
        grad_resid
        + scale_in * scaled_in
        - resid_in * scale_in**3 * jnp.mean(scaled_in * resid_in, axis=1, keepdims=True)
    ).astype(BF)
    grad_gain_mix = jnp.sum(grad_normed_in * resid_in * scale_in, axis=0)

    def to_owner(grad):
        run = grad.shape[0] // devices
        part = grad.astype(BF).reshape(groups, planes, run, -1).transpose(1, 0, 2, 3)
        part = scatter_shard(part.reshape(grad.shape))
        part = part.reshape(groups, run, -1)
        return lax.all_to_all(part, "seq", split_axis=0, concat_axis=0, tiled=True)

    def columns(part, block_run):
        source, run, cols = part.shape
        split = part.reshape(source, run, cols // block_run, block_run)
        return split.transpose(1, 2, 0, 3).reshape(run, -1).astype(F32)

    scaled_gated = (
        gated.astype(F32) * scale_all.reshape(total, 1)
    ).astype(BF)
    ff_grad = to_owner(dot(normed_ffn, grad_ff, "td,tf->df"))
    grad_w_ffgate = columns(ff_grad[..., :hidden], hidden // planes)
    grad_w_ffup = columns(ff_grad[..., hidden:], hidden // planes)
    rec_grad = to_owner(dot(normed_in, grad_pre, "td,tc->dc"))
    grad_w_in = columns(rec_grad[..., :mixw], mixw // planes)
    grad_w_forget = columns(rec_grad[..., mixw : mixw + chan], mixw // planes)
    grad_w_gate = columns(rec_grad[..., mixw + chan :], mixw // planes)

    pairs = []
    for s in range(groups):
        for w in range(planes):
            block = w * groups + s
            pairs.append((s * planes + w, block))

    def rows_to_owner(grad):
        part = scatter_shard(grad.astype(BF))
        return lax.ppermute(part, ("seq", "wshard"), pairs).astype(F32)

    grad_w_down = rows_to_owner(dot(ffn_hidden, upstream, "tf,td->fd"))
    grad_w_out = rows_to_owner(dot(scaled_gated, grad_branch, "tc,td->cd"))

    def spread(part, count):
        run = mixw // planes
        zero = jnp.zeros((count, groups, run), F32)
        zero = lax.dynamic_update_slice(zero, part.reshape(count, 1, run), (0, place, 0))
        return zero.reshape(-1)

    squares = jnp.stack(
        [
            jnp.sum(resid_in * resid_in),
            jnp.sum(branch_mix * branch_mix),
            jnp.sum(branch_ffn * branch_ffn),
        ]
    )
    half = planes // 2
    grad_gain_mix, grad_bias, grad_theta, grad_gain_out, grad_gain_ffn, squares = lax.psum(
        (
            grad_gain_mix,
            spread(sum_bias, half),
            spread(sum_theta, half),
            spread(jnp.concatenate([sum_gain_re, sum_gain_im], axis=1), planes),
            grad_gain_ffn,
            squares,
        ),
        ("seq", "wshard"),
    )
    rms_values = jnp.sqrt(squares / (rows * width * devices))
    return (
        result.reshape(seqs, seq_dev, width),
        grad_tokens.reshape(seqs, seq_dev, width),
        grad_gain_mix,
        grad_w_in,
        grad_w_forget,
        grad_bias,
        grad_theta,
        grad_w_gate,
        grad_gain_out,
        grad_w_out,
        grad_gain_ffn,
        grad_w_ffgate,
        grad_w_ffup,
        grad_w_down,
        rms_values,
    )


def solution(mesh):
    whole = P()
    rowed = P("wshard", None)
    stream = P("wshard", "seq", None)
    owned = P(("seq", "wshard"), None)
    return jax.shard_map(
        body,
        mesh=mesh,
        in_specs=(
            stream,
            rowed,
            whole,
            whole,
            rowed,
            rowed,
            whole,
            whole,
            rowed,
            whole,
            rowed,
            whole,
            rowed,
            rowed,
            rowed,
            stream,
        ),
        out_specs=(
            stream,
            stream,
            whole,
            owned,
            owned,
            whole,
            whole,
            owned,
            whole,
            owned,
            whole,
            owned,
            owned,
            owned,
            whole,
        ),
        check_vma=False,
    )
```

```python
import functools

import jax
import jax.numpy as jnp
from jax import lax
from jax.experimental import pallas as pl
from jax.experimental.pallas import tpu as pltpu
from jax.sharding import PartitionSpec as P

LAYERS = 24
EPS = 1e-06
BF = jnp.bfloat16
F32 = jnp.float32


def dot(left, right, form):
    return jnp.einsum(form, left, right, preferred_element_type=F32)


def swap(value, bit):
    size = lax.axis_size("seq")
    return lax.ppermute(value, "seq", [(i, i ^ bit) for i in range(size)])


def chip_bits():
    size = lax.axis_size("seq")
    return [1 << i for i in range(1, size.bit_length() - 1)]


def gather_even(own):
    bits = chip_bits()
    if len(bits) == 2:
        first, second = bits
        half = own.shape[0] // 2
        from_first = swap(own, first)
        from_second = swap(own, second)
        top = swap(from_first[:half], second)
        low = swap(from_second[half:], first)
        return jnp.concatenate([own, from_first, from_second, top, low], axis=0)
    held = own
    for bit in bits:
        held = jnp.concatenate([held, swap(held, bit)], axis=0)
    return held


def gather_seq(own):
    even = gather_even(own)
    return even, swap(even, 1)


def scatter_seq(even, odd):
    bits = chip_bits()
    joint = even.astype(F32) + swap(odd, 1).astype(F32)
    if len(bits) == 2:
        first, second = bits
        rows = joint.shape[0] // 4
        half = rows // 2
        low_joint = joint.astype(BF)
        near_first, near_second, far = (
            low_joint[rows : 2 * rows],
            low_joint[2 * rows : 3 * rows],
            low_joint[3 * rows :],
        )
        far_top = swap(far[:half], first)
        far_low = swap(far[half:], second)
        first_top = swap(near_first[:half], first)
        second_low = swap(near_second[half:], second)
        first_low = swap((near_first[half:].astype(F32) + far_low.astype(F32)).astype(BF), first)
        second_top = swap(
            (near_second[:half].astype(F32) + far_top.astype(F32)).astype(BF), second
        )
        first_all = jnp.concatenate([first_top, first_low], axis=0).astype(F32)
        second_all = jnp.concatenate([second_top, second_low], axis=0).astype(F32)
        return joint[:rows] + first_all + second_all
    for bit in reversed(bits):
        half = joint.shape[0] // 2
        joint = joint[:half] + swap(joint[half:].astype(BF), bit).astype(F32)
    return joint


def gather_small(own):
    held = own
    for bit in chip_bits() + [1]:
        held = jnp.concatenate([held, swap(held, bit)], axis=0)
    return held


def scatter_small(blocks):
    for bit in [1] + list(reversed(chip_bits())):
        half = blocks.shape[0] // 2
        blocks = blocks[:half] + swap(blocks[half:], bit)
    return blocks


def sum_all(value):
    for bit in [1] + chip_bits():
        value = value + swap(value, bit)
    planes = lax.axis_size("wshard")
    bit = 1
    while bit < planes:
        value = value + lax.ppermute(value, "wshard", [(i, i ^ bit) for i in range(planes)])
        bit *= 2
    return value


def gather_shard(value):
    return lax.all_gather(value, "wshard", axis=0, tiled=True)


def scatter_shard(value):
    return lax.psum_scatter(value, "wshard", scatter_dimension=0, tiled=True)


def slot_of(place, group, groups):
    key = place ^ group
    return (key >> 1) + (key & 1) * (groups // 2)


def group_of(place, half, index):
    return place ^ ((index << 1) | half)


def token_rows(slot, tokens):
    return pl.ds(pl.multiple_of(slot * tokens, tokens), tokens)


def keep_of(pre, flag, bias, floor, chan):
    logit = (pre[:, 2 * chan : 3 * chan] + bias).astype(BF).astype(F32)
    sig = jax.nn.sigmoid(logit)
    return (floor + (1.0 - floor) * sig) * (1.0 - flag), sig


def forward_kernel(
    place_ref,
    floor_ref,
    pre_even,
    pre_odd,
    flag_ref,
    bias_ref,
    theta_ref,
    gain_ref,
    state_ref,
    gated_even,
    gated_odd,
    square_ref,
    keep_s,
    val_re,
    val_im,
    prod_re,
    prod_im,
    carry_re,
    carry_im,
):
    groups, _, tokens, _ = flag_ref.shape
    chan = keep_s.shape[1]
    half_groups = groups // 2
    floor = floor_ref[0]
    place = place_ref[0]
    cosine = jnp.cos(theta_ref[...])
    sine = jnp.sin(theta_ref[...])

    for half, pre_ref in ((0, pre_even), (1, pre_odd)):

        @pl.loop(0, half_groups)
        def _(index, half=half, pre_ref=pre_ref):
            slot = index + half * half_groups
            rows = token_rows(slot, tokens)
            pre = pre_ref[index, 0]
            keep, _ = keep_of(pre, flag_ref[slot, 0], bias_ref[...], floor, chan)
            keep_s[rows, :] = keep
            fresh = 1.0 - keep
            value = pre[:, :chan]
            val_re[rows, :] = fresh * (value * jax.nn.sigmoid(value)).astype(BF).astype(F32)
            value = pre[:, chan : 2 * chan]
            val_im[rows, :] = fresh * (value * jax.nn.sigmoid(value)).astype(BF).astype(F32)

    def step(t, carry):
        h_re, h_im, p_re, p_im = carry
        rows = pl.ds(t, groups, stride=tokens)
        held = keep_s[rows, :]
        a_re = held * cosine
        a_im = held * sine
        n_re = a_re * h_re - a_im * h_im + val_re[rows, :]
        n_im = a_re * h_im + a_im * h_re + val_im[rows, :]
        q_re = a_re * p_re - a_im * p_im
        q_im = a_re * p_im + a_im * p_re
        val_re[rows, :] = n_re
        val_im[rows, :] = n_im
        prod_re[rows, :] = q_re
        prod_im[rows, :] = q_im
        return n_re, n_im, q_re, q_im

    zero = jnp.zeros((groups, chan), F32)
    lax.fori_loop(0, tokens, step, (zero, zero, zero + 1.0, zero), unroll=8)

    def link(group, carry):
        c_re, c_im = carry
        slot = slot_of(place, group, groups)
        carry_re[pl.ds(slot, 1), :] = c_re
        carry_im[pl.ds(slot, 1), :] = c_im
        last = pl.ds(slot * tokens + tokens - 1, 1)
        p_re = prod_re[last, :]
        p_im = prod_im[last, :]
        return (
            p_re * c_re - p_im * c_im + val_re[last, :],
            p_re * c_im + p_im * c_re + val_im[last, :],
        )

    nought = jnp.zeros((1, chan), F32)
    lax.fori_loop(0, groups, link, (nought, nought))

    for half, pre_ref, gated_ref in ((0, pre_even, gated_even), (1, pre_odd, gated_odd)):

        @pl.loop(0, half_groups)
        def _(index, half=half, pre_ref=pre_ref, gated_ref=gated_ref):
            slot = index + half * half_groups
            rows = token_rows(slot, tokens)
            c_re = carry_re[pl.ds(slot, 1), :]
            c_im = carry_im[pl.ds(slot, 1), :]
            p_re = prod_re[rows, :]
            p_im = prod_im[rows, :]
            h_re = val_re[rows, :] + p_re * c_re - p_im * c_im
            h_im = val_im[rows, :] + p_re * c_im + p_im * c_re
            state_ref[slot, 0, :, :chan] = h_re
            state_ref[slot, 0, :, chan:] = h_im
            m_re = h_re.astype(BF).astype(F32)
            m_im = h_im.astype(BF).astype(F32)
            gate = jax.nn.sigmoid(pre_ref[index, 0, :, 3 * chan :]) * gain_ref[...]
            gated_ref[index, 0, :, :chan] = (m_re * gate[:, :chan]).astype(BF)
            gated_ref[index, 0, :, chan:] = (m_im * gate[:, chan:]).astype(BF)
            square_ref[slot, 0] = jnp.sum(m_re * m_re + m_im * m_im, axis=1, keepdims=True)


def backward_kernel(
    place_ref,
    floor_ref,
    pre_even,
    pre_odd,
    flag_ref,
    bias_ref,
    theta_ref,
    gain_ref,
    state_ref,
    up_even,
    up_odd,
    scale_ref,
    term_ref,
    out_even,
    out_odd,
    sum_bias,
    sum_theta,
    sum_gain,
    keep_s,
    adj_re,
    adj_im,
    prod_re,
    prod_im,
    carry_re,
    carry_im,
    next_s,
):
    groups, _, tokens, _ = flag_ref.shape
    chan = keep_s.shape[1]
    half_groups = groups // 2
    floor = floor_ref[0]
    place = place_ref[0]
    cosine = jnp.cos(theta_ref[...])
    sine = jnp.sin(theta_ref[...])

    @pl.when(pl.program_id(0) == 0)
    def _():
        sum_bias[...] = jnp.zeros_like(sum_bias)
        sum_theta[...] = jnp.zeros_like(sum_theta)
        sum_gain[...] = jnp.zeros_like(sum_gain)

    for half, pre_ref, up_ref, out_ref in (
        (0, pre_even, up_even, out_even),
        (1, pre_odd, up_odd, out_odd),
    ):

        @pl.loop(0, half_groups)
        def _(index, half=half, pre_ref=pre_ref, up_ref=up_ref, out_ref=out_ref):
            slot = index + half * half_groups
            rows = token_rows(slot, tokens)
            pre = pre_ref[index, 0]
            keep, _ = keep_of(pre, flag_ref[slot, 0], bias_ref[...], floor, chan)
            keep_s[rows, :] = keep
            scale = scale_ref[slot, 0]
            mixed = state_ref[slot, 0].astype(BF).astype(F32)
            sig = jax.nn.sigmoid(pre[:, 3 * chan :])
            inner = up_ref[index, 0] * sig
            normed = inner * mixed * scale
            sum_gain[...] += jnp.sum(normed, axis=0, keepdims=True)
            out_ref[index, 0, :, 3 * chan :] = (normed * gain_ref[...] * (1.0 - sig)).astype(BF)
            grad = (scale * (inner * gain_ref[...]) - mixed * term_ref[slot, 0]).astype(BF)
            adj_re[rows, :] = grad[:, :chan].astype(F32)
            adj_im[rows, :] = grad[:, chan:].astype(F32)

    @pl.loop(0, groups)
    def _(group):
        slot = slot_of(place, group, groups)
        after = slot_of(place, lax.min(group + 1, groups - 1), groups)
        row = keep_s[pl.ds(after * tokens, 1), :]
        next_s[pl.ds(slot, 1), :] = jnp.where(group == groups - 1, 0.0, row)

    def turn(t, held, carry):
        g_re, g_im, p_re, p_im = carry
        rows = pl.ds(t, groups, stride=tokens)
        a_re = held * cosine
        a_im = held * sine
        n_re = a_re * g_re + a_im * g_im + adj_re[rows, :]
        n_im = a_re * g_im - a_im * g_re + adj_im[rows, :]
        q_re = a_re * p_re + a_im * p_im
        q_im = a_re * p_im - a_im * p_re
        adj_re[rows, :] = n_re
        adj_im[rows, :] = n_im
        prod_re[rows, :] = q_re
        prod_im[rows, :] = q_im
        return n_re, n_im, q_re, q_im

    def step(index, carry):
        t = tokens - 2 - index
        return turn(t, keep_s[pl.ds(t + 1, groups, stride=tokens), :], carry)

    zero = jnp.zeros((groups, chan), F32)
    carry = turn(tokens - 1, next_s[...], (zero, zero, zero + 1.0, zero))
    lax.fori_loop(0, tokens - 1, step, carry, unroll=4)

    def link(index, carry):
        c_re, c_im = carry
        slot = slot_of(place, groups - 1 - index, groups)
        carry_re[pl.ds(slot, 1), :] = c_re
        carry_im[pl.ds(slot, 1), :] = c_im
        first = pl.ds(slot * tokens, 1)
        p_re = prod_re[first, :]
        p_im = prod_im[first, :]
        return (
            p_re * c_re - p_im * c_im + adj_re[first, :],
            p_re * c_im + p_im * c_re + adj_im[first, :],
        )

    nought = jnp.zeros((1, chan), F32)
    lax.fori_loop(0, groups, link, (nought, nought))
    head = lax.broadcasted_iota(jnp.int32, (tokens, 2 * chan), 0) == 0

    for half, pre_ref, out_ref in ((0, pre_even, out_even), (1, pre_odd, out_odd)):

        @pl.loop(0, half_groups)
        def _(index, half=half, pre_ref=pre_ref, out_ref=out_ref):
            slot = index + half * half_groups
            rows = token_rows(slot, tokens)
            group = group_of(place, half, index)
            before = slot_of(place, lax.max(group - 1, 0), groups)
            tail = jnp.where(group == 0, 0.0, state_ref[before, 0, tokens - 1 :, :])
            prev = jnp.where(head, tail, pltpu.roll(state_ref[slot, 0], 1, 0))
            prev_re = prev[:, :chan]
            prev_im = prev[:, chan:]
            c_re = carry_re[pl.ds(slot, 1), :]
            c_im = carry_im[pl.ds(slot, 1), :]
            p_re = prod_re[rows, :]
            p_im = prod_im[rows, :]
            g_re = adj_re[rows, :] + p_re * c_re - p_im * c_im
            g_im = adj_im[rows, :] + p_re * c_im + p_im * c_re
            turn_re = cosine * prev_re - sine * prev_im
            turn_im = sine * prev_re + cosine * prev_im
            flag = flag_ref[slot, 0]
            pre = pre_ref[index, 0]
            keep, sig = keep_of(pre, flag, bias_ref[...], floor, chan)
            fresh = 1.0 - keep
            x_re = pre[:, :chan]
            x_im = pre[:, chan : 2 * chan]
            s_re = jax.nn.sigmoid(x_re)
            s_im = jax.nn.sigmoid(x_im)
            cand_re = (x_re * s_re).astype(BF).astype(F32)
            cand_im = (x_im * s_im).astype(BF).astype(F32)
            grad_keep = g_re * (turn_re - cand_re) + g_im * (turn_im - cand_im)
            sum_theta[...] -= jnp.sum(
                keep * (g_re * turn_im - g_im * turn_re), axis=0, keepdims=True
            )
            grad_forget = (
                grad_keep * (1.0 - flag) * ((1.0 - floor) * (sig * (1.0 - sig)))
            ).astype(BF)
            sum_bias[...] += jnp.sum(grad_forget.astype(F32), axis=0, keepdims=True)
            out_ref[index, 0, :, 2 * chan : 3 * chan] = grad_forget
            cand_grad = (fresh * g_re).astype(BF).astype(F32)
            out_ref[index, 0, :, :chan] = (
                cand_grad * s_re * (1.0 + x_re * (1.0 - s_re))
            ).astype(BF)
            cand_grad = (fresh * g_im).astype(BF).astype(F32)
            out_ref[index, 0, :, chan : 2 * chan] = (
                cand_grad * s_im * (1.0 + x_im * (1.0 - s_im))
            ).astype(BF)


def block_spec(groups, tokens, width):
    mode = pl.Buffered(1) if groups > 4 and width % 128 and width > 1 else None
    return pl.BlockSpec((groups, 1, tokens, width), lambda b: (0, b, 0, 0), pipeline_mode=mode)


def row_spec(width):
    return pl.BlockSpec((1, width), lambda b: (0, 0))


def recur_forward(place, floor, pre_even, pre_odd, flags, bias, theta, gain):
    groups, seqs, tokens, _ = flags.shape
    chan = bias.shape[1]
    half = groups // 2
    scalar = pl.BlockSpec(memory_space=pltpu.SMEM)
    rows = groups * tokens
    pre_spec = block_spec(half, tokens, 5 * chan)
    one = block_spec(groups, tokens, 1)
    gated = block_spec(half, tokens, 2 * chan)
    gated_shape = jax.ShapeDtypeStruct((half, seqs, tokens, 2 * chan), BF)
    size = seqs * rows * chan
    return pl.pallas_call(
        forward_kernel,
        grid=(seqs,),
        in_specs=[
            scalar,
            scalar,
            pre_spec,
            pre_spec,
            one,
            row_spec(chan),
            row_spec(chan),
            row_spec(2 * chan),
        ],
        out_specs=[block_spec(groups, tokens, 2 * chan), gated, gated, one],
        out_shape=[
            jax.ShapeDtypeStruct((groups, seqs, tokens, 2 * chan), F32),
            gated_shape,
            gated_shape,
            jax.ShapeDtypeStruct((groups, seqs, tokens, 1), F32),
        ],
        scratch_shapes=[pltpu.VMEM((rows, chan), F32)] * 5
        + [pltpu.VMEM((groups, chan), F32)] * 2,
        compiler_params=pltpu.CompilerParams(vmem_limit_bytes=56 * 2**20),
        cost_estimate=pl.CostEstimate(
            flops=60 * size, bytes_accessed=32 * size, transcendentals=5 * size
        ),
        name="recur_forward",
    )(place, floor, pre_even, pre_odd, flags, bias, theta, gain)


def recur_backward(
    place, floor, pre_even, pre_odd, flags, bias, theta, gain, state, up_even, up_odd, scale, term
):
    groups, seqs, tokens, _ = flags.shape
    chan = bias.shape[1]
    half = groups // 2
    scalar = pl.BlockSpec(memory_space=pltpu.SMEM)
    rows = groups * tokens
    pre_spec = block_spec(half, tokens, 5 * chan)
    one = block_spec(groups, tokens, 1)
    up_spec = block_spec(half, tokens, 2 * chan)
    out_shape = jax.ShapeDtypeStruct((half, seqs, tokens, 5 * chan), BF)
    size = seqs * rows * chan
    return pl.pallas_call(
        backward_kernel,
        grid=(seqs,),
        in_specs=[
            scalar,
            scalar,
            pre_spec,
            pre_spec,
            one,
            row_spec(chan),
            row_spec(chan),
            row_spec(2 * chan),
            block_spec(groups, tokens, 2 * chan),
            up_spec,
            up_spec,
            one,
            one,
        ],
        out_specs=[pre_spec, pre_spec, row_spec(chan), row_spec(chan), row_spec(2 * chan)],
        out_shape=[
            out_shape,
            out_shape,
            jax.ShapeDtypeStruct((1, chan), F32),
            jax.ShapeDtypeStruct((1, chan), F32),
            jax.ShapeDtypeStruct((1, 2 * chan), F32),
        ],
        scratch_shapes=[pltpu.VMEM((rows, chan), F32)] * 5
        + [pltpu.VMEM((groups, chan), F32)] * 3,
        compiler_params=pltpu.CompilerParams(vmem_limit_bytes=56 * 2**20),
        cost_estimate=pl.CostEstimate(
            flops=100 * size, bytes_accessed=50 * size, transcendentals=8 * size
        ),
        name="recur_backward",
    )(
        place, floor, pre_even, pre_odd, flags, bias, theta, gain, state, up_even, up_odd, scale, term
    )


def body(
    tokens,
    starts,
    layer_index,
    gain_mix,
    w_in,
    w_forget,
    bias_forget,
    theta,
    w_gate_out,
    gain_out,
    w_out,
    gain_ffn,
    w_ffgate,
    w_ffup,
    w_down,
    out_grad,
):
    seqs, seq_dev, width = tokens.shape
    rows = seqs * seq_dev
    groups = lax.axis_size("seq")
    planes = lax.axis_size("wshard")
    half = groups // 2
    devices = groups * planes
    place = lax.axis_index("seq")
    floor = layer_index.astype(F32) / LAYERS
    mix_run = w_out.shape[0] // groups
    ffn_run = w_down.shape[0] // groups
    chan = mix_run * planes // 2
    hidden = ffn_run * planes

    def own_columns(array, run):
        count = array.shape[1] // (run * groups)
        column = lax.broadcasted_iota(jnp.int32, (array.shape[1], count * run), 0)
        index = lax.broadcasted_iota(jnp.int32, (array.shape[1], count * run), 1)
        block = index // run
        chosen = column == block * (run * groups) + place * run + (index - block * run)
        return dot(array, chosen.astype(BF), "rc,cj->rj").astype(BF)

    def own_parts(vector):
        count = vector.shape[0] // (mix_run * groups)
        split = vector.reshape(count, groups, mix_run)
        return lax.dynamic_slice_in_dim(split, place, 1, 1).reshape(1, count * mix_run)

    def own_rows(array):
        run = array.shape[0] // groups
        return lax.dynamic_slice_in_dim(array, place * run, run, 0)

    resid_in = tokens.reshape(rows, width).astype(F32)
    scale_in = lax.rsqrt(jnp.mean(resid_in * resid_in, axis=1, keepdims=True) + EPS)
    normed_own = (resid_in * scale_in * gain_mix).astype(BF)
    normed_even, normed_odd = gather_seq(normed_own)
    upstream_own = out_grad.reshape(rows, width)

    rec_w = gather_shard(
        jnp.concatenate(
            [
                own_columns(w_in, mix_run),
                own_columns(w_forget, mix_run),
                own_columns(w_gate_out, mix_run),
            ],
            axis=1,
        )
    )
    out_w = gather_shard(own_rows(w_out))
    ff_w = gather_shard(
        jnp.concatenate([own_columns(w_ffgate, ffn_run), own_columns(w_ffup, ffn_run)], axis=1)
    )
    down_w = gather_shard(own_rows(w_down))

    slots = lax.broadcasted_iota(jnp.int32, (groups, groups), 0)
    sources = lax.broadcasted_iota(jnp.int32, (groups, groups), 1)
    keys = jnp.where(slots < half, 2 * slots, 2 * (slots - half) + 1)
    chosen = ((place ^ keys) == sources).astype(F32)
    marks = starts.astype(F32).reshape(seqs, groups, seq_dev).transpose(1, 0, 2)
    flags = jnp.sum(chosen[:, :, None, None] * marks[None], axis=1)[..., None]
    bias_own = own_parts(bias_forget)
    theta_own = own_parts(theta)
    gain_own = own_parts(gain_out)
    place_one = place.reshape(1)

    def blocks(array):
        return array.reshape(half, seqs, seq_dev, -1)

    pre_even = blocks(dot(normed_even, rec_w, "td,dc->tc"))
    pre_odd = blocks(dot(normed_odd, rec_w, "td,dc->tc"))
    state, gated_even, gated_odd, square = recur_forward(
        place_one, floor, pre_even, pre_odd, flags, bias_own, theta_own, gain_own
    )
    gated_even = gated_even.reshape(half * rows, 2 * chan)
    gated_odd = gated_odd.reshape(half * rows, 2 * chan)

    def mix(gated):
        return dot(gated, out_w, "tc,cd->td").astype(BF)

    square_own = scatter_small(square.reshape(groups, rows))
    scale_own = lax.rsqrt(square_own / width + EPS)
    scale_out = scale_own.reshape(rows, 1)
    branch_mix = scale_out * scatter_seq(mix(gated_even), mix(gated_odd))
    resid = resid_in + branch_mix
    scale_ffn = lax.rsqrt(jnp.mean(resid * resid, axis=1, keepdims=True) + EPS)
    ffn_even, ffn_odd = gather_seq((resid * scale_ffn * gain_ffn).astype(BF))
    scale_all = gather_small(scale_own)
    up_even, up_odd = gather_seq(upstream_own)

    def ffn(normed, upstream):
        ff = dot(normed, ff_w, "td,df->tf")
        ffn_gate, ffn_up = ff[:, :hidden], ff[:, hidden:]
        sig_ffn = jax.nn.sigmoid(ffn_gate)
        silu_ffn = ffn_gate * sig_ffn
        ffn_hidden = (silu_ffn * ffn_up).astype(BF)
        grad_hidden = dot(upstream, down_w, "td,fd->tf")
        grad_gate = grad_hidden * ffn_up * sig_ffn * (1.0 + ffn_gate * (1.0 - sig_ffn))
        grad_up = grad_hidden * silu_ffn
        grad_ff = jnp.concatenate([grad_gate.astype(BF), grad_up.astype(BF)], axis=1)
        return ffn_hidden, grad_ff

    hidden_odd, grad_ff_odd = ffn(ffn_odd, up_odd)
    hidden_even, grad_ff_even = ffn(ffn_even, up_even)
    grad_normed_ffn = scatter_seq(
        dot(grad_ff_even, ff_w, "tf,df->td").astype(BF),
        dot(grad_ff_odd, ff_w, "tf,df->td").astype(BF),
    )
    branch_ffn = scatter_seq(
        dot(hidden_even, down_w, "tf,fd->td").astype(BF),
        dot(hidden_odd, down_w, "tf,fd->td").astype(BF),
    )
    result = (resid + branch_ffn).astype(BF)

    scaled_ffn = grad_normed_ffn * gain_ffn
    grad_resid = (
        upstream_own.astype(F32)
        + scale_ffn * scaled_ffn
        - resid * scale_ffn**3 * jnp.mean(scaled_ffn * resid, axis=1, keepdims=True)
    )
    grad_gain_ffn = jnp.sum(grad_normed_ffn * resid * scale_ffn, axis=0)
    grad_branch_own = grad_resid.astype(BF)
    overlap = jnp.sum(grad_branch_own.astype(F32) * branch_mix, axis=1)
    term_all = gather_small((scale_out[:, 0] ** 2 * overlap / width)[None])
    branch_even, branch_odd = gather_seq(grad_branch_own)
    grad_gated_even = blocks(dot(branch_even, out_w, "td,cd->tc"))
    grad_gated_odd = blocks(dot(branch_odd, out_w, "td,cd->tc"))

    shape_one = (groups, seqs, seq_dev, 1)
    grad_even, grad_odd, sum_bias, sum_theta, sum_gain = recur_backward(
        place_one,
        floor,
        pre_even,
        pre_odd,
        flags,
        bias_own,
        theta_own,
        gain_own,
        state,
        grad_gated_even,
        grad_gated_odd,
        scale_all.reshape(shape_one),
        term_all.reshape(shape_one),
    )
    grad_even = grad_even.reshape(half * rows, 5 * chan)
    grad_odd = grad_odd.reshape(half * rows, 5 * chan)
    grad_normed_in = scatter_seq(
        dot(grad_even, rec_w, "tc,dc->td").astype(BF),
        dot(grad_odd, rec_w, "tc,dc->td").astype(BF),
    )
    scaled_in = grad_normed_in * gain_mix
    grad_tokens = (
        grad_resid
        + scale_in * scaled_in
        - resid_in * scale_in**3 * jnp.mean(scaled_in * resid_in, axis=1, keepdims=True)
    ).astype(BF)
    grad_gain_mix = jnp.sum(grad_normed_in * resid_in * scale_in, axis=0)

    def pair_dot(left, right, form):
        return dot(left[0], right[0], form) + dot(left[1], right[1], form)

    def to_owner(grad):
        run = grad.shape[0] // devices
        part = grad.astype(BF).reshape(groups, planes, run, -1).transpose(1, 0, 2, 3)
        part = scatter_shard(part.reshape(grad.shape)).reshape(groups, run, -1)
        return lax.all_to_all(part, "seq", split_axis=0, concat_axis=0, tiled=True)

    def columns(part, run):
        source, count, cols = part.shape
        split = part.reshape(source, count, cols // run, run)
        return split.transpose(1, 2, 0, 3).reshape(count, -1).astype(F32)

    scaled_even = (gated_even.astype(F32) * scale_all[:half].reshape(-1, 1)).astype(BF)
    scaled_odd = (gated_odd.astype(F32) * scale_all[half:].reshape(-1, 1)).astype(BF)
    ff_grad = to_owner(
        pair_dot((ffn_even, ffn_odd), (grad_ff_even, grad_ff_odd), "td,tf->df")
    )
    grad_w_ffgate = columns(ff_grad[..., :hidden], ffn_run)
    grad_w_ffup = columns(ff_grad[..., hidden:], ffn_run)
    rec_grad = to_owner(pair_dot((normed_even, normed_odd), (grad_even, grad_odd), "td,tc->dc"))
    grad_w_in = columns(rec_grad[..., : 2 * chan], mix_run)
    grad_w_forget = columns(rec_grad[..., 2 * chan : 3 * chan], mix_run)
    grad_w_gate = columns(rec_grad[..., 3 * chan :], mix_run)

    pairs = [
        (s * planes + w, w * groups + s) for s in range(groups) for w in range(planes)
    ]

    def rows_to_owner(grad):
        part = scatter_shard(grad.astype(BF))
        return lax.ppermute(part, ("seq", "wshard"), pairs).astype(F32)

    grad_w_down = rows_to_owner(
        pair_dot((hidden_even, hidden_odd), (up_even, up_odd), "tf,td->fd")
    )
    grad_w_out = rows_to_owner(
        pair_dot((scaled_even, scaled_odd), (branch_even, branch_odd), "tc,td->cd")
    )

    def spread(part):
        count = part.shape[1] // mix_run
        zero = jnp.zeros((count, groups, mix_run), F32)
        zero = lax.dynamic_update_slice(zero, part.reshape(count, 1, mix_run), (0, place, 0))
        return zero.reshape(-1)

    pieces = [
        spread(sum_bias),
        spread(sum_theta),
        spread(sum_gain),
        grad_gain_ffn,
        grad_gain_mix,
        jnp.stack(
            [
                jnp.sum(resid_in * resid_in),
                jnp.sum(branch_mix * branch_mix),
                jnp.sum(branch_ffn * branch_ffn),
            ]
        ),
    ]
    sums = sum_all(jnp.concatenate(pieces))
    cuts = []
    offset = 0
    for piece in pieces:
        cuts.append(sums[offset : offset + piece.shape[0]])
        offset += piece.shape[0]
    grad_bias, grad_theta, grad_gain_out, grad_gain_ffn, grad_gain_mix, squares = cuts
    rms_values = jnp.sqrt(squares / (rows * width * devices))
    return (
        result.reshape(seqs, seq_dev, width),
        grad_tokens.reshape(seqs, seq_dev, width),
        grad_gain_mix,
        grad_w_in,
        grad_w_forget,
        grad_bias,
        grad_theta,
        grad_w_gate,
        grad_gain_out,
        grad_w_out,
        grad_gain_ffn,
        grad_w_ffgate,
        grad_w_ffup,
        grad_w_down,
        rms_values,
    )


def solution(mesh):
    whole = P()
    rowed = P("wshard", None)
    stream = P("wshard", "seq", None)
    owned = P(("seq", "wshard"), None)
    return jax.shard_map(
        body,
        mesh=mesh,
        in_specs=(
            stream,
            rowed,
            whole,
            whole,
            rowed,
            rowed,
            whole,
            whole,
            rowed,
            whole,
            rowed,
            whole,
            rowed,
            rowed,
            rowed,
            stream,
        ),
        out_specs=(
            stream,
            stream,
            whole,
            owned,
            owned,
            whole,
            whole,
            owned,
            whole,
            owned,
            whole,
            owned,
            owned,
            owned,
            whole,
        ),
        check_vma=False,
    )
```

```python
import functools

import jax
import jax.numpy as jnp
from jax import lax
from jax.experimental import pallas as pl
from jax.experimental.pallas import tpu as pltpu
from jax.sharding import PartitionSpec as P

LAYERS = 24
EPS = 1e-06
BF = jnp.bfloat16
F32 = jnp.float32


def dot(left, right, form):
    return jnp.einsum(form, left, right, preferred_element_type=F32)


def swap(value, bit):
    size = lax.axis_size("seq")
    return lax.ppermute(value, "seq", [(i, i ^ bit) for i in range(size)])


def chip_bits():
    size = lax.axis_size("seq")
    return [1 << i for i in range(1, size.bit_length() - 1)]


def plain_even(own):
    bits = chip_bits()
    if len(bits) == 2:
        first, second = bits
        half = own.shape[0] // 2
        from_first = swap(own, first)
        from_second = swap(own, second)
        top = swap(from_first[:half], second)
        low = swap(from_second[half:], first)
        return jnp.concatenate([own, from_first, from_second, top, low], axis=0)
    held = own
    for bit in bits:
        held = jnp.concatenate([held, swap(held, bit)], axis=0)
    return held


def plain_gather(own):
    even = plain_even(own)
    return even, swap(even, 1)


def plain_scatter(even, odd):
    bits = chip_bits()
    joint = even.astype(F32) + swap(odd, 1).astype(F32)
    if len(bits) == 2:
        first, second = bits
        rows = joint.shape[0] // 4
        half = rows // 2
        low_joint = joint.astype(BF)
        near_first, near_second, far = (
            low_joint[rows : 2 * rows],
            low_joint[2 * rows : 3 * rows],
            low_joint[3 * rows :],
        )
        far_top = swap(far[:half], first)
        far_low = swap(far[half:], second)
        first_top = swap(near_first[:half], first)
        second_low = swap(near_second[half:], second)
        first_low = swap((near_first[half:].astype(F32) + far_low.astype(F32)).astype(BF), first)
        second_top = swap(
            (near_second[:half].astype(F32) + far_top.astype(F32)).astype(BF), second
        )
        first_all = jnp.concatenate([first_top, first_low], axis=0).astype(F32)
        second_all = jnp.concatenate([second_top, second_low], axis=0).astype(F32)
        return joint[:rows] + first_all + second_all
    for bit in reversed(bits):
        half = joint.shape[0] // 2
        joint = joint[:half] + swap(joint[half:].astype(BF), bit).astype(F32)
    return joint


def gather_first(own):
    return tuple(swap(own, bit) for bit in chip_bits())


def gather_far(own, stage):
    first, second = chip_bits()
    half = own.shape[0] // 2
    return swap(stage[0][:half], second), swap(stage[1][half:], first)


def cross(pieces):
    return tuple(swap(piece, 1) for piece in pieces)


def joints(even, crossed):
    half = even[0].shape[0] // 2
    sums = []
    for index in (1, 2, 3):
        for rows in (slice(0, half), slice(half, None)):
            both = even[index][rows].astype(F32) + crossed[index][rows].astype(F32)
            sums.append(both.astype(BF))
    return tuple(sums)


def scatter_first(sums):
    first, second = chip_bits()
    return swap(sums[4], first), swap(sums[5], second), swap(sums[0], first), swap(sums[3], second)


def scatter_last(even, crossed, sums, stage):
    first, second = chip_bits()
    far_top, far_low, first_top, second_low = stage
    first_low = swap((sums[1].astype(F32) + far_low.astype(F32)).astype(BF), first)
    second_top = swap((sums[2].astype(F32) + far_top.astype(F32)).astype(BF), second)
    first_all = jnp.concatenate([first_top, first_low], axis=0).astype(F32)
    second_all = jnp.concatenate([second_top, second_low], axis=0).astype(F32)
    return even[0].astype(F32) + crossed[0].astype(F32) + first_all + second_all


def tied(*values):
    return lax.optimization_barrier(values)


def grow(held, bit):
    return jnp.concatenate([held, swap(held, bit)], axis=0)


def shrink(blocks, bit):
    half = blocks.shape[0] // 2
    return blocks[:half] + swap(blocks[half:], bit)


def slot_rows(held):
    pairs = held.reshape(held.shape[0] // 2, 2, -1)
    return pairs.transpose(1, 0, 2).reshape(held.shape)


def gather_small(own):
    for bit in [1] + chip_bits():
        own = grow(own, bit)
    return slot_rows(own)


def scatter_small(blocks):
    for bit in [1] + list(reversed(chip_bits())):
        blocks = shrink(blocks, bit)
    return blocks


def sum_all(value):
    for bit in [1] + chip_bits():
        value = value + swap(value, bit)
    planes = lax.axis_size("wshard")
    bit = 1
    while bit < planes:
        value = value + lax.ppermute(value, "wshard", [(i, i ^ bit) for i in range(planes)])
        bit *= 2
    return value


LANES = 128
SMALL = pl.CostEstimate(flops=1024, transcendentals=0, bytes_accessed=1024)


def filler(flops):
    return pl.CostEstimate(flops=flops, transcendentals=0, bytes_accessed=1024)


def pack(arrays):
    lines = []
    for array in arrays:
        count, rows, cols = array.shape
        split = array.reshape(count, rows, cols // LANES, LANES).transpose(0, 2, 1, 3)
        lines.append(split.reshape(count, rows * cols // LANES, LANES))
    return jnp.concatenate(lines, axis=1)


def gather_packed(packed):
    return lax.all_gather(packed, "wshard", axis=0, tiled=True)


def scatter_packed(packed):
    return lax.psum_scatter(
        packed.reshape(-1, LANES), "wshard", scatter_dimension=0, tiled=True
    )


def after(value, *others):
    return lax.optimization_barrier((value, others))[0]


def slot_of(place, group, groups):
    key = place ^ group
    return (key >> 1) + (key & 1) * (groups // 2)


def group_of(place, half, index):
    return place ^ ((index << 1) | half)


def token_rows(slot, tokens):
    return pl.ds(pl.multiple_of(slot * tokens, tokens), tokens)


def keep_of(pre, flag, bias, floor, chan):
    logit = (pre[:, 2 * chan : 3 * chan] + bias).astype(BF).astype(F32)
    sig = jax.nn.sigmoid(logit)
    return (floor + (1.0 - floor) * sig) * (1.0 - flag), sig


def forward_kernel(
    place_ref,
    floor_ref,
    pre_even,
    pre_odd,
    flag_ref,
    bias_ref,
    theta_ref,
    gain_ref,
    state_ref,
    gated_even,
    gated_odd,
    square_ref,
    keep_s,
    val_re,
    val_im,
    prod_re,
    prod_im,
    carry_re,
    carry_im,
):
    groups, _, tokens, _ = flag_ref.shape
    chan = keep_s.shape[1]
    half_groups = groups // 2
    floor = floor_ref[0]
    place = place_ref[0]
    cosine = jnp.cos(theta_ref[...])
    sine = jnp.sin(theta_ref[...])

    for half, pre_ref in ((0, pre_even), (1, pre_odd)):

        @pl.loop(0, half_groups)
        def _(index, half=half, pre_ref=pre_ref):
            slot = index + half * half_groups
            rows = token_rows(slot, tokens)
            pre = pre_ref[index, 0]
            keep, _ = keep_of(pre, flag_ref[slot, 0], bias_ref[...], floor, chan)
            keep_s[rows, :] = keep
            fresh = 1.0 - keep
            value = pre[:, :chan]
            val_re[rows, :] = fresh * (value * jax.nn.sigmoid(value)).astype(BF).astype(F32)
            value = pre[:, chan : 2 * chan]
            val_im[rows, :] = fresh * (value * jax.nn.sigmoid(value)).astype(BF).astype(F32)

    def step(t, carry):
        h_re, h_im, p_re, p_im = carry
        rows = pl.ds(t, groups, stride=tokens)
        held = keep_s[rows, :]
        a_re = held * cosine
        a_im = held * sine
        n_re = a_re * h_re - a_im * h_im + val_re[rows, :]
        n_im = a_re * h_im + a_im * h_re + val_im[rows, :]
        q_re = a_re * p_re - a_im * p_im
        q_im = a_re * p_im + a_im * p_re
        val_re[rows, :] = n_re
        val_im[rows, :] = n_im
        prod_re[rows, :] = q_re
        prod_im[rows, :] = q_im
        return n_re, n_im, q_re, q_im

    zero = jnp.zeros((groups, chan), F32)
    lax.fori_loop(0, tokens, step, (zero, zero, zero + 1.0, zero), unroll=8)

    def link(group, carry):
        c_re, c_im = carry
        slot = slot_of(place, group, groups)
        carry_re[pl.ds(slot, 1), :] = c_re
        carry_im[pl.ds(slot, 1), :] = c_im
        last = pl.ds(slot * tokens + tokens - 1, 1)
        p_re = prod_re[last, :]
        p_im = prod_im[last, :]
        return (
            p_re * c_re - p_im * c_im + val_re[last, :],
            p_re * c_im + p_im * c_re + val_im[last, :],
        )

    nought = jnp.zeros((1, chan), F32)
    lax.fori_loop(0, groups, link, (nought, nought))

    for half, pre_ref, gated_ref in ((0, pre_even, gated_even), (1, pre_odd, gated_odd)):

        @pl.loop(0, half_groups)
        def _(index, half=half, pre_ref=pre_ref, gated_ref=gated_ref):
            slot = index + half * half_groups
            rows = token_rows(slot, tokens)
            c_re = carry_re[pl.ds(slot, 1), :]
            c_im = carry_im[pl.ds(slot, 1), :]
            p_re = prod_re[rows, :]
            p_im = prod_im[rows, :]
            h_re = val_re[rows, :] + p_re * c_re - p_im * c_im
            h_im = val_im[rows, :] + p_re * c_im + p_im * c_re
            state_ref[slot, 0, :, :chan] = h_re
            state_ref[slot, 0, :, chan:] = h_im
            m_re = h_re.astype(BF).astype(F32)
            m_im = h_im.astype(BF).astype(F32)
            gate = jax.nn.sigmoid(pre_ref[index, 0, :, 3 * chan :]) * gain_ref[...]
            gated_ref[index, 0, :, :chan] = (m_re * gate[:, :chan]).astype(BF)
            gated_ref[index, 0, :, chan:] = (m_im * gate[:, chan:]).astype(BF)
            square_ref[slot, 0] = jnp.sum(m_re * m_re + m_im * m_im, axis=1, keepdims=True)


def backward_kernel(
    place_ref,
    floor_ref,
    pre_even,
    pre_odd,
    flag_ref,
    bias_ref,
    theta_ref,
    gain_ref,
    state_ref,
    up_even,
    up_odd,
    scale_ref,
    term_ref,
    out_even,
    out_odd,
    scaled_even,
    scaled_odd,
    sum_bias,
    sum_theta,
    sum_gain,
    keep_s,
    adj_re,
    adj_im,
    prod_re,
    prod_im,
    carry_re,
    carry_im,
    next_s,
):
    groups, _, tokens, _ = flag_ref.shape
    chan = keep_s.shape[1]
    half_groups = groups // 2
    floor = floor_ref[0]
    place = place_ref[0]
    cosine = jnp.cos(theta_ref[...])
    sine = jnp.sin(theta_ref[...])

    @pl.when(pl.program_id(0) == 0)
    def _():
        sum_bias[...] = jnp.zeros_like(sum_bias)
        sum_theta[...] = jnp.zeros_like(sum_theta)
        sum_gain[...] = jnp.zeros_like(sum_gain)

    for half, pre_ref, up_ref, out_ref, scaled_ref in (
        (0, pre_even, up_even, out_even, scaled_even),
        (1, pre_odd, up_odd, out_odd, scaled_odd),
    ):

        @pl.loop(0, half_groups)
        def _(
            index, half=half, pre_ref=pre_ref, up_ref=up_ref, out_ref=out_ref, scaled_ref=scaled_ref
        ):
            slot = index + half * half_groups
            rows = token_rows(slot, tokens)
            pre = pre_ref[index, 0]
            keep, _ = keep_of(pre, flag_ref[slot, 0], bias_ref[...], floor, chan)
            keep_s[rows, :] = keep
            scale = scale_ref[slot, 0]
            mixed = state_ref[slot, 0].astype(BF).astype(F32)
            sig = jax.nn.sigmoid(pre[:, 3 * chan :])
            inner = up_ref[index, 0] * sig
            scaled_ref[index, 0] = (mixed * gain_ref[...] * sig * scale).astype(BF)
            normed = inner * mixed * scale
            sum_gain[...] += jnp.sum(normed, axis=0, keepdims=True)
            out_ref[index, 0, :, 3 * chan :] = (normed * gain_ref[...] * (1.0 - sig)).astype(BF)
            grad = (scale * (inner * gain_ref[...]) - mixed * term_ref[slot, 0]).astype(BF)
            adj_re[rows, :] = grad[:, :chan].astype(F32)
            adj_im[rows, :] = grad[:, chan:].astype(F32)

    @pl.loop(0, groups)
    def _(group):
        slot = slot_of(place, group, groups)
        after = slot_of(place, lax.min(group + 1, groups - 1), groups)
        row = keep_s[pl.ds(after * tokens, 1), :]
        next_s[pl.ds(slot, 1), :] = jnp.where(group == groups - 1, 0.0, row)

    def turn(t, held, carry):
        g_re, g_im, p_re, p_im = carry
        rows = pl.ds(t, groups, stride=tokens)
        a_re = held * cosine
        a_im = held * sine
        n_re = a_re * g_re + a_im * g_im + adj_re[rows, :]
        n_im = a_re * g_im - a_im * g_re + adj_im[rows, :]
        q_re = a_re * p_re + a_im * p_im
        q_im = a_re * p_im - a_im * p_re
        adj_re[rows, :] = n_re
        adj_im[rows, :] = n_im
        prod_re[rows, :] = q_re
        prod_im[rows, :] = q_im
        return n_re, n_im, q_re, q_im

    def step(index, carry):
        t = tokens - 2 - index
        return turn(t, keep_s[pl.ds(t + 1, groups, stride=tokens), :], carry)

    zero = jnp.zeros((groups, chan), F32)
    carry = turn(tokens - 1, next_s[...], (zero, zero, zero + 1.0, zero))
    lax.fori_loop(0, tokens - 1, step, carry, unroll=4)

    def link(index, carry):
        c_re, c_im = carry
        slot = slot_of(place, groups - 1 - index, groups)
        carry_re[pl.ds(slot, 1), :] = c_re
        carry_im[pl.ds(slot, 1), :] = c_im
        first = pl.ds(slot * tokens, 1)
        p_re = prod_re[first, :]
        p_im = prod_im[first, :]
        return (
            p_re * c_re - p_im * c_im + adj_re[first, :],
            p_re * c_im + p_im * c_re + adj_im[first, :],
        )

    nought = jnp.zeros((1, chan), F32)
    lax.fori_loop(0, groups, link, (nought, nought))
    head = lax.broadcasted_iota(jnp.int32, (tokens, 2 * chan), 0) == 0

    for half, pre_ref, out_ref in ((0, pre_even, out_even), (1, pre_odd, out_odd)):

        @pl.loop(0, half_groups)
        def _(index, half=half, pre_ref=pre_ref, out_ref=out_ref):
            slot = index + half * half_groups
            rows = token_rows(slot, tokens)
            group = group_of(place, half, index)
            before = slot_of(place, lax.max(group - 1, 0), groups)
            tail = jnp.where(group == 0, 0.0, state_ref[before, 0, tokens - 1 :, :])
            prev = jnp.where(head, tail, pltpu.roll(state_ref[slot, 0], 1, 0))
            prev_re = prev[:, :chan]
            prev_im = prev[:, chan:]
            c_re = carry_re[pl.ds(slot, 1), :]
            c_im = carry_im[pl.ds(slot, 1), :]
            p_re = prod_re[rows, :]
            p_im = prod_im[rows, :]
            g_re = adj_re[rows, :] + p_re * c_re - p_im * c_im
            g_im = adj_im[rows, :] + p_re * c_im + p_im * c_re
            turn_re = cosine * prev_re - sine * prev_im
            turn_im = sine * prev_re + cosine * prev_im
            flag = flag_ref[slot, 0]
            pre = pre_ref[index, 0]
            keep, sig = keep_of(pre, flag, bias_ref[...], floor, chan)
            fresh = 1.0 - keep
            x_re = pre[:, :chan]
            x_im = pre[:, chan : 2 * chan]
            s_re = jax.nn.sigmoid(x_re)
            s_im = jax.nn.sigmoid(x_im)
            cand_re = (x_re * s_re).astype(BF).astype(F32)
            cand_im = (x_im * s_im).astype(BF).astype(F32)
            grad_keep = g_re * (turn_re - cand_re) + g_im * (turn_im - cand_im)
            sum_theta[...] -= jnp.sum(
                keep * (g_re * turn_im - g_im * turn_re), axis=0, keepdims=True
            )
            grad_forget = (
                grad_keep * (1.0 - flag) * ((1.0 - floor) * (sig * (1.0 - sig)))
            ).astype(BF)
            sum_bias[...] += jnp.sum(grad_forget.astype(F32), axis=0, keepdims=True)
            out_ref[index, 0, :, 2 * chan : 3 * chan] = grad_forget
            cand_grad = (fresh * g_re).astype(BF).astype(F32)
            out_ref[index, 0, :, :chan] = (
                cand_grad * s_re * (1.0 + x_re * (1.0 - s_re))
            ).astype(BF)
            cand_grad = (fresh * g_im).astype(BF).astype(F32)
            out_ref[index, 0, :, chan : 2 * chan] = (
                cand_grad * s_im * (1.0 + x_im * (1.0 - s_im))
            ).astype(BF)


def block_spec(groups, tokens, width):
    mode = pl.Buffered(1) if groups > 4 and width % 128 and width > 1 else None
    return pl.BlockSpec((groups, 1, tokens, width), lambda b: (0, b, 0, 0), pipeline_mode=mode)


def row_spec(width):
    return pl.BlockSpec((1, width), lambda b: (0, 0))


def recur_forward(place, floor, pre_even, pre_odd, flags, bias, theta, gain):
    groups, seqs, tokens, _ = flags.shape
    chan = bias.shape[1]
    half = groups // 2
    scalar = pl.BlockSpec(memory_space=pltpu.SMEM)
    rows = groups * tokens
    pre_spec = block_spec(half, tokens, 5 * chan)
    one = block_spec(groups, tokens, 1)
    gated = block_spec(half, tokens, 2 * chan)
    gated_shape = jax.ShapeDtypeStruct((half, seqs, tokens, 2 * chan), BF)
    size = seqs * rows * chan
    return pl.pallas_call(
        forward_kernel,
        grid=(seqs,),
        in_specs=[
            scalar,
            scalar,
            pre_spec,
            pre_spec,
            one,
            row_spec(chan),
            row_spec(chan),
            row_spec(2 * chan),
        ],
        out_specs=[block_spec(groups, tokens, 2 * chan), gated, gated, one],
        out_shape=[
            jax.ShapeDtypeStruct((groups, seqs, tokens, 2 * chan), F32),
            gated_shape,
            gated_shape,
            jax.ShapeDtypeStruct((groups, seqs, tokens, 1), F32),
        ],
        scratch_shapes=[pltpu.VMEM((rows, chan), F32)] * 5
        + [pltpu.VMEM((groups, chan), F32)] * 2,
        compiler_params=pltpu.CompilerParams(vmem_limit_bytes=56 * 2**20),
        cost_estimate=SMALL,
        name="recur_forward",
    )(place, floor, pre_even, pre_odd, flags, bias, theta, gain)


def recur_backward(
    place, floor, pre_even, pre_odd, flags, bias, theta, gain, state, up_even, up_odd, scale, term
):
    groups, seqs, tokens, _ = flags.shape
    chan = bias.shape[1]
    half = groups // 2
    scalar = pl.BlockSpec(memory_space=pltpu.SMEM)
    rows = groups * tokens
    pre_spec = block_spec(half, tokens, 5 * chan)
    one = block_spec(groups, tokens, 1)
    up_spec = block_spec(half, tokens, 2 * chan)
    out_shape = jax.ShapeDtypeStruct((half, seqs, tokens, 5 * chan), BF)
    scaled_shape = jax.ShapeDtypeStruct((half, seqs, tokens, 2 * chan), BF)
    size = seqs * rows * chan
    return pl.pallas_call(
        backward_kernel,
        grid=(seqs,),
        in_specs=[
            scalar,
            scalar,
            pre_spec,
            pre_spec,
            one,
            row_spec(chan),
            row_spec(chan),
            row_spec(2 * chan),
            block_spec(groups, tokens, 2 * chan),
            up_spec,
            up_spec,
            one,
            one,
        ],
        out_specs=[
            pre_spec,
            pre_spec,
            up_spec,
            up_spec,
            row_spec(chan),
            row_spec(chan),
            row_spec(2 * chan),
        ],
        out_shape=[
            out_shape,
            out_shape,
            scaled_shape,
            scaled_shape,
            jax.ShapeDtypeStruct((1, chan), F32),
            jax.ShapeDtypeStruct((1, chan), F32),
            jax.ShapeDtypeStruct((1, 2 * chan), F32),
        ],
        scratch_shapes=[pltpu.VMEM((rows, chan), F32)] * 5
        + [pltpu.VMEM((groups, chan), F32)] * 3,
        compiler_params=pltpu.CompilerParams(vmem_limit_bytes=56 * 2**20),
        cost_estimate=SMALL,
        name="recur_backward",
    )(
        place, floor, pre_even, pre_odd, flags, bias, theta, gain, state, up_even, up_odd, scale, term
    )


def unpack_columns(packed, out):
    planes = packed.shape[0]
    rows = out.shape[0] // planes
    for plane in range(planes):
        for tile in range(out.shape[1] // LANES):
            out[plane * rows : (plane + 1) * rows, tile * LANES : (tile + 1) * LANES] = packed[
                plane, tile * rows : (tile + 1) * rows, :
            ]


def unpack_rows(packed, first, out):
    planes = packed.shape[0]
    rows = out.shape[0] // planes
    for plane in range(planes):
        for tile in range(out.shape[1] // LANES):
            base = first + tile * rows
            out[plane * rows : (plane + 1) * rows, tile * LANES : (tile + 1) * LANES] = packed[
                plane, base : base + rows, :
            ]


def dot_nn(left, right):
    return jnp.dot(left, right, preferred_element_type=F32)


def dot_nt(left, right):
    return lax.dot_general(left, right, (((1,), (1,)), ((), ())), preferred_element_type=F32)


def dot_tn(left, right):
    return lax.dot_general(left, right, (((0,), (0,)), ((), ())), preferred_element_type=F32)


def dot_nn(left, right):
    return jnp.dot(left, right, preferred_element_type=F32)


def dot_nt(left, right):
    return lax.dot_general(left, right, (((1,), (1,)), ((), ())), preferred_element_type=F32)


def dot_tn(left, right):
    return lax.dot_general(left, right, (((0,), (0,)), ((), ())), preferred_element_type=F32)


PIECES = 5
ANYWHERE = pl.BlockSpec(memory_space=pl.ANY)
SCALAR = pl.BlockSpec(memory_space=pltpu.SMEM)


def slot_copies(pieces, held, sems, slot):
    if slot < 3:
        return [pltpu.make_async_copy(pieces[slot], held.at[slot], sems.at[slot])]
    half = held.shape[1] // 2
    return [
        pltpu.make_async_copy(
            pieces[3 + part], held.at[3, part * half : (part + 1) * half], sems.at[3 + part]
        )
        for part in range(2)
    ]


def ffn_kernel(based, last, *refs):
    packed_ref = refs[0]
    normed, up = refs[1 : 1 + PIECES], refs[1 + PIECES : 1 + 2 * PIECES]
    rest = list(refs[1 + 2 * PIECES :])
    base_ref = rest.pop(0) if based else None
    hidden_ref, grad_ref = rest[:2]
    backs = rest[2 : 6 if last else 3]
    ff_s, down_s, normed_s, up_s, normed_sems, up_sems = rest[6 if last else 3 :]
    hidden = down_s.shape[0]
    step = pl.program_id(0)
    slots = normed_s.shape[0]

    @pl.when(step == 0)
    def _():
        for slot in range(slots):
            for copy in slot_copies(normed, normed_s, normed_sems, slot):
                copy.start()
            for copy in slot_copies(up, up_s, up_sems, slot):
                copy.start()
        first = ff_s.shape[0] // packed_ref.shape[0] * (ff_s.shape[1] // LANES)
        unpack_columns(packed_ref, ff_s)
        unpack_rows(packed_ref, first, down_s)

    for slot in range(slots):

        @pl.when(step == slot)
        def _(slot=slot):
            for copy in slot_copies(normed, normed_s, normed_sems, slot):
                copy.wait()
            for copy in slot_copies(up, up_s, up_sems, slot):
                copy.wait()

    ff = dot_nn(normed_s[step], ff_s[...])
    gate, value = ff[:, :hidden], ff[:, hidden:]
    sig = jax.nn.sigmoid(gate)
    silu = gate * sig
    hidden_ref[...] = (silu * value).astype(BF)
    grad = dot_nt(up_s[step], down_s[...])
    grad_ref[:, :hidden] = (grad * value * sig * (1.0 + gate * (1.0 - sig))).astype(BF)
    grad_ref[:, hidden:] = (grad * silu).astype(BF)
    back = dot_nt(grad_ref[...], ff_s[...])
    if based:
        back = back + base_ref[...]
    if last:
        for slot in range(slots):

            @pl.when(step == slot)
            def _(slot=slot):
                backs[slot][...] = back.astype(BF)
    else:
        backs[0][...] = back


def ffn_call(normed, upstream, packed, ff_cols, base, last):
    rows, width = normed[0].shape
    slots = 4
    tokens = slots * rows
    hidden = ff_cols // 2
    wide = pl.BlockSpec((rows, width), lambda i: (i, 0))
    whole = pl.BlockSpec((rows, width), lambda i: (0, 0))
    operands = [packed, *normed, *upstream]
    in_specs = [
        pl.BlockSpec(packed.shape, lambda i: (0, 0, 0), pipeline_mode=pl.Buffered(1)),
    ] + [ANYWHERE] * (2 * PIECES)
    if base is not None:
        operands.append(base)
        in_specs.append(wide)
    backs = [jax.ShapeDtypeStruct((tokens, width), F32)]
    if last:
        backs = [jax.ShapeDtypeStruct((rows, width), BF)] * slots
    return pl.pallas_call(
        functools.partial(ffn_kernel, base is not None, last),
        grid=(slots,),
        in_specs=in_specs,
        out_specs=[
            pl.BlockSpec((rows, hidden), lambda i: (i, 0)),
            pl.BlockSpec((rows, ff_cols), lambda i: (i, 0)),
        ]
        + ([whole] * slots if last else [wide]),
        out_shape=[
            jax.ShapeDtypeStruct((tokens, hidden), BF),
            jax.ShapeDtypeStruct((tokens, ff_cols), BF),
            *backs,
        ],
        scratch_shapes=[
            pltpu.VMEM((width, ff_cols), BF),
            pltpu.VMEM((hidden, width), BF),
            pltpu.VMEM((slots, rows, width), BF),
            pltpu.VMEM((slots, rows, width), BF),
            pltpu.SemaphoreType.DMA((PIECES,)),
            pltpu.SemaphoreType.DMA((PIECES,)),
        ],
        compiler_params=pltpu.CompilerParams(vmem_limit_bytes=56 * 2**20),
        cost_estimate=SMALL,
        name="ffn",
    )(*operands)


def grads_kernel(planes, *refs):
    left = refs[: 2 * PIECES]
    up = refs[2 * PIECES : 4 * PIECES]
    cols_even, cols_odd, rows_even, rows_odd, out_ref = refs[4 * PIECES :]
    step = pl.program_id(0)
    steps = pl.num_programs(0)
    block = left[0].shape[1]
    run = block // planes
    tiles = cols_even.shape[1] // LANES
    count = rows_even.shape[1] // planes

    def joined(pieces):
        return jnp.concatenate([piece[...] for piece in pieces], axis=0)

    grad = dot_tn(joined(left[:PIECES]), cols_even[...])
    grad = (grad + dot_tn(joined(left[PIECES:]), cols_odd[...])).astype(BF)
    for plane in range(planes):
        for tile in range(tiles):
            lines = pl.ds(pl.multiple_of((step * tiles + tile) * run, run), run)
            out_ref[plane, lines, :] = grad[
                plane * run : (plane + 1) * run, tile * LANES : (tile + 1) * LANES
            ]
    grad = dot_tn(rows_even[...], joined(up[:PIECES]))
    grad = (grad + dot_tn(rows_odd[...], joined(up[PIECES:]))).astype(BF)
    first = block // planes * tiles * steps
    for plane in range(planes):
        for tile in range(block // LANES):
            base = first + (step * (block // LANES) + tile) * count
            lines = pl.ds(pl.multiple_of(base, 16), count)
            out_ref[plane, lines, :] = grad[
                plane * count : (plane + 1) * count, tile * LANES : (tile + 1) * LANES
            ]


def grads_call(groups, planes, left, cols, rows, up):
    width = left[0][0].shape[1]
    tokens = cols[0].shape[0]
    block = width // groups
    col_count = cols[0].shape[1]
    row_count = rows[0].shape[1]
    lines = (col_count * width + row_count * width) // (planes * LANES)
    pieces = [*left[0], *left[1], *up[0], *up[1]]

    def whole(array):
        return pl.BlockSpec(array.shape, lambda i: (0, 0), pipeline_mode=pl.Buffered(1))

    return pl.pallas_call(
        functools.partial(grads_kernel, planes),
        grid=(groups,),
        in_specs=[pl.BlockSpec((piece.shape[0], block), lambda i: (0, i)) for piece in pieces]
        + [whole(cols[0]), whole(cols[1]), whole(rows[0]), whole(rows[1])],
        out_specs=pl.BlockSpec((planes, lines, LANES), lambda i: (0, 0, 0)),
        out_shape=jax.ShapeDtypeStruct((planes, lines, LANES), BF),
        compiler_params=pltpu.CompilerParams(vmem_limit_bytes=56 * 2**20),
        cost_estimate=filler(4 * tokens * width * (col_count + row_count)),
        name="weight_grads",
    )(*pieces, *cols, *rows)


def result_kernel(firsts, *refs):
    hidden_first, hidden_second, packed_first, packed_second = refs[:4]
    outs, down_s = refs[4:-1], refs[-1]
    rows = hidden_first.shape[1]
    step = pl.program_id(0)

    @pl.when(step == 0)
    def _():
        unpack_rows(packed_first, firsts[0], down_s.at[:rows])
        unpack_rows(packed_second, firsts[1], down_s.at[rows:])

    out = dot_nn(hidden_first[...], down_s[:rows, :]) + dot_nn(hidden_second[...], down_s[rows:, :])
    for slot in range(len(outs)):

        @pl.when(step == slot)
        def _(slot=slot):
            outs[slot][...] = out.astype(BF)


def result_call(hidden, packed, width):
    slots = 4
    tokens = hidden[0].shape[0]
    rows = tokens // slots
    total = sum(item.shape[1] for item in hidden)
    firsts = tuple(
        part.shape[1] - item.shape[1] // part.shape[0] * width // LANES
        for part, item in zip(packed, hidden)
    )
    return pl.pallas_call(
        functools.partial(result_kernel, firsts),
        grid=(slots,),
        in_specs=[pl.BlockSpec((rows, item.shape[1]), lambda i: (i, 0)) for item in hidden]
        + [
            pl.BlockSpec(part.shape, lambda i: (0, 0, 0), pipeline_mode=pl.Buffered(1))
            for part in packed
        ],
        out_specs=[pl.BlockSpec((rows, width), lambda i: (0, 0))] * slots,
        out_shape=[jax.ShapeDtypeStruct((rows, width), BF)] * slots,
        scratch_shapes=[pltpu.VMEM((total, width), BF)],
        compiler_params=pltpu.CompilerParams(vmem_limit_bytes=48 * 2**20),
        cost_estimate=filler(2 * tokens * width * total),
        name="ffn_result",
    )(*hidden, *packed)


def seq_copies(pieces, held, sems, seq):
    tokens = held.shape[2]
    rows = slice(seq * tokens, (seq + 1) * tokens)
    copies = [
        pltpu.make_async_copy(pieces[slot].at[rows], held.at[seq, slot], sems.at[seq, slot])
        for slot in range(3)
    ]
    copies.append(pltpu.make_async_copy(pieces[3 + seq], held.at[seq, 3], sems.at[seq, 3]))
    return copies


def fetch(groups):
    seqs = groups[0][1].shape[0]

    @pl.when(pl.program_id(0) == 0)
    def _():
        for seq in range(seqs):
            for pieces, held, sems in groups:
                for copy in seq_copies(pieces, held, sems, seq):
                    copy.start()


def arrive(groups):
    for seq in range(groups[0][1].shape[0]):

        @pl.when(pl.program_id(0) == seq)
        def _(seq=seq):
            for pieces, held, sems in groups:
                for copy in seq_copies(pieces, held, sems, seq):
                    copy.wait()


def unpack_mix(packed_ref, rec_s, out_s):
    @pl.when(pl.program_id(0) == 0)
    def _():
        lines = rec_s.shape[0] // packed_ref.shape[0] * (rec_s.shape[1] // LANES)
        unpack_columns(packed_ref, rec_s)
        unpack_rows(packed_ref, lines, out_s)


def mix_forward_kernel(*refs):
    place_ref, floor_ref, packed_ref, flag_ref, bias_ref, theta_ref, gain_ref = refs[:7]
    refs = refs[7:]
    even, odd = refs[:PIECES], refs[PIECES : 2 * PIECES]
    refs = refs[2 * PIECES :]
    pre_even, pre_odd, state_ref, square_ref = refs[:4]
    mix_even, mix_odd = refs[4:8], refs[8:12]
    rec_s, out_s, gated_even, gated_odd, x_even, x_odd, sems_even, sems_odd = refs[12:20]
    scratch = refs[20:]
    half, _, tokens, _ = pre_even.shape
    seq = pl.program_id(0)
    groups = ((even, x_even, sems_even), (odd, x_odd, sems_odd))
    fetch(groups)
    unpack_mix(packed_ref, rec_s, out_s)
    arrive(groups)
    for x_ref, pre_ref in ((x_even, pre_even), (x_odd, pre_odd)):

        @pl.loop(0, half, step=2)
        def _(index, x_ref=x_ref, pre_ref=pre_ref):
            pair = pl.ds(index, 2)
            x = x_ref[seq, pair].reshape(2 * tokens, -1)
            pre_ref[pair, 0] = dot_nn(x, rec_s[...]).reshape(2, tokens, -1)

    forward_kernel(
        place_ref,
        floor_ref,
        pre_even,
        pre_odd,
        flag_ref,
        bias_ref,
        theta_ref,
        gain_ref,
        state_ref,
        gated_even,
        gated_odd,
        square_ref,
        *scratch,
    )
    for gated_ref, mixes in ((gated_odd, mix_odd), (gated_even, mix_even)):
        for index in range(0, half, 2):
            gated = gated_ref[index : index + 2, 0].reshape(2 * tokens, -1)
            mix = dot_nn(gated, out_s[...]).astype(BF)
            mixes[index][0] = mix[:tokens]
            mixes[index + 1][0] = mix[tokens:]


def mix_forward(place, floor, even, odd, packed, flags, bias, theta, gain):
    groups, seqs, tokens, _ = flags.shape
    chan = bias.shape[1]
    half = groups // 2
    width = even[0].shape[-1]
    rows = groups * tokens
    pre_spec = block_spec(half, tokens, 5 * chan)
    one = block_spec(groups, tokens, 1)
    pre_shape = jax.ShapeDtypeStruct((half, seqs, tokens, 5 * chan), F32)
    mix_spec = pl.BlockSpec((1, tokens, width), lambda b: (b, 0, 0))
    mix_shape = jax.ShapeDtypeStruct((seqs, tokens, width), BF)
    gated = pltpu.VMEM((half, 1, tokens, 2 * chan), BF)
    held = pltpu.VMEM((seqs, half, tokens, width), BF)
    sems = pltpu.SemaphoreType.DMA((seqs, half))
    return pl.pallas_call(
        mix_forward_kernel,
        grid=(seqs,),
        in_specs=[
            SCALAR,
            SCALAR,
            pl.BlockSpec(packed.shape, lambda b: (0, 0, 0), pipeline_mode=pl.Buffered(1)),
            one,
            row_spec(chan),
            row_spec(chan),
            row_spec(2 * chan),
        ]
        + [ANYWHERE] * (2 * PIECES),
        out_specs=[pre_spec, pre_spec, block_spec(groups, tokens, 2 * chan), one]
        + [mix_spec] * (2 * half),
        out_shape=[
            pre_shape,
            pre_shape,
            jax.ShapeDtypeStruct((groups, seqs, tokens, 2 * chan), F32),
            jax.ShapeDtypeStruct((groups, seqs, tokens, 1), F32),
        ]
        + [mix_shape] * (2 * half),
        scratch_shapes=[
            pltpu.VMEM((width, 5 * chan), BF),
            pltpu.VMEM((2 * chan, width), BF),
            gated,
            gated,
            held,
            held,
            sems,
            sems,
        ]
        + [pltpu.VMEM((rows, chan), F32)] * 5
        + [pltpu.VMEM((groups, chan), F32)] * 2,
        compiler_params=pltpu.CompilerParams(vmem_limit_bytes=60 * 2**20),
        cost_estimate=SMALL,
        name="mix_forward",
    )(place, floor, packed, flags, bias, theta, gain, *even, *odd)


def mix_backward_kernel(*refs):
    place_ref, floor_ref, packed_ref = refs[:3]
    pre_even, pre_odd, flag_ref, bias_ref, theta_ref, gain_ref, state_ref = refs[3:10]
    scale_ref, term_ref = refs[10:12]
    refs = refs[12:]
    even, odd = refs[:PIECES], refs[PIECES : 2 * PIECES]
    refs = refs[2 * PIECES :]
    out_even, out_odd, scaled_even, scaled_odd, sum_bias, sum_theta, sum_gain = refs[:7]
    back_even, back_odd = refs[7:11], refs[11:15]
    rec_s, out_s, up_even, up_odd, x_even, x_odd, sems_even, sems_odd = refs[15:23]
    scratch = refs[23:]
    half, _, tokens, _ = pre_even.shape
    seq = pl.program_id(0)
    groups = ((even, x_even, sems_even), (odd, x_odd, sems_odd))
    fetch(groups)
    unpack_mix(packed_ref, rec_s, out_s)
    arrive(groups)
    for x_ref, up_ref in ((x_even, up_even), (x_odd, up_odd)):

        @pl.loop(0, half, step=2)
        def _(index, x_ref=x_ref, up_ref=up_ref):
            pair = pl.ds(index, 2)
            branch = x_ref[seq, pair].reshape(2 * tokens, -1)
            up_ref[pair, 0] = dot_nt(branch, out_s[...]).reshape(2, tokens, -1)

    backward_kernel(
        place_ref,
        floor_ref,
        pre_even,
        pre_odd,
        flag_ref,
        bias_ref,
        theta_ref,
        gain_ref,
        state_ref,
        up_even,
        up_odd,
        scale_ref,
        term_ref,
        out_even,
        out_odd,
        scaled_even,
        scaled_odd,
        sum_bias,
        sum_theta,
        sum_gain,
        *scratch,
    )
    for out_ref, backs in ((out_odd, back_odd), (out_even, back_even)):
        for index in range(0, half, 2):
            grad = out_ref[index : index + 2, 0].reshape(2 * tokens, -1)
            back = dot_nt(grad, rec_s[...]).astype(BF)
            backs[index][0] = back[:tokens]
            backs[index + 1][0] = back[tokens:]


def mix_backward(
    place, floor, packed, pre_even, pre_odd, flags, bias, theta, gain, state, scale, term,
    even, odd,
):
    groups, seqs, tokens, _ = flags.shape
    chan = bias.shape[1]
    half = groups // 2
    width = even[0].shape[-1]
    rows = groups * tokens
    pre_spec = block_spec(half, tokens, 5 * chan)
    one = block_spec(groups, tokens, 1)
    pair_spec = block_spec(half, tokens, 2 * chan)
    back_spec = pl.BlockSpec((1, tokens, width), lambda b: (b, 0, 0))
    pre_shape = jax.ShapeDtypeStruct((half, seqs, tokens, 5 * chan), BF)
    pair_shape = jax.ShapeDtypeStruct((half, seqs, tokens, 2 * chan), BF)
    up = pltpu.VMEM((half, 1, tokens, 2 * chan), F32)
    held = pltpu.VMEM((seqs, half, tokens, width), BF)
    sems = pltpu.SemaphoreType.DMA((seqs, half))
    return pl.pallas_call(
        mix_backward_kernel,
        grid=(seqs,),
        in_specs=[
            SCALAR,
            SCALAR,
            pl.BlockSpec(packed.shape, lambda b: (0, 0, 0), pipeline_mode=pl.Buffered(1)),
            pre_spec,
            pre_spec,
            one,
            row_spec(chan),
            row_spec(chan),
            row_spec(2 * chan),
            block_spec(groups, tokens, 2 * chan),
            one,
            one,
        ]
        + [ANYWHERE] * (2 * PIECES),
        out_specs=[
            pre_spec,
            pre_spec,
            pair_spec,
            pair_spec,
            row_spec(chan),
            row_spec(chan),
            row_spec(2 * chan),
        ]
        + [back_spec] * (2 * half),
        out_shape=[
            pre_shape,
            pre_shape,
            pair_shape,
            pair_shape,
            jax.ShapeDtypeStruct((1, chan), F32),
            jax.ShapeDtypeStruct((1, chan), F32),
            jax.ShapeDtypeStruct((1, 2 * chan), F32),
        ]
        + [jax.ShapeDtypeStruct((seqs, tokens, width), BF)] * (2 * half),
        scratch_shapes=[
            pltpu.VMEM((width, 5 * chan), BF),
            pltpu.VMEM((2 * chan, width), BF),
            up,
            up,
            held,
            held,
            sems,
            sems,
        ]
        + [pltpu.VMEM((rows, chan), F32)] * 5
        + [pltpu.VMEM((groups, chan), F32)] * 3,
        compiler_params=pltpu.CompilerParams(vmem_limit_bytes=60 * 2**20),
        cost_estimate=SMALL,
        name="mix_backward",
    )(
        place, floor, packed, pre_even, pre_odd, flags, bias, theta, gain, state, scale,
        term, *even, *odd,
    )


def assemble_tiles_kernel(shares, *refs):
    sources, outs = refs[: len(shares)], refs[len(shares) :]
    groups = sources[0].shape[0]
    run = sum(shares)
    for group in range(groups):
        wides = [
            jnp.concatenate(
                [source[group, tile].astype(F32) for tile in range(source.shape[1])], axis=1
            )
            for source in sources
        ]
        firsts = [0] * len(shares)
        for out in outs:
            for block in range(out.shape[1] // (groups * run)):
                base = (block * groups + group) * run
                for index, share in enumerate(shares):
                    first = firsts[index]
                    out[:, base : base + share] = wides[index][:, first : first + share]
                    firsts[index] += share
                    base += share


def assemble_tiles(parts, shares, widths):
    rows = parts[0].shape[2]
    return pl.pallas_call(
        functools.partial(assemble_tiles_kernel, shares),
        out_shape=[jax.ShapeDtypeStruct((rows, width), F32) for width in widths],
        compiler_params=pltpu.CompilerParams(vmem_limit_bytes=48 * 2**20),
        cost_estimate=SMALL,
        name="assemble_columns",
    )(*parts)


def assemble_rows_kernel(*refs):
    out = refs[-1]
    base = 0
    for source in refs[:-1]:
        tiles, rows, _ = source.shape
        for tile in range(tiles):
            out[base : base + rows, tile * LANES : (tile + 1) * LANES] = source[tile].astype(F32)
        base += rows


def assemble_rows(parts):
    rows = sum(part.shape[1] for part in parts)
    width = parts[0].shape[0] * LANES
    return pl.pallas_call(
        assemble_rows_kernel,
        out_shape=jax.ShapeDtypeStruct((rows, width), F32),
        compiler_params=pltpu.CompilerParams(vmem_limit_bytes=48 * 2**20),
        cost_estimate=SMALL,
        name="assemble_rows",
    )(*parts)


def shard_gather(value):
    return lax.all_gather(value, "wshard", axis=0, tiled=True)


def shard_scatter(value):
    return lax.psum_scatter(value, "wshard", scatter_dimension=0, tiled=True)


def plain_body(
    tokens,
    starts,
    layer_index,
    gain_mix,
    w_in,
    w_forget,
    bias_forget,
    theta,
    w_gate_out,
    gain_out,
    w_out,
    gain_ffn,
    w_ffgate,
    w_ffup,
    w_down,
    out_grad,
):
    seqs, seq_dev, width = tokens.shape
    rows = seqs * seq_dev
    groups = lax.axis_size("seq")
    planes = lax.axis_size("wshard")
    half = groups // 2
    devices = groups * planes
    place = lax.axis_index("seq")
    floor = layer_index.astype(F32) / LAYERS
    mix_run = w_out.shape[0] // groups
    ffn_run = w_down.shape[0] // groups
    chan = mix_run * planes // 2
    hidden = ffn_run * planes

    def own_columns(array, run):
        count = array.shape[1] // (run * groups)
        column = lax.broadcasted_iota(jnp.int32, (array.shape[1], count * run), 0)
        index = lax.broadcasted_iota(jnp.int32, (array.shape[1], count * run), 1)
        block = index // run
        chosen = column == block * (run * groups) + place * run + (index - block * run)
        return dot(array, chosen.astype(BF), "rc,cj->rj").astype(BF)

    def own_parts(vector):
        count = vector.shape[0] // (mix_run * groups)
        split = vector.reshape(count, groups, mix_run)
        return lax.dynamic_slice_in_dim(split, place, 1, 1).reshape(1, count * mix_run)

    def own_rows(array):
        run = array.shape[0] // groups
        return lax.dynamic_slice_in_dim(array, place * run, run, 0)

    resid_in = tokens.reshape(rows, width).astype(F32)
    scale_in = lax.rsqrt(jnp.mean(resid_in * resid_in, axis=1, keepdims=True) + EPS)
    normed_own = (resid_in * scale_in * gain_mix).astype(BF)
    normed_even, normed_odd = plain_gather(normed_own)
    upstream_own = out_grad.reshape(rows, width)

    rec_w = shard_gather(
        jnp.concatenate(
            [
                own_columns(w_in, mix_run),
                own_columns(w_forget, mix_run),
                own_columns(w_gate_out, mix_run),
            ],
            axis=1,
        )
    )
    out_w = shard_gather(own_rows(w_out))
    ff_w = shard_gather(
        jnp.concatenate([own_columns(w_ffgate, ffn_run), own_columns(w_ffup, ffn_run)], axis=1)
    )
    down_w = shard_gather(own_rows(w_down))

    slots = lax.broadcasted_iota(jnp.int32, (groups, groups), 0)
    sources = lax.broadcasted_iota(jnp.int32, (groups, groups), 1)
    keys = jnp.where(slots < half, 2 * slots, 2 * (slots - half) + 1)
    chosen = ((place ^ keys) == sources).astype(F32)
    marks = starts.astype(F32).reshape(seqs, groups, seq_dev).transpose(1, 0, 2)
    flags = jnp.sum(chosen[:, :, None, None] * marks[None], axis=1)[..., None]
    bias_own = own_parts(bias_forget)
    theta_own = own_parts(theta)
    gain_own = own_parts(gain_out)
    place_one = place.reshape(1)

    def blocks(array):
        return array.reshape(half, seqs, seq_dev, -1)

    pre_even = blocks(dot(normed_even, rec_w, "td,dc->tc"))
    pre_odd = blocks(dot(normed_odd, rec_w, "td,dc->tc"))
    state, gated_even, gated_odd, square = recur_forward(
        place_one, floor, pre_even, pre_odd, flags, bias_own, theta_own, gain_own
    )
    gated_even = gated_even.reshape(half * rows, 2 * chan)
    gated_odd = gated_odd.reshape(half * rows, 2 * chan)

    def mix(gated):
        return dot(gated, out_w, "tc,cd->td").astype(BF)

    square_own = scatter_small(square.reshape(groups, rows))
    scale_own = lax.rsqrt(square_own / width + EPS)
    scale_out = scale_own.reshape(rows, 1)
    branch_mix = scale_out * plain_scatter(mix(gated_even), mix(gated_odd))
    resid = resid_in + branch_mix
    scale_ffn = lax.rsqrt(jnp.mean(resid * resid, axis=1, keepdims=True) + EPS)
    ffn_even, ffn_odd = plain_gather((resid * scale_ffn * gain_ffn).astype(BF))
    scale_all = gather_small(scale_own)
    up_even, up_odd = plain_gather(upstream_own)

    def ffn(normed, upstream):
        ff = dot(normed, ff_w, "td,df->tf")
        ffn_gate, ffn_up = ff[:, :hidden], ff[:, hidden:]
        sig_ffn = jax.nn.sigmoid(ffn_gate)
        silu_ffn = ffn_gate * sig_ffn
        ffn_hidden = (silu_ffn * ffn_up).astype(BF)
        grad_hidden = dot(upstream, down_w, "td,fd->tf")
        grad_gate = grad_hidden * ffn_up * sig_ffn * (1.0 + ffn_gate * (1.0 - sig_ffn))
        grad_up = grad_hidden * silu_ffn
        grad_ff = jnp.concatenate([grad_gate.astype(BF), grad_up.astype(BF)], axis=1)
        return ffn_hidden, grad_ff

    hidden_odd, grad_ff_odd = ffn(ffn_odd, up_odd)
    hidden_even, grad_ff_even = ffn(ffn_even, up_even)
    grad_normed_ffn = plain_scatter(
        dot(grad_ff_even, ff_w, "tf,df->td").astype(BF),
        dot(grad_ff_odd, ff_w, "tf,df->td").astype(BF),
    )
    branch_ffn = plain_scatter(
        dot(hidden_even, down_w, "tf,fd->td").astype(BF),
        dot(hidden_odd, down_w, "tf,fd->td").astype(BF),
    )
    result = (resid + branch_ffn).astype(BF)

    scaled_ffn = grad_normed_ffn * gain_ffn
    grad_resid = (
        upstream_own.astype(F32)
        + scale_ffn * scaled_ffn
        - resid * scale_ffn**3 * jnp.mean(scaled_ffn * resid, axis=1, keepdims=True)
    )
    grad_gain_ffn = jnp.sum(grad_normed_ffn * resid * scale_ffn, axis=0)
    grad_branch_own = grad_resid.astype(BF)
    overlap = jnp.sum(grad_branch_own.astype(F32) * branch_mix, axis=1)
    term_all = gather_small((scale_out[:, 0] ** 2 * overlap / width)[None])
    branch_even, branch_odd = plain_gather(grad_branch_own)
    grad_gated_even = blocks(dot(branch_even, out_w, "td,cd->tc"))
    grad_gated_odd = blocks(dot(branch_odd, out_w, "td,cd->tc"))

    shape_one = (groups, seqs, seq_dev, 1)
    grad_even, grad_odd, scaled_even, scaled_odd, sum_bias, sum_theta, sum_gain = recur_backward(
        place_one,
        floor,
        pre_even,
        pre_odd,
        flags,
        bias_own,
        theta_own,
        gain_own,
        state,
        grad_gated_even,
        grad_gated_odd,
        scale_all.reshape(shape_one),
        term_all.reshape(shape_one),
    )
    grad_even = grad_even.reshape(half * rows, 5 * chan)
    grad_odd = grad_odd.reshape(half * rows, 5 * chan)
    grad_normed_in = plain_scatter(
        dot(grad_even, rec_w, "tc,dc->td").astype(BF),
        dot(grad_odd, rec_w, "tc,dc->td").astype(BF),
    )
    scaled_in = grad_normed_in * gain_mix
    grad_tokens = (
        grad_resid
        + scale_in * scaled_in
        - resid_in * scale_in**3 * jnp.mean(scaled_in * resid_in, axis=1, keepdims=True)
    ).astype(BF)
    grad_gain_mix = jnp.sum(grad_normed_in * resid_in * scale_in, axis=0)

    def pair_dot(left, right, form):
        return dot(left[0], right[0], form) + dot(left[1], right[1], form)

    def to_owner(grad):
        run = grad.shape[0] // devices
        part = grad.astype(BF).reshape(groups, planes, run, -1).transpose(1, 0, 2, 3)
        part = shard_scatter(part.reshape(grad.shape)).reshape(groups, run, -1)
        return lax.all_to_all(part, "seq", split_axis=0, concat_axis=0, tiled=True)

    def columns(part, run):
        source, count, cols = part.shape
        split = part.reshape(source, count, cols // run, run)
        return split.transpose(1, 2, 0, 3).reshape(count, -1).astype(F32)

    scaled_even = scaled_even.reshape(half * rows, 2 * chan)
    scaled_odd = scaled_odd.reshape(half * rows, 2 * chan)
    ff_grad = to_owner(
        pair_dot((ffn_even, ffn_odd), (grad_ff_even, grad_ff_odd), "td,tf->df")
    )
    grad_w_ffgate = columns(ff_grad[..., :hidden], ffn_run)
    grad_w_ffup = columns(ff_grad[..., hidden:], ffn_run)
    rec_grad = to_owner(pair_dot((normed_even, normed_odd), (grad_even, grad_odd), "td,tc->dc"))
    grad_w_in = columns(rec_grad[..., : 2 * chan], mix_run)
    grad_w_forget = columns(rec_grad[..., 2 * chan : 3 * chan], mix_run)
    grad_w_gate = columns(rec_grad[..., 3 * chan :], mix_run)

    pairs = [
        (s * planes + w, w * groups + s) for s in range(groups) for w in range(planes)
    ]

    def rows_to_owner(grad):
        part = shard_scatter(grad.astype(BF))
        return lax.ppermute(part, ("seq", "wshard"), pairs).astype(F32)

    grad_w_down = rows_to_owner(
        pair_dot((hidden_even, hidden_odd), (up_even, up_odd), "tf,td->fd")
    )
    grad_w_out = rows_to_owner(
        pair_dot((scaled_even, scaled_odd), (branch_even, branch_odd), "tc,td->cd")
    )

    def spread(part):
        count = part.shape[1] // mix_run
        zero = jnp.zeros((count, groups, mix_run), F32)
        zero = lax.dynamic_update_slice(zero, part.reshape(count, 1, mix_run), (0, place, 0))
        return zero.reshape(-1)

    pieces = [
        spread(sum_bias),
        spread(sum_theta),
        spread(sum_gain),
        grad_gain_ffn,
        grad_gain_mix,
        jnp.stack(
            [
                jnp.sum(resid_in * resid_in),
                jnp.sum(branch_mix * branch_mix),
                jnp.sum(branch_ffn * branch_ffn),
            ]
        ),
    ]
    sums = sum_all(jnp.concatenate(pieces))
    cuts = []
    offset = 0
    for piece in pieces:
        cuts.append(sums[offset : offset + piece.shape[0]])
        offset += piece.shape[0]
    grad_bias, grad_theta, grad_gain_out, grad_gain_ffn, grad_gain_mix, squares = cuts
    rms_values = jnp.sqrt(squares / (rows * width * devices))
    return (
        result.reshape(seqs, seq_dev, width),
        grad_tokens.reshape(seqs, seq_dev, width),
        grad_gain_mix,
        grad_w_in,
        grad_w_forget,
        grad_bias,
        grad_theta,
        grad_w_gate,
        grad_gain_out,
        grad_w_out,
        grad_gain_ffn,
        grad_w_ffgate,
        grad_w_ffup,
        grad_w_down,
        rms_values,
    )


def body(
    tokens,
    starts,
    layer_index,
    gain_mix,
    w_in,
    w_forget,
    bias_forget,
    theta,
    w_gate_out,
    gain_out,
    w_out,
    gain_ffn,
    w_ffgate,
    w_ffup,
    w_down,
    out_grad,
):
    seqs, seq_dev, width = tokens.shape
    rows = seqs * seq_dev
    groups = lax.axis_size("seq")
    planes = lax.axis_size("wshard")
    half = groups // 2
    devices = groups * planes
    mix_run = w_out.shape[0] // groups
    ffn_run = w_down.shape[0] // groups
    chan = mix_run * planes // 2
    shares = (ffn_run * 6 // 11, ffn_run - ffn_run * 6 // 11)
    if not (
        groups == 8
        and seqs == 2
        and chan % LANES == 0
        and all(2 * planes * share % LANES == 0 and share % 16 == 0 for share in shares)
    ):
        return plain_body(
            tokens,
            starts,
            layer_index,
            gain_mix,
            w_in,
            w_forget,
            bias_forget,
            theta,
            w_gate_out,
            gain_out,
            w_out,
            gain_ffn,
            w_ffgate,
            w_ffup,
            w_down,
            out_grad,
        )
    place = lax.axis_index("seq")
    floor = layer_index.astype(F32) / LAYERS
    place_one = place.reshape(1)

    first_bit, second_bit = chip_bits()

    def own_columns(array, run, first, count):
        blocks = array.shape[1] // (run * groups)
        column = lax.broadcasted_iota(jnp.int32, (array.shape[1], blocks * count), 0)
        index = lax.broadcasted_iota(jnp.int32, (array.shape[1], blocks * count), 1)
        block = index // count
        wanted = block * (run * groups) + place * run + first + (index - block * count)
        return dot(array, (column == wanted).astype(BF), "rc,cj->rj").astype(BF)

    def own_parts(vector):
        count = vector.shape[0] // (mix_run * groups)
        split = vector.reshape(count, groups, mix_run)
        return lax.dynamic_slice_in_dim(split, place, 1, 1).reshape(1, count * mix_run)

    def own_rows(array, first, count):
        run = array.shape[0] // groups
        return lax.dynamic_slice_in_dim(array, place * run + first, count, 0)

    rec_own = jnp.concatenate(
        [own_columns(array, mix_run, 0, mix_run) for array in (w_in, w_forget, w_gate_out)], axis=1
    )
    packs = [pack([rec_own[None], own_rows(w_out, 0, mix_run)[None]])]
    first = 0
    for share in shares:
        ff_own = jnp.concatenate(
            [own_columns(array, ffn_run, first, share) for array in (w_ffgate, w_ffup)], axis=1
        )
        packs.append(pack([ff_own[None], own_rows(w_down, first, share)[None]]))
        first += share
    rec_packed = gather_packed(packs[0])
    packed = [gather_packed(item) for item in packs[1:]]

    resid_in = after(tokens, packs[0]).reshape(rows, width).astype(F32)
    scale_in = lax.rsqrt(jnp.mean(resid_in * resid_in, axis=1, keepdims=True) + EPS)
    normed_own = (resid_in * scale_in * gain_mix).astype(BF)
    normed_stage = gather_first(normed_own)
    normed_far = gather_far(normed_own, normed_stage)
    normed_even = (normed_own, *normed_stage, *normed_far)
    normed_odd = cross(normed_even)
    upstream_own = out_grad.reshape(rows, width)
    up_gate = after(upstream_own, normed_far)
    up_stage = gather_first(up_gate)
    up_far = gather_far(up_gate, up_stage)
    rec_packed, up_stage, _ = tied(rec_packed, up_stage, packs[1:])

    slots = lax.broadcasted_iota(jnp.int32, (groups, groups), 0)
    sources = lax.broadcasted_iota(jnp.int32, (groups, groups), 1)
    keys = jnp.where(slots < half, 2 * slots, 2 * (slots - half) + 1)
    chosen = ((place ^ keys) == sources).astype(F32)
    marks = starts.astype(F32).reshape(seqs, groups, seq_dev).transpose(1, 0, 2)
    flags = jnp.sum(chosen[:, :, None, None] * marks[None], axis=1)[..., None]
    bias_own = own_parts(bias_forget)
    theta_own = own_parts(theta)
    gain_own = own_parts(gain_out)

    pre_even, pre_odd, state, square, *mixes = mix_forward(
        place_one,
        floor,
        normed_even,
        normed_odd,
        rec_packed,
        flags,
        bias_own,
        theta_own,
        gain_own,
    )
    mixes = tuple(item.reshape(rows, width) for item in mixes)
    mix_even, mix_odd = mixes[:half], mixes[half:]
    mix_odd, up_far = tied(mix_odd, up_far)
    up_even = (up_gate, *up_stage, *up_far)
    square = shrink(square.reshape(groups, rows), 1)
    mix_crossed = cross(mix_odd)
    mix_sums = joints(mix_even, mix_crossed)
    square_next = shrink(square, second_bit)
    mix_stage, square_next = tied(scatter_first(mix_sums), square_next)
    up_odd = cross(up_even)
    square_own = shrink(square_next, first_bit)
    scale_own = lax.rsqrt(square_own / width + EPS)
    scale_out = scale_own.reshape(rows, 1)
    branch_mix = scale_out * scatter_last(mix_even, mix_crossed, mix_sums, mix_stage)
    resid = resid_in + branch_mix
    scale_ffn = lax.rsqrt(jnp.mean(resid * resid, axis=1, keepdims=True) + EPS)
    ffn_own = (resid * scale_ffn * gain_ffn).astype(BF)
    ffn_stage = gather_first(ffn_own)
    ffn_far = gather_far(ffn_own, ffn_stage)
    ffn_even = (ffn_own, *ffn_stage, *ffn_far)
    ffn_odd = cross(ffn_even)
    scale_all = gather_small(scale_own)

    ff_even, ff_odd, ff_grads = [], [], []

    def share_grads(index):
        (hidden_e, grad_e), (hidden_o, grad_o) = ff_even[index], ff_odd[index]
        return grads_call(
            groups,
            planes,
            (ffn_even, ffn_odd),
            (grad_e, grad_o),
            (hidden_e, hidden_o),
            (up_even, up_odd),
        )

    cols = [2 * planes * share for share in shares]
    hidden, grad, back_odd = ffn_call(
        ffn_odd, up_odd, packed[0], cols[0], None, False
    )
    ff_odd.append((hidden, grad))
    hidden, grad, back_even = ffn_call(
        ffn_even, up_even, packed[0], cols[0], None, False
    )
    ff_even.append((hidden, grad))
    ff_grads.append(share_grads(0))
    packed[1], ff_grads[0], back_even, scale_all = tied(
        packed[1], ff_grads[0], back_even, scale_all
    )
    hidden, grad, *back_odd = ffn_call(
        ffn_odd, up_odd, packed[1], cols[1], back_odd, True
    )
    ff_odd.append((hidden, grad))
    hidden, grad, *back_even = ffn_call(
        ffn_even, up_even, packed[1], cols[1], back_even, True
    )
    ff_even.append((hidden, grad))
    back_crossed = cross(back_odd)
    back_sums = joints(back_even, back_crossed)
    back_stage = scatter_first(back_sums)
    ff_even[1] = (ff_even[1][0], after(ff_even[1][1], back_sums))
    ff_grads.append(share_grads(1))
    back_stage, ff_grads[1] = tied(back_stage, ff_grads[1])
    grad_normed_ffn = scatter_last(back_even, back_crossed, back_sums, back_stage)

    scaled_ffn = grad_normed_ffn * gain_ffn
    grad_resid = (
        upstream_own.astype(F32)
        + scale_ffn * scaled_ffn
        - resid * scale_ffn**3 * jnp.mean(scaled_ffn * resid, axis=1, keepdims=True)
    )
    grad_gain_ffn = jnp.sum(grad_normed_ffn * resid * scale_ffn, axis=0)
    grad_branch_own = grad_resid.astype(BF)
    overlap = jnp.sum(grad_branch_own.astype(F32) * branch_mix, axis=1)
    term_own = (scale_out[:, 0] ** 2 * overlap / width)[None]
    branch_stage = gather_first(grad_branch_own)
    term_near = grow(grow(term_own, 1), first_bit)
    result_even, result_odd = (
        result_call(
                [after(share[0][0], grad_branch_own), share[1][0]],
            packed,
            width,
        )
        for share in (ff_even, ff_odd)
    )
    branch_stage, result_even, result_odd, term_near = tied(
        branch_stage, tuple(result_even), tuple(result_odd), term_near
    )
    branch_far = gather_far(grad_branch_own, branch_stage)
    result_crossed = cross(result_odd)
    result_sums = joints(result_even, result_crossed)
    term_all = grow(term_near, second_bit)
    branch_far, result_sums, term_all = tied(branch_far, result_sums, term_all)
    term_all = slot_rows(term_all)
    branch_even = (grad_branch_own, *branch_stage, *branch_far)
    branch_odd = cross(branch_even)
    result_stage = scatter_first(result_sums)

    pairs = [(s * planes + w, w * groups + s) for s in range(groups) for w in range(planes)]

    def owned(grads, count):
        part = scatter_packed(grads)
        lines = count * width // (planes * LANES)
        tiles = part[:lines].reshape(groups, -1, LANES)
        tiles = lax.all_to_all(tiles, "seq", split_axis=0, concat_axis=0, tiled=True)
        tiles = tiles.reshape(groups, count // LANES, -1, LANES)
        moved = lax.ppermute(part[lines:], ("seq", "wshard"), pairs)
        return tiles, moved.reshape(width // LANES, -1, LANES)

    first_tiles, first_lines = owned(ff_grads[0], cols[0])

    shape_one = (groups, seqs, seq_dev, 1)
    (
        grad_even,
        grad_odd,
        scaled_even,
        scaled_odd,
        sum_bias,
        sum_theta,
        sum_gain,
        *backs,
    ) = mix_backward(
        place_one,
        floor,
        rec_packed,
        pre_even,
        pre_odd,
        flags,
        bias_own,
        theta_own,
        gain_own,
        state,
        scale_all.reshape(shape_one),
        term_all.reshape(shape_one),
        branch_even,
        branch_odd,
    )
    grad_even = grad_even.reshape(half * rows, 5 * chan)
    grad_odd = grad_odd.reshape(half * rows, 5 * chan)
    scaled_even = scaled_even.reshape(half * rows, 2 * chan)
    scaled_odd = scaled_odd.reshape(half * rows, 2 * chan)
    backs = tuple(item.reshape(rows, width) for item in backs)
    grad_even, result_stage, first_tiles = tied(grad_even, result_stage, first_tiles)
    rec_grads = grads_call(
        groups,
        planes,
        (normed_even, normed_odd),
        (grad_even, grad_odd),
        (scaled_even, scaled_odd),
        (branch_even, branch_odd),
    )
    back_even, back_odd = backs[:half], backs[half:]
    back_crossed = cross(back_odd)
    back_crossed, rec_grads = tied(back_crossed, rec_grads)
    branch_ffn = scatter_last(result_even, result_crossed, result_sums, result_stage)
    result = (resid + branch_ffn).astype(BF)
    back_sums = joints(back_even, back_crossed)
    back_stage = tied(*scatter_first(back_sums))
    grad_normed_in = scatter_last(back_even, back_crossed, back_sums, back_stage)
    scaled_in = grad_normed_in * gain_mix
    grad_tokens = (
        grad_resid
        + scale_in * scaled_in
        - resid_in * scale_in**3 * jnp.mean(scaled_in * resid_in, axis=1, keepdims=True)
    ).astype(BF)
    grad_gain_mix = jnp.sum(grad_normed_in * resid_in * scale_in, axis=0)

    hidden_all = w_ffgate.shape[1]
    rec_widths = (w_in.shape[1], w_forget.shape[1], w_gate_out.shape[1])
    second_tiles, second_lines = owned(ff_grads[1], cols[1])
    grad_w_ffgate, grad_w_ffup = assemble_tiles(
        [first_tiles, second_tiles], shares, (hidden_all, hidden_all)
    )
    grad_w_down = assemble_rows([first_lines, second_lines])
    rec_tiles, rec_lines = owned(rec_grads, 5 * chan)
    grad_w_in, grad_w_forget, grad_w_gate = assemble_tiles([rec_tiles], (mix_run,), rec_widths)
    grad_w_out = assemble_rows([rec_lines])

    def spread(part):
        count = part.shape[1] // mix_run
        zero = jnp.zeros((count, groups, mix_run), F32)
        zero = lax.dynamic_update_slice(zero, part.reshape(count, 1, mix_run), (0, place, 0))
        return zero.reshape(-1)

    pieces = [
        spread(sum_bias),
        spread(sum_theta),
        spread(sum_gain),
        grad_gain_ffn,
        grad_gain_mix,
        jnp.stack(
            [
                jnp.sum(resid_in * resid_in),
                jnp.sum(branch_mix * branch_mix),
                jnp.sum(branch_ffn * branch_ffn),
            ]
        ),
    ]
    sums = sum_all(jnp.concatenate(pieces))
    cuts = []
    offset = 0
    for piece in pieces:
        cuts.append(sums[offset : offset + piece.shape[0]])
        offset += piece.shape[0]
    grad_bias, grad_theta, grad_gain_out, grad_gain_ffn, grad_gain_mix, squares = cuts
    rms_values = jnp.sqrt(squares / (rows * width * devices))
    return (
        result.reshape(seqs, seq_dev, width),
        grad_tokens.reshape(seqs, seq_dev, width),
        grad_gain_mix,
        grad_w_in,
        grad_w_forget,
        grad_bias,
        grad_theta,
        grad_w_gate,
        grad_gain_out,
        grad_w_out,
        grad_gain_ffn,
        grad_w_ffgate,
        grad_w_ffup,
        grad_w_down,
        rms_values,
    )


def solution(mesh):
    whole = P()
    rowed = P("wshard", None)
    stream = P("wshard", "seq", None)
    owned = P(("seq", "wshard"), None)
    return jax.shard_map(
        body,
        mesh=mesh,
        in_specs=(
            stream,
            rowed,
            whole,
            whole,
            rowed,
            rowed,
            whole,
            whole,
            rowed,
            whole,
            rowed,
            whole,
            rowed,
            rowed,
            rowed,
            stream,
        ),
        out_specs=(
            stream,
            stream,
            whole,
            owned,
            owned,
            whole,
            whole,
            owned,
            whole,
            owned,
            whole,
            owned,
            owned,
            owned,
            whole,
        ),
        check_vma=False,
    )
```

```python
import functools

import jax
import jax.numpy as jnp
from jax import lax
from jax.experimental import pallas as pl
from jax.experimental.pallas import tpu as pltpu
from jax.sharding import PartitionSpec as P

LAYERS = 24
EPS = 1e-06
BF = jnp.bfloat16
F32 = jnp.float32


def dot(left, right, form):
    return jnp.einsum(form, left, right, preferred_element_type=F32)


def swap(value, bit):
    size = lax.axis_size("seq")
    return lax.ppermute(value, "seq", [(i, i ^ bit) for i in range(size)])


def chip_bits():
    size = lax.axis_size("seq")
    return [1 << i for i in range(1, size.bit_length() - 1)]


def plain_even(own):
    bits = chip_bits()
    if len(bits) == 2:
        first, second = bits
        half = own.shape[0] // 2
        from_first = swap(own, first)
        from_second = swap(own, second)
        top = swap(from_first[:half], second)
        low = swap(from_second[half:], first)
        return jnp.concatenate([own, from_first, from_second, top, low], axis=0)
    held = own
    for bit in bits:
        held = jnp.concatenate([held, swap(held, bit)], axis=0)
    return held


def plain_gather(own):
    even = plain_even(own)
    return even, swap(even, 1)


def plain_scatter(even, odd):
    bits = chip_bits()
    joint = even.astype(F32) + swap(odd, 1).astype(F32)
    if len(bits) == 2:
        first, second = bits
        rows = joint.shape[0] // 4
        half = rows // 2
        low_joint = joint.astype(BF)
        near_first, near_second, far = (
            low_joint[rows : 2 * rows],
            low_joint[2 * rows : 3 * rows],
            low_joint[3 * rows :],
        )
        far_top = swap(far[:half], first)
        far_low = swap(far[half:], second)
        first_top = swap(near_first[:half], first)
        second_low = swap(near_second[half:], second)
        first_low = swap((near_first[half:].astype(F32) + far_low.astype(F32)).astype(BF), first)
        second_top = swap(
            (near_second[:half].astype(F32) + far_top.astype(F32)).astype(BF), second
        )
        first_all = jnp.concatenate([first_top, first_low], axis=0).astype(F32)
        second_all = jnp.concatenate([second_top, second_low], axis=0).astype(F32)
        return joint[:rows] + first_all + second_all
    for bit in reversed(bits):
        half = joint.shape[0] // 2
        joint = joint[:half] + swap(joint[half:].astype(BF), bit).astype(F32)
    return joint


def gather_first(own):
    return tuple(swap(own, bit) for bit in chip_bits())


def gather_far(own, stage):
    first, second = chip_bits()
    half = own.shape[0] // 2
    return swap(stage[0][:half], second), swap(stage[1][half:], first)


def cross(pieces):
    return tuple(swap(piece, 1) for piece in pieces)


def scatter_far(even, crossed):
    half = even.shape[0] // 2
    bits = chip_bits()
    return tuple(
        swap((even[rows].astype(F32) + crossed[rows].astype(F32)).astype(BF), bit)
        for rows, bit in zip((slice(0, half), slice(half, None)), bits)
    )


def onward_kernel(first_even, first_cross, far_low, second_even, second_cross, far_top, *outs):
    half = far_low.shape[0]
    first_out, second_out = outs
    both = first_even[...].astype(F32) + first_cross[...].astype(F32)
    first_out[:half, :] = both[:half].astype(BF)
    first_out[half:, :] = (both[half:] + far_low[...].astype(F32)).astype(BF)
    both = second_even[...].astype(F32) + second_cross[...].astype(F32)
    second_out[:half, :] = (both[:half] + far_top[...].astype(F32)).astype(BF)
    second_out[half:, :] = both[half:].astype(BF)


def near_sums(even, crossed, far):
    rows, width = even[0].shape
    step = width // 4
    whole = pl.BlockSpec((rows, step), lambda i: (0, i))
    part = pl.BlockSpec((rows // 2, step), lambda i: (0, i))
    return pl.pallas_call(
        onward_kernel,
        grid=(width // step,),
        in_specs=[whole, whole, part] * 2,
        out_specs=[whole] * 2,
        out_shape=[jax.ShapeDtypeStruct((rows, width), BF)] * 2,
        cost_estimate=SMALL,
        name="onward_sums",
    )(even[0], crossed[0], far[1], even[1], crossed[1], far[0])


def to_neighbours(sums):
    return tuple(swap(item, bit) for item, bit in zip(sums, chip_bits()))


def scatter_near(even, crossed, far):
    return to_neighbours(near_sums(even, crossed, far))


def joint_kernel(*refs):
    count = len(refs) // 3
    for index in range(count):
        both = refs[index][...].astype(F32) + refs[count + index][...].astype(F32)
        refs[2 * count + index][...] = both.astype(BF)


FIRST_SUMS = ((3, 0), (3, 1), (1, 0), (2, 1))


def joints(even, crossed):
    rows, width = even[0].shape
    half = rows // 2
    step = width // 4

    def spec(part):
        return pl.BlockSpec((half, step), lambda i, part=part: (part, i))

    return pl.pallas_call(
        joint_kernel,
        grid=(width // step,),
        in_specs=[spec(part) for _, part in FIRST_SUMS] * 2,
        out_specs=[spec(0)] * len(FIRST_SUMS),
        out_shape=[jax.ShapeDtypeStruct((half, width), BF)] * len(FIRST_SUMS),
        cost_estimate=SMALL,
        name="chip_sums",
    )(*[even[index] for index, _ in FIRST_SUMS], *[crossed[index] for index, _ in FIRST_SUMS])


def scatter_first(sums):
    first, second = chip_bits()
    return tuple(swap(item, bit) for item, bit in zip(sums, (first, second, first, second)))


def scatter_last(even, crossed, stage):
    first, second = chip_bits()
    half = even[0].shape[0] // 2
    far_top, far_low, first_top, second_low = stage

    def onward(index, rows, far):
        both = even[index][rows].astype(F32) + crossed[index][rows].astype(F32)
        return (both + far.astype(F32)).astype(BF)

    first_low = swap(onward(1, slice(half, None), far_low), first)
    second_top = swap(onward(2, slice(0, half), far_top), second)
    first_all = jnp.concatenate([first_top, first_low], axis=0).astype(F32)
    second_all = jnp.concatenate([second_top, second_low], axis=0).astype(F32)
    return even[0].astype(F32) + crossed[0].astype(F32) + first_all + second_all


def scatter_sum(even, crossed, near):
    return (even.astype(F32) + crossed.astype(F32)) + (near[0].astype(F32) + near[1].astype(F32))


def tied(*values):
    return lax.optimization_barrier(values)


def grow(held, bit):
    return jnp.concatenate([held, swap(held, bit)], axis=0)


def shrink(blocks, bit):
    half = blocks.shape[0] // 2
    return blocks[:half] + swap(blocks[half:], bit)


def slot_rows(held):
    pairs = held.reshape(held.shape[0] // 2, 2, -1)
    return pairs.transpose(1, 0, 2).reshape(held.shape)


def gather_small(own):
    for bit in [1] + chip_bits():
        own = grow(own, bit)
    return slot_rows(own)


def scatter_small(blocks):
    for bit in [1] + list(reversed(chip_bits())):
        blocks = shrink(blocks, bit)
    return blocks


def sum_seq(value):
    for bit in [1] + chip_bits():
        value = value + swap(value, bit)
    return value


def others(value):
    planes = lax.axis_size("wshard")
    return [
        lax.ppermute(value, "wshard", [(i, i ^ key) for i in range(planes)])
        for key in range(1, planes)
    ]


def sum_tree(values):
    while len(values) > 1:
        values = [values[i] + values[i + 1] for i in range(0, len(values), 2)]
    return values[0]


LANES = 128
SMALL = pl.CostEstimate(flops=1024, transcendentals=0, bytes_accessed=1024)


def filler(flops):
    return pl.CostEstimate(flops=flops, transcendentals=0, bytes_accessed=1024)


def pack(arrays):
    lines = []
    for array in arrays:
        count, rows, cols = array.shape
        split = array.reshape(count, rows, cols // LANES, LANES).transpose(0, 2, 1, 3)
        lines.append(split.reshape(count, rows * cols // LANES, LANES))
    return jnp.concatenate(lines, axis=1)


def gather_packed(packed):
    return lax.all_gather(packed, "wshard", axis=0, tiled=True)


def scatter_packed(packed):
    return lax.psum_scatter(
        packed.reshape(-1, LANES), "wshard", scatter_dimension=0, tiled=True
    )


def after(value, *others):
    return lax.optimization_barrier((value, others))[0]


def slot_of(place, group, groups):
    key = place ^ group
    return (key >> 1) + (key & 1) * (groups // 2)


def group_of(place, half, index):
    return place ^ ((index << 1) | half)


def token_rows(slot, tokens):
    return pl.ds(pl.multiple_of(slot * tokens, tokens), tokens)


def keep_of(pre, flag, bias, floor, chan):
    logit = (pre[:, 2 * chan : 3 * chan] + bias).astype(BF).astype(F32)
    sig = jax.nn.sigmoid(logit)
    return (floor + (1.0 - floor) * sig) * (1.0 - flag), sig


def forward_kernel(
    place_ref,
    floor_ref,
    pre_even,
    pre_odd,
    flag_ref,
    bias_ref,
    theta_ref,
    gain_ref,
    state_ref,
    gated_even,
    gated_odd,
    square_ref,
    keep_s,
    val_re,
    val_im,
    prod_re,
    prod_im,
    carry_re,
    carry_im,
):
    groups, _, tokens, _ = flag_ref.shape
    chan = keep_s.shape[1]
    half_groups = groups // 2
    floor = floor_ref[0]
    place = place_ref[0]
    cosine = jnp.cos(theta_ref[...])
    sine = jnp.sin(theta_ref[...])

    for half, pre_ref in ((0, pre_even), (1, pre_odd)):

        @pl.loop(0, half_groups)
        def _(index, half=half, pre_ref=pre_ref):
            slot = index + half * half_groups
            rows = token_rows(slot, tokens)
            pre = pre_ref[index, 0]
            keep, _ = keep_of(pre, flag_ref[slot, 0], bias_ref[...], floor, chan)
            keep_s[rows, :] = keep
            fresh = 1.0 - keep
            value = pre[:, :chan]
            val_re[rows, :] = fresh * (value * jax.nn.sigmoid(value)).astype(BF).astype(F32)
            value = pre[:, chan : 2 * chan]
            val_im[rows, :] = fresh * (value * jax.nn.sigmoid(value)).astype(BF).astype(F32)

    def step(t, carry):
        h_re, h_im, p_re, p_im = carry
        rows = pl.ds(t, groups, stride=tokens)
        held = keep_s[rows, :]
        a_re = held * cosine
        a_im = held * sine
        n_re = a_re * h_re - a_im * h_im + val_re[rows, :]
        n_im = a_re * h_im + a_im * h_re + val_im[rows, :]
        q_re = a_re * p_re - a_im * p_im
        q_im = a_re * p_im + a_im * p_re
        val_re[rows, :] = n_re
        val_im[rows, :] = n_im
        prod_re[rows, :] = q_re
        prod_im[rows, :] = q_im
        return n_re, n_im, q_re, q_im

    zero = jnp.zeros((groups, chan), F32)
    lax.fori_loop(0, tokens, step, (zero, zero, zero + 1.0, zero), unroll=8)

    def link(group, carry):
        c_re, c_im = carry
        slot = slot_of(place, group, groups)
        carry_re[pl.ds(slot, 1), :] = c_re
        carry_im[pl.ds(slot, 1), :] = c_im
        last = pl.ds(slot * tokens + tokens - 1, 1)
        p_re = prod_re[last, :]
        p_im = prod_im[last, :]
        return (
            p_re * c_re - p_im * c_im + val_re[last, :],
            p_re * c_im + p_im * c_re + val_im[last, :],
        )

    nought = jnp.zeros((1, chan), F32)
    lax.fori_loop(0, groups, link, (nought, nought))

    for half, pre_ref, gated_ref in ((0, pre_even, gated_even), (1, pre_odd, gated_odd)):

        @pl.loop(0, half_groups)
        def _(index, half=half, pre_ref=pre_ref, gated_ref=gated_ref):
            slot = index + half * half_groups
            rows = token_rows(slot, tokens)
            c_re = carry_re[pl.ds(slot, 1), :]
            c_im = carry_im[pl.ds(slot, 1), :]
            p_re = prod_re[rows, :]
            p_im = prod_im[rows, :]
            h_re = val_re[rows, :] + p_re * c_re - p_im * c_im
            h_im = val_im[rows, :] + p_re * c_im + p_im * c_re
            state_ref[slot, 0, :, :chan] = h_re
            state_ref[slot, 0, :, chan:] = h_im
            m_re = h_re.astype(BF).astype(F32)
            m_im = h_im.astype(BF).astype(F32)
            gate = jax.nn.sigmoid(pre_ref[index, 0, :, 3 * chan :]) * gain_ref[...]
            gated_ref[index, 0, :, :chan] = (m_re * gate[:, :chan]).astype(BF)
            gated_ref[index, 0, :, chan:] = (m_im * gate[:, chan:]).astype(BF)
            square_ref[slot, 0] = jnp.sum(m_re * m_re + m_im * m_im, axis=1, keepdims=True)


def backward_kernel(
    place_ref,
    floor_ref,
    pre_even,
    pre_odd,
    flag_ref,
    bias_ref,
    theta_ref,
    gain_ref,
    state_ref,
    up_even,
    up_odd,
    scale_ref,
    term_ref,
    out_even,
    out_odd,
    scaled_even,
    scaled_odd,
    sum_bias,
    sum_theta,
    sum_gain,
    keep_s,
    adj_re,
    adj_im,
    prod_re,
    prod_im,
    carry_re,
    carry_im,
    next_s,
):
    groups, _, tokens, _ = flag_ref.shape
    chan = keep_s.shape[1]
    half_groups = groups // 2
    floor = floor_ref[0]
    place = place_ref[0]
    cosine = jnp.cos(theta_ref[...])
    sine = jnp.sin(theta_ref[...])

    @pl.when(pl.program_id(0) == 0)
    def _():
        sum_bias[...] = jnp.zeros_like(sum_bias)
        sum_theta[...] = jnp.zeros_like(sum_theta)
        sum_gain[...] = jnp.zeros_like(sum_gain)

    for half, pre_ref, up_ref, out_ref, scaled_ref in (
        (0, pre_even, up_even, out_even, scaled_even),
        (1, pre_odd, up_odd, out_odd, scaled_odd),
    ):

        @pl.loop(0, half_groups)
        def _(
            index, half=half, pre_ref=pre_ref, up_ref=up_ref, out_ref=out_ref, scaled_ref=scaled_ref
        ):
            slot = index + half * half_groups
            rows = token_rows(slot, tokens)
            pre = pre_ref[index, 0]
            keep, _ = keep_of(pre, flag_ref[slot, 0], bias_ref[...], floor, chan)
            keep_s[rows, :] = keep
            scale = scale_ref[slot, 0]
            mixed = state_ref[slot, 0].astype(BF).astype(F32)
            sig = jax.nn.sigmoid(pre[:, 3 * chan :])
            inner = up_ref[index, 0] * sig
            scaled_ref[index, 0] = (mixed * gain_ref[...] * sig * scale).astype(BF)
            normed = inner * mixed * scale
            sum_gain[...] += jnp.sum(normed, axis=0, keepdims=True)
            out_ref[index, 0, :, 3 * chan :] = (normed * gain_ref[...] * (1.0 - sig)).astype(BF)
            grad = (scale * (inner * gain_ref[...]) - mixed * term_ref[slot, 0]).astype(BF)
            adj_re[rows, :] = grad[:, :chan].astype(F32)
            adj_im[rows, :] = grad[:, chan:].astype(F32)

    @pl.loop(0, groups)
    def _(group):
        slot = slot_of(place, group, groups)
        after = slot_of(place, lax.min(group + 1, groups - 1), groups)
        row = keep_s[pl.ds(after * tokens, 1), :]
        next_s[pl.ds(slot, 1), :] = jnp.where(group == groups - 1, 0.0, row)

    def turn(t, held, carry):
        g_re, g_im, p_re, p_im = carry
        rows = pl.ds(t, groups, stride=tokens)
        a_re = held * cosine
        a_im = held * sine
        n_re = a_re * g_re + a_im * g_im + adj_re[rows, :]
        n_im = a_re * g_im - a_im * g_re + adj_im[rows, :]
        q_re = a_re * p_re + a_im * p_im
        q_im = a_re * p_im - a_im * p_re
        adj_re[rows, :] = n_re
        adj_im[rows, :] = n_im
        prod_re[rows, :] = q_re
        prod_im[rows, :] = q_im
        return n_re, n_im, q_re, q_im

    def step(index, carry):
        t = tokens - 2 - index
        return turn(t, keep_s[pl.ds(t + 1, groups, stride=tokens), :], carry)

    zero = jnp.zeros((groups, chan), F32)
    carry = turn(tokens - 1, next_s[...], (zero, zero, zero + 1.0, zero))
    lax.fori_loop(0, tokens - 1, step, carry, unroll=4)

    def link(index, carry):
        c_re, c_im = carry
        slot = slot_of(place, groups - 1 - index, groups)
        carry_re[pl.ds(slot, 1), :] = c_re
        carry_im[pl.ds(slot, 1), :] = c_im
        first = pl.ds(slot * tokens, 1)
        p_re = prod_re[first, :]
        p_im = prod_im[first, :]
        return (
            p_re * c_re - p_im * c_im + adj_re[first, :],
            p_re * c_im + p_im * c_re + adj_im[first, :],
        )

    nought = jnp.zeros((1, chan), F32)
    lax.fori_loop(0, groups, link, (nought, nought))
    head = lax.broadcasted_iota(jnp.int32, (tokens, 2 * chan), 0) == 0

    for half, pre_ref, out_ref in ((0, pre_even, out_even), (1, pre_odd, out_odd)):

        @pl.loop(0, half_groups)
        def _(index, half=half, pre_ref=pre_ref, out_ref=out_ref):
            slot = index + half * half_groups
            rows = token_rows(slot, tokens)
            group = group_of(place, half, index)
            before = slot_of(place, lax.max(group - 1, 0), groups)
            tail = jnp.where(group == 0, 0.0, state_ref[before, 0, tokens - 1 :, :])
            prev = jnp.where(head, tail, pltpu.roll(state_ref[slot, 0], 1, 0))
            prev_re = prev[:, :chan]
            prev_im = prev[:, chan:]
            c_re = carry_re[pl.ds(slot, 1), :]
            c_im = carry_im[pl.ds(slot, 1), :]
            p_re = prod_re[rows, :]
            p_im = prod_im[rows, :]
            g_re = adj_re[rows, :] + p_re * c_re - p_im * c_im
            g_im = adj_im[rows, :] + p_re * c_im + p_im * c_re
            turn_re = cosine * prev_re - sine * prev_im
            turn_im = sine * prev_re + cosine * prev_im
            flag = flag_ref[slot, 0]
            pre = pre_ref[index, 0]
            keep, sig = keep_of(pre, flag, bias_ref[...], floor, chan)
            fresh = 1.0 - keep
            x_re = pre[:, :chan]
            x_im = pre[:, chan : 2 * chan]
            s_re = jax.nn.sigmoid(x_re)
            s_im = jax.nn.sigmoid(x_im)
            cand_re = (x_re * s_re).astype(BF).astype(F32)
            cand_im = (x_im * s_im).astype(BF).astype(F32)
            grad_keep = g_re * (turn_re - cand_re) + g_im * (turn_im - cand_im)
            sum_theta[...] -= jnp.sum(
                keep * (g_re * turn_im - g_im * turn_re), axis=0, keepdims=True
            )
            grad_forget = (
                grad_keep * (1.0 - flag) * ((1.0 - floor) * (sig * (1.0 - sig)))
            ).astype(BF)
            sum_bias[...] += jnp.sum(grad_forget.astype(F32), axis=0, keepdims=True)
            out_ref[index, 0, :, 2 * chan : 3 * chan] = grad_forget
            cand_grad = (fresh * g_re).astype(BF).astype(F32)
            out_ref[index, 0, :, :chan] = (
                cand_grad * s_re * (1.0 + x_re * (1.0 - s_re))
            ).astype(BF)
            cand_grad = (fresh * g_im).astype(BF).astype(F32)
            out_ref[index, 0, :, chan : 2 * chan] = (
                cand_grad * s_im * (1.0 + x_im * (1.0 - s_im))
            ).astype(BF)


def block_spec(groups, tokens, width):
    mode = pl.Buffered(1) if groups > 4 and width % 128 and width > 1 else None
    return pl.BlockSpec((groups, 1, tokens, width), lambda b: (0, b, 0, 0), pipeline_mode=mode)


def row_spec(width):
    return pl.BlockSpec((1, width), lambda b: (0, 0))


def recur_forward(place, floor, pre_even, pre_odd, flags, bias, theta, gain):
    groups, seqs, tokens, _ = flags.shape
    chan = bias.shape[1]
    half = groups // 2
    scalar = pl.BlockSpec(memory_space=pltpu.SMEM)
    rows = groups * tokens
    pre_spec = block_spec(half, tokens, 5 * chan)
    one = block_spec(groups, tokens, 1)
    gated = block_spec(half, tokens, 2 * chan)
    gated_shape = jax.ShapeDtypeStruct((half, seqs, tokens, 2 * chan), BF)
    size = seqs * rows * chan
    return pl.pallas_call(
        forward_kernel,
        grid=(seqs,),
        in_specs=[
            scalar,
            scalar,
            pre_spec,
            pre_spec,
            one,
            row_spec(chan),
            row_spec(chan),
            row_spec(2 * chan),
        ],
        out_specs=[block_spec(groups, tokens, 2 * chan), gated, gated, one],
        out_shape=[
            jax.ShapeDtypeStruct((groups, seqs, tokens, 2 * chan), F32),
            gated_shape,
            gated_shape,
            jax.ShapeDtypeStruct((groups, seqs, tokens, 1), F32),
        ],
        scratch_shapes=[pltpu.VMEM((rows, chan), F32)] * 5
        + [pltpu.VMEM((groups, chan), F32)] * 2,
        compiler_params=pltpu.CompilerParams(vmem_limit_bytes=56 * 2**20),
        cost_estimate=SMALL,
        name="recur_forward",
    )(place, floor, pre_even, pre_odd, flags, bias, theta, gain)


def recur_backward(
    place, floor, pre_even, pre_odd, flags, bias, theta, gain, state, up_even, up_odd, scale, term
):
    groups, seqs, tokens, _ = flags.shape
    chan = bias.shape[1]
    half = groups // 2
    scalar = pl.BlockSpec(memory_space=pltpu.SMEM)
    rows = groups * tokens
    pre_spec = block_spec(half, tokens, 5 * chan)
    one = block_spec(groups, tokens, 1)
    up_spec = block_spec(half, tokens, 2 * chan)
    out_shape = jax.ShapeDtypeStruct((half, seqs, tokens, 5 * chan), BF)
    scaled_shape = jax.ShapeDtypeStruct((half, seqs, tokens, 2 * chan), BF)
    size = seqs * rows * chan
    return pl.pallas_call(
        backward_kernel,
        grid=(seqs,),
        in_specs=[
            scalar,
            scalar,
            pre_spec,
            pre_spec,
            one,
            row_spec(chan),
            row_spec(chan),
            row_spec(2 * chan),
            block_spec(groups, tokens, 2 * chan),
            up_spec,
            up_spec,
            one,
            one,
        ],
        out_specs=[
            pre_spec,
            pre_spec,
            up_spec,
            up_spec,
            row_spec(chan),
            row_spec(chan),
            row_spec(2 * chan),
        ],
        out_shape=[
            out_shape,
            out_shape,
            scaled_shape,
            scaled_shape,
            jax.ShapeDtypeStruct((1, chan), F32),
            jax.ShapeDtypeStruct((1, chan), F32),
            jax.ShapeDtypeStruct((1, 2 * chan), F32),
        ],
        scratch_shapes=[pltpu.VMEM((rows, chan), F32)] * 5
        + [pltpu.VMEM((groups, chan), F32)] * 3,
        compiler_params=pltpu.CompilerParams(vmem_limit_bytes=56 * 2**20),
        cost_estimate=SMALL,
        name="recur_backward",
    )(
        place, floor, pre_even, pre_odd, flags, bias, theta, gain, state, up_even, up_odd, scale, term
    )


def unpack_columns(packed, out):
    planes = packed.shape[0]
    rows = out.shape[0] // planes
    for plane in range(planes):
        for tile in range(out.shape[1] // LANES):
            out[plane * rows : (plane + 1) * rows, tile * LANES : (tile + 1) * LANES] = packed[
                plane, tile * rows : (tile + 1) * rows, :
            ]


def unpack_rows(packed, first, out):
    planes = packed.shape[0]
    rows = out.shape[0] // planes
    for plane in range(planes):
        for tile in range(out.shape[1] // LANES):
            base = first + tile * rows
            out[plane * rows : (plane + 1) * rows, tile * LANES : (tile + 1) * LANES] = packed[
                plane, base : base + rows, :
            ]


def dot_nn(left, right):
    return jnp.dot(left, right, preferred_element_type=F32)


def dot_nt(left, right):
    return lax.dot_general(left, right, (((1,), (1,)), ((), ())), preferred_element_type=F32)


def dot_tn(left, right):
    return lax.dot_general(left, right, (((0,), (0,)), ((), ())), preferred_element_type=F32)


def dot_nn(left, right):
    return jnp.dot(left, right, preferred_element_type=F32)


def dot_nt(left, right):
    return lax.dot_general(left, right, (((1,), (1,)), ((), ())), preferred_element_type=F32)


def dot_tn(left, right):
    return lax.dot_general(left, right, (((0,), (0,)), ((), ())), preferred_element_type=F32)


PIECES = 5
ANYWHERE = pl.BlockSpec(memory_space=pl.ANY)
SCALAR = pl.BlockSpec(memory_space=pltpu.SMEM)


def block_copies(pieces, held, sems):
    copies = []
    index = 0
    for block, parts in enumerate(pieces):
        copies.append([])
        rows = held.shape[1] // len(parts)
        for part, (ref, offset) in enumerate(parts):
            source = ref if offset is None else ref.at[offset : offset + rows]
            target = held.at[block, part * rows : (part + 1) * rows]
            copies[-1].append(pltpu.make_async_copy(source, target, sems.at[index]))
            index += 1
    return copies


def ffn_kernel(counts, offsets, last, *refs):
    refs = list(refs)

    def take(count):
        taken = refs[:count]
        del refs[:count]
        return taken

    (packed_ref,) = take(1)
    blocks = len(counts)
    normed = [[(ref, None) for ref in take(count)] for count in counts]
    up = [[(ref, None) for ref in take(count)] for count in counts]
    groups = [normed, up]
    if offsets:
        groups.append([[(ref, offset)] for ref, offset in zip(take(blocks), offsets)])
    hidden_ref, grad_ref = take(2)
    backs = take(blocks if last else 1)
    ff_s, down_s = take(2)
    helds = take(len(groups))
    sems = take(len(groups))
    copies = [block_copies(*item) for item in zip(groups, helds, sems)]
    hidden = down_s.shape[0]
    step = pl.program_id(0)

    @pl.when(step == 0)
    def _():
        for block in range(blocks):
            for group in copies:
                for copy in group[block]:
                    copy.start()
        first = ff_s.shape[0] // packed_ref.shape[0] * (ff_s.shape[1] // LANES)
        unpack_columns(packed_ref, ff_s)
        unpack_rows(packed_ref, first, down_s)

    for block in range(blocks):

        @pl.when(step == block)
        def _(block=block):
            for group in copies:
                for copy in group[block]:
                    copy.wait()

    ff = dot_nn(helds[0][step], ff_s[...])
    gate, value = ff[:, :hidden], ff[:, hidden:]
    sig = jax.nn.sigmoid(gate)
    silu = gate * sig
    hidden_ref[...] = (silu * value).astype(BF)
    grad = dot_nt(helds[1][step], down_s[...])
    grad_ref[:, :hidden] = (grad * value * sig * (1.0 + gate * (1.0 - sig))).astype(BF)
    grad_ref[:, hidden:] = (grad * silu).astype(BF)
    back = dot_nt(grad_ref[...], ff_s[...])
    if offsets:
        back = back + helds[2][step]
    if last:
        for block in range(blocks):

            @pl.when(step == block)
            def _(block=block):
                backs[block][...] = back.astype(BF)
    else:
        backs[0][...] = back


def ffn_call(blocks, packed, ff_cols, bases=None, fills=False):
    rows = sum(piece.shape[0] for piece in blocks[0][0])
    width = blocks[0][0][0].shape[1]
    count = len(blocks)
    tokens = count * rows
    hidden = ff_cols // 2
    last = bases is not None
    counts = tuple(len(block[0]) for block in blocks)
    pieces = sum(counts)
    operands = [packed]
    for index in range(2):
        for block in blocks:
            operands += block[index]
    held = pltpu.VMEM((count, rows, width), BF)
    helds = [held, held]
    sems = [pltpu.SemaphoreType.DMA((pieces,))] * 2
    if last:
        operands += [array for array, _ in bases]
        helds.append(pltpu.VMEM((count, rows, width), F32))
        sems.append(pltpu.SemaphoreType.DMA((count,)))
    backs = [jax.ShapeDtypeStruct((tokens, width), F32)]
    back_specs = [pl.BlockSpec((rows, width), lambda i: (i, 0))]
    if last:
        backs = [jax.ShapeDtypeStruct((rows, width), BF)] * count
        back_specs = [pl.BlockSpec((rows, width), lambda i: (0, 0))] * count
    offsets = tuple(offset for _, offset in bases) if last else ()
    return pl.pallas_call(
        functools.partial(ffn_kernel, counts, offsets, last),
        grid=(count,),
        in_specs=[pl.BlockSpec(packed.shape, lambda i: (0, 0, 0), pipeline_mode=pl.Buffered(1))]
        + [ANYWHERE] * (len(operands) - 1),
        out_specs=[
            pl.BlockSpec((rows, hidden), lambda i: (i, 0)),
            pl.BlockSpec((rows, ff_cols), lambda i: (i, 0)),
        ]
        + back_specs,
        out_shape=[
            jax.ShapeDtypeStruct((tokens, hidden), BF),
            jax.ShapeDtypeStruct((tokens, ff_cols), BF),
            *backs,
        ],
        scratch_shapes=[pltpu.VMEM((width, ff_cols), BF), pltpu.VMEM((hidden, width), BF)]
        + helds
        + sems,
        compiler_params=pltpu.CompilerParams(vmem_limit_bytes=60 * 2**20),
        cost_estimate=filler(5 * tokens * width * ff_cols if fills else 1024),
        name="ffn",
    )(*operands)


def grads_kernel(planes, counts, turn_ref, *refs):
    refs = list(refs)
    out_ref = refs.pop()

    def take(count):
        taken = refs[:count]
        del refs[:count]
        return taken

    groups = [(take(count), take(count), *take(2)) for count in counts]
    step = pl.program_id(0)
    steps = pl.num_programs(0)
    block = groups[0][0][0].shape[1]
    run = block // planes
    tiles = groups[0][2].shape[1] // LANES
    count = groups[0][3].shape[1] // planes

    def joined(pieces):
        return jnp.concatenate([piece[...] for piece in pieces], axis=0)

    grad = sum(dot_tn(joined(left), cols[...]) for left, _, cols, _ in groups).astype(BF)
    for plane in range(planes):
        for tile in range(tiles):
            lines = pl.ds(pl.multiple_of((step * tiles + tile) * run, run), run)
            out_ref[plane, lines, :] = grad[
                plane * run : (plane + 1) * run, tile * LANES : (tile + 1) * LANES
            ]
    grad = sum(dot_tn(rows[...], joined(up)) for _, up, _, rows in groups).astype(BF)
    first = block // planes * tiles * steps
    for index in range(planes):
        plane = lax.rem(turn_ref[0] + index, planes)
        for tile in range(block // LANES):
            base = first + (step * (block // LANES) + tile) * count
            lines = pl.ds(pl.multiple_of(base, 16), count)
            out_ref[plane, lines, :] = grad[
                index * count : (index + 1) * count, tile * LANES : (tile + 1) * LANES
            ]


def grads_call(steps, planes, turn, groups):
    width = groups[0][0][0].shape[1]
    block = width // steps
    col_count = groups[0][2].shape[1]
    row_count = groups[0][3].shape[1]
    tokens = sum(group[2].shape[0] for group in groups)
    lines = (col_count * width + row_count * width) // (planes * LANES)
    operands, specs = [turn], [SCALAR]
    for left, up, cols, rows in groups:
        for piece in (*left, *up):
            operands.append(piece)
            specs.append(pl.BlockSpec((piece.shape[0], block), lambda i: (0, i)))
        for array in (cols, rows):
            operands.append(array)
            specs.append(
                pl.BlockSpec(array.shape, lambda i: (0, 0), pipeline_mode=pl.Buffered(1))
            )
    return pl.pallas_call(
        functools.partial(grads_kernel, planes, tuple(len(group[0]) for group in groups)),
        grid=(steps,),
        in_specs=specs,
        out_specs=pl.BlockSpec((planes, lines, LANES), lambda i: (0, 0, 0)),
        out_shape=jax.ShapeDtypeStruct((planes, lines, LANES), BF),
        compiler_params=pltpu.CompilerParams(vmem_limit_bytes=60 * 2**20),
        cost_estimate=filler(4 * tokens * width * (col_count + row_count)),
        name="weight_grads",
    )(*operands)


def result_kernel(firsts, places, counts, *refs):
    hiddens = (refs[: counts[0]], refs[counts[0] : sum(counts)])
    refs = refs[sum(counts) :]
    outs, down_s = refs[2:-1], refs[-1]
    step = pl.program_id(0)
    first_rows = hiddens[0][0].shape[1]

    @pl.when(step == 0)
    def _():
        unpack_rows(refs[0], firsts[0], down_s.at[:first_rows])
        unpack_rows(refs[1], firsts[1], down_s.at[first_rows:])

    for slot, out in enumerate(outs):

        @pl.when(step == slot)
        def _(slot=slot, out=out):
            rows = out.shape[0]
            parts = []
            for arrays, (index, offset) in zip(hiddens, places[slot]):
                parts.append(arrays[index][offset : offset + rows, :])
            total = dot_nn(parts[0], down_s[:first_rows, :])
            total = total + dot_nn(parts[1], down_s[first_rows:, :])
            out[...] = total.astype(BF)


def result_call(hiddens, places, packed, rows, width):
    slots = len(places)
    total = hiddens[0][0].shape[1] + hiddens[1][0].shape[1]
    firsts = tuple(
        part.shape[1] - arrays[0].shape[1] // part.shape[0] * width // LANES
        for part, arrays in zip(packed, hiddens)
    )
    arrays = [*hiddens[0], *hiddens[1]]

    def whole(array):
        zeros = (0,) * array.ndim
        return pl.BlockSpec(array.shape, lambda i: zeros, pipeline_mode=pl.Buffered(1))

    return pl.pallas_call(
        functools.partial(
            result_kernel, firsts, places, (len(hiddens[0]), len(hiddens[1]))
        ),
        grid=(slots,),
        in_specs=[whole(array) for array in arrays] + [whole(part) for part in packed],
        out_specs=[pl.BlockSpec((rows, width), lambda i: (0, 0))] * slots,
        out_shape=[jax.ShapeDtypeStruct((rows, width), BF)] * slots,
        scratch_shapes=[pltpu.VMEM((total, width), BF)],
        compiler_params=pltpu.CompilerParams(vmem_limit_bytes=48 * 2**20),
        cost_estimate=filler(2 * slots * rows * width * total),
        name="ffn_result",
    )(*arrays, *packed)


def seq_copies(pieces, held, sems, seq):
    tokens = held.shape[2]
    rows = slice(seq * tokens, (seq + 1) * tokens)
    copies = [
        pltpu.make_async_copy(pieces[slot].at[rows], held.at[seq, slot], sems.at[seq, slot])
        for slot in range(3)
    ]
    copies.append(pltpu.make_async_copy(pieces[3 + seq], held.at[seq, 3], sems.at[seq, 3]))
    return copies


def fetch(groups):
    seqs = groups[0][1].shape[0]

    @pl.when(pl.program_id(0) == 0)
    def _():
        for seq in range(seqs):
            for pieces, held, sems in groups:
                for copy in seq_copies(pieces, held, sems, seq):
                    copy.start()


def arrive(groups):
    for seq in range(groups[0][1].shape[0]):

        @pl.when(pl.program_id(0) == seq)
        def _(seq=seq):
            for pieces, held, sems in groups:
                for copy in seq_copies(pieces, held, sems, seq):
                    copy.wait()


def unpack_mix(packed_ref, rec_s, out_s):
    @pl.when(pl.program_id(0) == 0)
    def _():
        lines = rec_s.shape[0] // packed_ref.shape[0] * (rec_s.shape[1] // LANES)
        unpack_columns(packed_ref, rec_s)
        unpack_rows(packed_ref, lines, out_s)


def mix_forward_kernel(*refs):
    place_ref, floor_ref, packed_ref, flag_ref, bias_ref, theta_ref, gain_ref = refs[:7]
    refs = refs[7:]
    even, odd = refs[:PIECES], refs[PIECES : 2 * PIECES]
    refs = refs[2 * PIECES :]
    pre_even, pre_odd, state_ref, square_ref = refs[:4]
    mix_even, mix_odd = refs[4:8], refs[8:12]
    rec_s, out_s, gated_even, gated_odd, x_even, x_odd, sems_even, sems_odd = refs[12:20]
    scratch = refs[20:]
    half, _, tokens, _ = pre_even.shape
    seq = pl.program_id(0)
    groups = ((even, x_even, sems_even), (odd, x_odd, sems_odd))
    fetch(groups)
    unpack_mix(packed_ref, rec_s, out_s)
    arrive(groups)
    for x_ref, pre_ref in ((x_even, pre_even), (x_odd, pre_odd)):

        @pl.loop(0, half, step=2)
        def _(index, x_ref=x_ref, pre_ref=pre_ref):
            pair = pl.ds(index, 2)
            x = x_ref[seq, pair].reshape(2 * tokens, -1)
            pre_ref[pair, 0] = dot_nn(x, rec_s[...]).reshape(2, tokens, -1)

    forward_kernel(
        place_ref,
        floor_ref,
        pre_even,
        pre_odd,
        flag_ref,
        bias_ref,
        theta_ref,
        gain_ref,
        state_ref,
        gated_even,
        gated_odd,
        square_ref,
        *scratch,
    )
    for gated_ref, mixes in ((gated_odd, mix_odd), (gated_even, mix_even)):
        for index in range(0, half, 2):
            gated = gated_ref[index : index + 2, 0].reshape(2 * tokens, -1)
            mix = dot_nn(gated, out_s[...]).astype(BF)
            mixes[index][0] = mix[:tokens]
            mixes[index + 1][0] = mix[tokens:]


def mix_forward(place, floor, even, odd, packed, flags, bias, theta, gain):
    groups, seqs, tokens, _ = flags.shape
    chan = bias.shape[1]
    half = groups // 2
    width = even[0].shape[-1]
    rows = groups * tokens
    pre_spec = block_spec(half, tokens, 5 * chan)
    one = block_spec(groups, tokens, 1)
    pre_shape = jax.ShapeDtypeStruct((half, seqs, tokens, 5 * chan), F32)
    mix_spec = pl.BlockSpec((1, tokens, width), lambda b: (b, 0, 0))
    mix_shape = jax.ShapeDtypeStruct((seqs, tokens, width), BF)
    gated = pltpu.VMEM((half, 1, tokens, 2 * chan), BF)
    held = pltpu.VMEM((seqs, half, tokens, width), BF)
    sems = pltpu.SemaphoreType.DMA((seqs, half))
    return pl.pallas_call(
        mix_forward_kernel,
        grid=(seqs,),
        in_specs=[
            SCALAR,
            SCALAR,
            pl.BlockSpec(packed.shape, lambda b: (0, 0, 0), pipeline_mode=pl.Buffered(1)),
            one,
            row_spec(chan),
            row_spec(chan),
            row_spec(2 * chan),
        ]
        + [ANYWHERE] * (2 * PIECES),
        out_specs=[pre_spec, pre_spec, block_spec(groups, tokens, 2 * chan), one]
        + [mix_spec] * (2 * half),
        out_shape=[
            pre_shape,
            pre_shape,
            jax.ShapeDtypeStruct((groups, seqs, tokens, 2 * chan), F32),
            jax.ShapeDtypeStruct((groups, seqs, tokens, 1), F32),
        ]
        + [mix_shape] * (2 * half),
        scratch_shapes=[
            pltpu.VMEM((width, 5 * chan), BF),
            pltpu.VMEM((2 * chan, width), BF),
            gated,
            gated,
            held,
            held,
            sems,
            sems,
        ]
        + [pltpu.VMEM((rows, chan), F32)] * 5
        + [pltpu.VMEM((groups, chan), F32)] * 2,
        compiler_params=pltpu.CompilerParams(vmem_limit_bytes=60 * 2**20),
        cost_estimate=SMALL,
        name="mix_forward",
    )(place, floor, packed, flags, bias, theta, gain, *even, *odd)


def mix_backward_kernel(*refs):
    place_ref, floor_ref, packed_ref = refs[:3]
    pre_even, pre_odd, flag_ref, bias_ref, theta_ref, gain_ref, state_ref = refs[3:10]
    scale_ref, term_ref = refs[10:12]
    refs = refs[12:]
    even, odd = refs[:PIECES], refs[PIECES : 2 * PIECES]
    refs = refs[2 * PIECES :]
    out_even, out_odd, scaled_even, scaled_odd, sum_bias, sum_theta, sum_gain = refs[:7]
    back_even, back_odd = refs[7:11], refs[11:15]
    rec_s, out_s, up_even, up_odd, x_even, x_odd, sems_even, sems_odd = refs[15:23]
    scratch = refs[23:]
    half, _, tokens, _ = pre_even.shape
    seq = pl.program_id(0)
    groups = ((even, x_even, sems_even), (odd, x_odd, sems_odd))
    fetch(groups)
    unpack_mix(packed_ref, rec_s, out_s)
    arrive(groups)
    for x_ref, up_ref in ((x_even, up_even), (x_odd, up_odd)):

        @pl.loop(0, half, step=2)
        def _(index, x_ref=x_ref, up_ref=up_ref):
            pair = pl.ds(index, 2)
            branch = x_ref[seq, pair].reshape(2 * tokens, -1)
            up_ref[pair, 0] = dot_nt(branch, out_s[...]).reshape(2, tokens, -1)

    backward_kernel(
        place_ref,
        floor_ref,
        pre_even,
        pre_odd,
        flag_ref,
        bias_ref,
        theta_ref,
        gain_ref,
        state_ref,
        up_even,
        up_odd,
        scale_ref,
        term_ref,
        out_even,
        out_odd,
        scaled_even,
        scaled_odd,
        sum_bias,
        sum_theta,
        sum_gain,
        *scratch,
    )
    for out_ref, backs in ((out_odd, back_odd), (out_even, back_even)):
        for index in range(0, half, 2):
            grad = out_ref[index : index + 2, 0].reshape(2 * tokens, -1)
            back = dot_nt(grad, rec_s[...]).astype(BF)
            backs[index][0] = back[:tokens]
            backs[index + 1][0] = back[tokens:]


def mix_backward(
    place, floor, packed, pre_even, pre_odd, flags, bias, theta, gain, state, scale, term,
    even, odd,
):
    groups, seqs, tokens, _ = flags.shape
    chan = bias.shape[1]
    half = groups // 2
    width = even[0].shape[-1]
    rows = groups * tokens
    pre_spec = block_spec(half, tokens, 5 * chan)
    one = block_spec(groups, tokens, 1)
    pair_spec = block_spec(half, tokens, 2 * chan)
    back_spec = pl.BlockSpec((1, tokens, width), lambda b: (b, 0, 0))
    pre_shape = jax.ShapeDtypeStruct((half, seqs, tokens, 5 * chan), BF)
    pair_shape = jax.ShapeDtypeStruct((half, seqs, tokens, 2 * chan), BF)
    up = pltpu.VMEM((half, 1, tokens, 2 * chan), F32)
    held = pltpu.VMEM((seqs, half, tokens, width), BF)
    sems = pltpu.SemaphoreType.DMA((seqs, half))
    return pl.pallas_call(
        mix_backward_kernel,
        grid=(seqs,),
        in_specs=[
            SCALAR,
            SCALAR,
            pl.BlockSpec(packed.shape, lambda b: (0, 0, 0), pipeline_mode=pl.Buffered(1)),
            pre_spec,
            pre_spec,
            one,
            row_spec(chan),
            row_spec(chan),
            row_spec(2 * chan),
            block_spec(groups, tokens, 2 * chan),
            one,
            one,
        ]
        + [ANYWHERE] * (2 * PIECES),
        out_specs=[
            pre_spec,
            pre_spec,
            pair_spec,
            pair_spec,
            row_spec(chan),
            row_spec(chan),
            row_spec(2 * chan),
        ]
        + [back_spec] * (2 * half),
        out_shape=[
            pre_shape,
            pre_shape,
            pair_shape,
            pair_shape,
            jax.ShapeDtypeStruct((1, chan), F32),
            jax.ShapeDtypeStruct((1, chan), F32),
            jax.ShapeDtypeStruct((1, 2 * chan), F32),
        ]
        + [jax.ShapeDtypeStruct((seqs, tokens, width), BF)] * (2 * half),
        scratch_shapes=[
            pltpu.VMEM((width, 5 * chan), BF),
            pltpu.VMEM((2 * chan, width), BF),
            up,
            up,
            held,
            held,
            sems,
            sems,
        ]
        + [pltpu.VMEM((rows, chan), F32)] * 5
        + [pltpu.VMEM((groups, chan), F32)] * 3,
        compiler_params=pltpu.CompilerParams(vmem_limit_bytes=60 * 2**20),
        cost_estimate=SMALL,
        name="mix_backward",
    )(
        place, floor, packed, pre_even, pre_odd, flags, bias, theta, gain, state, scale,
        term, *even, *odd,
    )


def assemble_tiles_kernel(shares, planes, *refs):
    sources, outs = refs[: len(shares)], refs[len(shares) :]
    groups = sources[0].shape[0]
    run = sum(shares)
    for group in range(groups):
        wides = [
            jnp.concatenate(
                [source[group, tile].astype(F32) for tile in range(source.shape[1])], axis=1
            )
            for source in sources
        ]
        firsts = [0] * len(shares)
        for out in outs:
            for block in range(out.shape[1] // (groups * run)):
                where = group
                if planes:
                    where = (block + group) % planes + planes * (group // planes)
                base = (block * groups + where) * run
                for index, share in enumerate(shares):
                    first = firsts[index]
                    out[:, base : base + share] = wides[index][:, first : first + share]
                    firsts[index] += share
                    base += share


def assemble_tiles(parts, shares, planes, widths):
    rows = parts[0].shape[2]
    return pl.pallas_call(
        functools.partial(assemble_tiles_kernel, shares, planes),
        out_shape=[jax.ShapeDtypeStruct((rows, width), F32) for width in widths],
        compiler_params=pltpu.CompilerParams(vmem_limit_bytes=48 * 2**20),
        cost_estimate=SMALL,
        name="assemble_columns",
    )(*parts)


def assemble_rows_kernel(*refs):
    out = refs[-1]
    base = 0
    for source in refs[:-1]:
        tiles, rows, _ = source.shape
        for tile in range(tiles):
            out[base : base + rows, tile * LANES : (tile + 1) * LANES] = source[tile].astype(F32)
        base += rows


def assemble_rows(parts):
    rows = sum(part.shape[1] for part in parts)
    width = parts[0].shape[0] * LANES
    return pl.pallas_call(
        assemble_rows_kernel,
        out_shape=jax.ShapeDtypeStruct((rows, width), F32),
        compiler_params=pltpu.CompilerParams(vmem_limit_bytes=48 * 2**20),
        cost_estimate=SMALL,
        name="assemble_rows",
    )(*parts)


def shard_gather(value):
    return lax.all_gather(value, "wshard", axis=0, tiled=True)


def shard_scatter(value):
    return lax.psum_scatter(value, "wshard", scatter_dimension=0, tiled=True)


def plain_body(
    tokens,
    starts,
    layer_index,
    gain_mix,
    w_in,
    w_forget,
    bias_forget,
    theta,
    w_gate_out,
    gain_out,
    w_out,
    gain_ffn,
    w_ffgate,
    w_ffup,
    w_down,
    out_grad,
):
    seqs, seq_dev, width = tokens.shape
    rows = seqs * seq_dev
    groups = lax.axis_size("seq")
    planes = lax.axis_size("wshard")
    half = groups // 2
    devices = groups * planes
    place = lax.axis_index("seq")
    floor = layer_index.astype(F32) / LAYERS
    mix_run = w_out.shape[0] // groups
    ffn_run = w_down.shape[0] // groups
    chan = mix_run * planes // 2
    hidden = ffn_run * planes

    def own_columns(array, run):
        count = array.shape[1] // (run * groups)
        column = lax.broadcasted_iota(jnp.int32, (array.shape[1], count * run), 0)
        index = lax.broadcasted_iota(jnp.int32, (array.shape[1], count * run), 1)
        block = index // run
        chosen = column == block * (run * groups) + place * run + (index - block * run)
        return dot(array, chosen.astype(BF), "rc,cj->rj").astype(BF)

    def own_parts(vector):
        count = vector.shape[0] // (mix_run * groups)
        split = vector.reshape(count, groups, mix_run)
        return lax.dynamic_slice_in_dim(split, place, 1, 1).reshape(1, count * mix_run)

    def own_rows(array):
        run = array.shape[0] // groups
        return lax.dynamic_slice_in_dim(array, place * run, run, 0)

    resid_in = tokens.reshape(rows, width).astype(F32)
    scale_in = lax.rsqrt(jnp.mean(resid_in * resid_in, axis=1, keepdims=True) + EPS)
    normed_own = (resid_in * scale_in * gain_mix).astype(BF)
    normed_even, normed_odd = plain_gather(normed_own)
    upstream_own = out_grad.reshape(rows, width)

    rec_w = shard_gather(
        jnp.concatenate(
            [
                own_columns(w_in, mix_run),
                own_columns(w_forget, mix_run),
                own_columns(w_gate_out, mix_run),
            ],
            axis=1,
        )
    )
    out_w = shard_gather(own_rows(w_out))
    ff_w = shard_gather(
        jnp.concatenate([own_columns(w_ffgate, ffn_run), own_columns(w_ffup, ffn_run)], axis=1)
    )
    down_w = shard_gather(own_rows(w_down))

    slots = lax.broadcasted_iota(jnp.int32, (groups, groups), 0)
    sources = lax.broadcasted_iota(jnp.int32, (groups, groups), 1)
    keys = jnp.where(slots < half, 2 * slots, 2 * (slots - half) + 1)
    chosen = ((place ^ keys) == sources).astype(F32)
    marks = starts.astype(F32).reshape(seqs, groups, seq_dev).transpose(1, 0, 2)
    flags = jnp.sum(chosen[:, :, None, None] * marks[None], axis=1)[..., None]
    bias_own = own_parts(bias_forget)
    theta_own = own_parts(theta)
    gain_own = own_parts(gain_out)
    place_one = place.reshape(1)

    def blocks(array):
        return array.reshape(half, seqs, seq_dev, -1)

    pre_even = blocks(dot(normed_even, rec_w, "td,dc->tc"))
    pre_odd = blocks(dot(normed_odd, rec_w, "td,dc->tc"))
    state, gated_even, gated_odd, square = recur_forward(
        place_one, floor, pre_even, pre_odd, flags, bias_own, theta_own, gain_own
    )
    gated_even = gated_even.reshape(half * rows, 2 * chan)
    gated_odd = gated_odd.reshape(half * rows, 2 * chan)

    def mix(gated):
        return dot(gated, out_w, "tc,cd->td").astype(BF)

    square_own = scatter_small(square.reshape(groups, rows))
    scale_own = lax.rsqrt(square_own / width + EPS)
    scale_out = scale_own.reshape(rows, 1)
    branch_mix = scale_out * plain_scatter(mix(gated_even), mix(gated_odd))
    resid = resid_in + branch_mix
    scale_ffn = lax.rsqrt(jnp.mean(resid * resid, axis=1, keepdims=True) + EPS)
    ffn_even, ffn_odd = plain_gather((resid * scale_ffn * gain_ffn).astype(BF))
    scale_all = gather_small(scale_own)
    up_even, up_odd = plain_gather(upstream_own)

    def ffn(normed, upstream):
        ff = dot(normed, ff_w, "td,df->tf")
        ffn_gate, ffn_up = ff[:, :hidden], ff[:, hidden:]
        sig_ffn = jax.nn.sigmoid(ffn_gate)
        silu_ffn = ffn_gate * sig_ffn
        ffn_hidden = (silu_ffn * ffn_up).astype(BF)
        grad_hidden = dot(upstream, down_w, "td,fd->tf")
        grad_gate = grad_hidden * ffn_up * sig_ffn * (1.0 + ffn_gate * (1.0 - sig_ffn))
        grad_up = grad_hidden * silu_ffn
        grad_ff = jnp.concatenate([grad_gate.astype(BF), grad_up.astype(BF)], axis=1)
        return ffn_hidden, grad_ff

    hidden_odd, grad_ff_odd = ffn(ffn_odd, up_odd)
    hidden_even, grad_ff_even = ffn(ffn_even, up_even)
    grad_normed_ffn = plain_scatter(
        dot(grad_ff_even, ff_w, "tf,df->td").astype(BF),
        dot(grad_ff_odd, ff_w, "tf,df->td").astype(BF),
    )
    branch_ffn = plain_scatter(
        dot(hidden_even, down_w, "tf,fd->td").astype(BF),
        dot(hidden_odd, down_w, "tf,fd->td").astype(BF),
    )
    result = (resid + branch_ffn).astype(BF)

    scaled_ffn = grad_normed_ffn * gain_ffn
    grad_resid = (
        upstream_own.astype(F32)
        + scale_ffn * scaled_ffn
        - resid * scale_ffn**3 * jnp.mean(scaled_ffn * resid, axis=1, keepdims=True)
    )
    grad_gain_ffn = jnp.sum(grad_normed_ffn * resid * scale_ffn, axis=0)
    grad_branch_own = grad_resid.astype(BF)
    overlap = jnp.sum(grad_branch_own.astype(F32) * branch_mix, axis=1)
    term_all = gather_small((scale_out[:, 0] ** 2 * overlap / width)[None])
    branch_even, branch_odd = plain_gather(grad_branch_own)
    grad_gated_even = blocks(dot(branch_even, out_w, "td,cd->tc"))
    grad_gated_odd = blocks(dot(branch_odd, out_w, "td,cd->tc"))

    shape_one = (groups, seqs, seq_dev, 1)
    grad_even, grad_odd, scaled_even, scaled_odd, sum_bias, sum_theta, sum_gain = recur_backward(
        place_one,
        floor,
        pre_even,
        pre_odd,
        flags,
        bias_own,
        theta_own,
        gain_own,
        state,
        grad_gated_even,
        grad_gated_odd,
        scale_all.reshape(shape_one),
        term_all.reshape(shape_one),
    )
    grad_even = grad_even.reshape(half * rows, 5 * chan)
    grad_odd = grad_odd.reshape(half * rows, 5 * chan)
    grad_normed_in = plain_scatter(
        dot(grad_even, rec_w, "tc,dc->td").astype(BF),
        dot(grad_odd, rec_w, "tc,dc->td").astype(BF),
    )
    scaled_in = grad_normed_in * gain_mix
    grad_tokens = (
        grad_resid
        + scale_in * scaled_in
        - resid_in * scale_in**3 * jnp.mean(scaled_in * resid_in, axis=1, keepdims=True)
    ).astype(BF)
    grad_gain_mix = jnp.sum(grad_normed_in * resid_in * scale_in, axis=0)

    def pair_dot(left, right, form):
        return dot(left[0], right[0], form) + dot(left[1], right[1], form)

    def to_owner(grad):
        run = grad.shape[0] // devices
        part = grad.astype(BF).reshape(groups, planes, run, -1).transpose(1, 0, 2, 3)
        part = shard_scatter(part.reshape(grad.shape)).reshape(groups, run, -1)
        return lax.all_to_all(part, "seq", split_axis=0, concat_axis=0, tiled=True)

    def columns(part, run):
        source, count, cols = part.shape
        split = part.reshape(source, count, cols // run, run)
        return split.transpose(1, 2, 0, 3).reshape(count, -1).astype(F32)

    scaled_even = scaled_even.reshape(half * rows, 2 * chan)
    scaled_odd = scaled_odd.reshape(half * rows, 2 * chan)
    ff_grad = to_owner(
        pair_dot((ffn_even, ffn_odd), (grad_ff_even, grad_ff_odd), "td,tf->df")
    )
    grad_w_ffgate = columns(ff_grad[..., :hidden], ffn_run)
    grad_w_ffup = columns(ff_grad[..., hidden:], ffn_run)
    rec_grad = to_owner(pair_dot((normed_even, normed_odd), (grad_even, grad_odd), "td,tc->dc"))
    grad_w_in = columns(rec_grad[..., : 2 * chan], mix_run)
    grad_w_forget = columns(rec_grad[..., 2 * chan : 3 * chan], mix_run)
    grad_w_gate = columns(rec_grad[..., 3 * chan :], mix_run)

    pairs = [
        (s * planes + w, w * groups + s) for s in range(groups) for w in range(planes)
    ]

    def rows_to_owner(grad):
        part = shard_scatter(grad.astype(BF))
        return lax.ppermute(part, ("seq", "wshard"), pairs).astype(F32)

    grad_w_down = rows_to_owner(
        pair_dot((hidden_even, hidden_odd), (up_even, up_odd), "tf,td->fd")
    )
    grad_w_out = rows_to_owner(
        pair_dot((scaled_even, scaled_odd), (branch_even, branch_odd), "tc,td->cd")
    )

    def spread(part):
        count = part.shape[1] // mix_run
        zero = jnp.zeros((count, groups, mix_run), F32)
        zero = lax.dynamic_update_slice(zero, part.reshape(count, 1, mix_run), (0, place, 0))
        return zero.reshape(-1)

    pieces = [
        spread(sum_bias),
        spread(sum_theta),
        spread(sum_gain),
        grad_gain_ffn,
        grad_gain_mix,
        jnp.stack(
            [
                jnp.sum(resid_in * resid_in),
                jnp.sum(branch_mix * branch_mix),
                jnp.sum(branch_ffn * branch_ffn),
            ]
        ),
    ]
    sums = sum_seq(jnp.concatenate(pieces))
    sums = sum_tree([sums, *others(sums)])
    cuts = []
    offset = 0
    for piece in pieces:
        cuts.append(sums[offset : offset + piece.shape[0]])
        offset += piece.shape[0]
    grad_bias, grad_theta, grad_gain_out, grad_gain_ffn, grad_gain_mix, squares = cuts
    rms_values = jnp.sqrt(squares / (rows * width * devices))
    return (
        result.reshape(seqs, seq_dev, width),
        grad_tokens.reshape(seqs, seq_dev, width),
        grad_gain_mix,
        grad_w_in,
        grad_w_forget,
        grad_bias,
        grad_theta,
        grad_w_gate,
        grad_gain_out,
        grad_w_out,
        grad_gain_ffn,
        grad_w_ffgate,
        grad_w_ffup,
        grad_w_down,
        rms_values,
    )


def body(
    tokens,
    starts,
    layer_index,
    gain_mix,
    w_in,
    w_forget,
    bias_forget,
    theta,
    w_gate_out,
    gain_out,
    w_out,
    gain_ffn,
    w_ffgate,
    w_ffup,
    w_down,
    out_grad,
):
    seqs, seq_dev, width = tokens.shape
    rows = seqs * seq_dev
    groups = lax.axis_size("seq")
    planes = lax.axis_size("wshard")
    half = groups // 2
    devices = groups * planes
    mix_run = w_out.shape[0] // groups
    ffn_run = w_down.shape[0] // groups
    chan = mix_run * planes // 2
    shares = (ffn_run * 6 // 11, ffn_run - ffn_run * 6 // 11)
    if not (
        groups == 8
        and groups % planes == 0
        and seqs == 2
        and chan % LANES == 0
        and all(2 * planes * share % LANES == 0 and share % 16 == 0 for share in shares)
    ):
        return plain_body(
            tokens,
            starts,
            layer_index,
            gain_mix,
            w_in,
            w_forget,
            bias_forget,
            theta,
            w_gate_out,
            gain_out,
            w_out,
            gain_ffn,
            w_ffgate,
            w_ffup,
            w_down,
            out_grad,
        )
    place = lax.axis_index("seq")
    floor = layer_index.astype(F32) / LAYERS
    place_one = place.reshape(1)

    first_bit, second_bit = chip_bits()

    def turned(block):
        return lax.rem(block + place, planes) + planes * (place // planes)

    def own_columns(array, run, first, count, where):
        blocks = array.shape[1] // (run * groups)
        column = lax.broadcasted_iota(jnp.int32, (array.shape[1], blocks * count), 0)
        index = lax.broadcasted_iota(jnp.int32, (array.shape[1], blocks * count), 1)
        block = index // count
        wanted = (block * groups + where(block)) * run + first + (index - block * count)
        return dot(array, (column == wanted).astype(BF), "rc,cj->rj").astype(BF)

    def own_parts(vector):
        count = vector.shape[0] // (mix_run * groups)
        split = vector.reshape(count, groups, mix_run)
        return lax.dynamic_slice_in_dim(split, place, 1, 1).reshape(1, count * mix_run)

    def own_rows(array, first, count, where):
        run = array.shape[0] // groups
        return lax.dynamic_slice_in_dim(array, where * run + first, count, 0)

    rec_own = jnp.concatenate(
        [
            own_columns(array, mix_run, 0, mix_run, lambda block: place)
            for array in (w_in, w_forget, w_gate_out)
        ],
        axis=1,
    )
    packs = [pack([rec_own[None], own_rows(w_out, 0, mix_run, place)[None]])]
    first = 0
    for share in shares:
        ff_own = jnp.concatenate(
            [own_columns(array, ffn_run, first, share, turned) for array in (w_ffgate, w_ffup)], axis=1
        )
        packs.append(pack([ff_own[None], own_rows(w_down, first, share, turned(lax.axis_index("wshard")))[None]]))
        first += share
    rec_packed = gather_packed(packs[0])

    upstream_own = out_grad.reshape(rows, width)
    up_stage = gather_first(upstream_own)
    tokens_, up_stage = tied(after(tokens, packs[0]), up_stage)
    resid_in = tokens_.reshape(rows, width).astype(F32)
    scale_in = lax.rsqrt(jnp.mean(resid_in * resid_in, axis=1, keepdims=True) + EPS)
    normed_own = (resid_in * scale_in * gain_mix).astype(BF)
    normed_stage = gather_first(normed_own)
    normed_stage, packs[1], packs[2] = tied(normed_stage, packs[1], packs[2])
    normed_far = gather_far(normed_own, normed_stage)
    normed_even = (normed_own, *normed_stage, *normed_far)
    normed_odd = cross(normed_even)
    up_far = gather_far(upstream_own, up_stage)
    packed = [gather_packed(item) for item in packs[1:]]

    slots = lax.broadcasted_iota(jnp.int32, (groups, groups), 0)
    sources = lax.broadcasted_iota(jnp.int32, (groups, groups), 1)
    keys = jnp.where(slots < half, 2 * slots, 2 * (slots - half) + 1)
    chosen = ((place ^ keys) == sources).astype(F32)
    marks = starts.astype(F32).reshape(seqs, groups, seq_dev).transpose(1, 0, 2)
    flags = jnp.sum(chosen[:, :, None, None] * marks[None], axis=1)[..., None]
    bias_own = own_parts(bias_forget)
    theta_own = own_parts(theta)
    gain_own = own_parts(gain_out)

    pre_even, pre_odd, state, square, *mixes = mix_forward(
        place_one,
        floor,
        normed_even,
        normed_odd,
        rec_packed,
        flags,
        bias_own,
        theta_own,
        gain_own,
    )
    mixes = tuple(item.reshape(rows, width) for item in mixes)
    mix_even, mix_odd = mixes[:half], mixes[half:]
    mix_odd, up_far = tied(mix_odd, up_far)
    up_even = (upstream_own, *up_stage, *up_far)
    square = shrink(square.reshape(groups, rows), 1)
    mix_crossed = cross(mix_odd)
    mix_far = scatter_far(mix_even[3], mix_crossed[3])
    square_next = shrink(square, second_bit)
    mix_far, square_next = tied(mix_far, square_next)
    mix_near = scatter_near(mix_even[1:3], mix_crossed[1:3], mix_far)
    up_odd = cross(up_even)
    square_own = shrink(square_next, first_bit)
    scale_own = lax.rsqrt(square_own / width + EPS)
    scale_out = scale_own.reshape(rows, 1)
    branch_mix = scale_out * scatter_sum(mix_even[0], mix_crossed[0], mix_near)
    resid = resid_in + branch_mix
    scale_ffn = lax.rsqrt(jnp.mean(resid * resid, axis=1, keepdims=True) + EPS)
    ffn_own = (resid * scale_ffn * gain_ffn).astype(BF)
    ffn_stage = gather_first(ffn_own)
    ffn_far = gather_far(ffn_own, ffn_stage)
    scale_all = gather_small(scale_own)

    cols = [2 * planes * share for share in shares]

    def block(normed, up, slot):
        cut = slice(slot, slot + 1) if slot < 3 else slice(3, None)
        return normed[cut], up[cut]

    def grouped(blocks, out):
        return (
            [piece for item in blocks for piece in item[0]],
            [piece for item in blocks for piece in item[1]],
            out[1],
            out[0],
        )

    def gradients(groups_, turn):
        return grads_call(groups, planes, turn, groups_)

    ffn_near = (ffn_own, *ffn_stage)
    even_blocks = [block(ffn_near, up_even, slot) for slot in range(3)]
    even_out = ffn_call(even_blocks, packed[0], cols[0], fills=True)
    odd_near = cross(ffn_near)
    odd_blocks = [block(odd_near, up_odd, slot) for slot in range(3)]
    odd_out = ffn_call(odd_blocks, packed[0], cols[0], fills=True)
    ffn_far, odd_out = tied(ffn_far, odd_out)
    odd_far = cross(ffn_far)
    ffn_even = (*ffn_near, *ffn_far)
    ffn_odd = (*odd_near, *odd_far)
    far_blocks = [block(ffn_even, up_even, 3), block(ffn_odd, up_odd, 3)]
    far_out = ffn_call(far_blocks, packed[0], cols[0])
    firsts = [
        (even_blocks, even_out),
        (odd_blocks, odd_out),
        (far_blocks, far_out),
    ]
    ff_grads = [gradients([grouped(*item) for item in firsts], place_one)]
    even_place = [(0, 0), (0, rows), (0, 2 * rows), (2, 0)]
    odd_place = [(1, 0), (1, rows), (1, 2 * rows), (2, rows)]

    def base(place_):
        return firsts[place_[0]][1][2], place_[1]

    packed[1], ff_grads[0], scale_all, _ = tied(packed[1], ff_grads[0], scale_all, far_out)
    far_blocks = [block(ffn_odd, up_odd, 3), block(ffn_even, up_even, 3)]
    far_out = ffn_call(far_blocks, packed[1], cols[1], [base(odd_place[3]), base(even_place[3])])
    (far_crossed,) = cross([far_out[2]])
    back_far = scatter_far(far_out[3], far_crossed)
    near_packed, _ = tied(packed[1], far_crossed)
    near_blocks = [block(ffn_odd, up_odd, slot) for slot in (1, 2)]
    near_blocks += [block(ffn_even, up_even, slot) for slot in (1, 2)]
    near_out = ffn_call(
        near_blocks,
        near_packed,
        cols[1],
        [base(odd_place[1]), base(odd_place[2]), base(even_place[1]), base(even_place[2])],
        True,
    )
    back_far, near_out = tied(back_far, near_out)
    near_crossed = cross(near_out[2:4])
    back_sums = near_sums(near_out[4:6], near_crossed, back_far)
    back_near = to_neighbours(back_sums)
    own_packed, _ = tied(packed[1], back_sums)
    own_blocks = [block(ffn_odd, up_odd, 0), block(ffn_even, up_even, 0)]
    own_out = ffn_call(
        own_blocks, own_packed, cols[1], [base(odd_place[0]), base(even_place[0])], True
    )
    (own_crossed,) = cross([own_out[2]])
    seconds = [(far_blocks, far_out), (near_blocks, near_out), (own_blocks, own_out)]
    ff_grads.append(gradients([grouped(*item) for item in seconds], place_one))
    back_near, ff_grads[1], own_crossed = tied(back_near, ff_grads[1], own_crossed)
    grad_normed_ffn = scatter_sum(own_out[3], own_crossed, back_near)

    scaled_ffn = grad_normed_ffn * gain_ffn
    grad_resid = (
        upstream_own.astype(F32)
        + scale_ffn * scaled_ffn
        - resid * scale_ffn**3 * jnp.mean(scaled_ffn * resid, axis=1, keepdims=True)
    )
    grad_gain_ffn = jnp.sum(grad_normed_ffn * resid * scale_ffn, axis=0)
    grad_branch_own = grad_resid.astype(BF)
    overlap = jnp.sum(grad_branch_own.astype(F32) * branch_mix, axis=1)
    term_own = (scale_out[:, 0] ** 2 * overlap / width)[None]
    branch_stage = gather_first(grad_branch_own)
    term_near = grow(grow(term_own, 1), first_bit)
    hiddens = [[item[1][0] for item in firsts], [item[1][0] for item in seconds]]
    hiddens[1][2] = after(hiddens[1][2], grad_branch_own)
    odd_second = [(2, 0), (1, 0), (1, rows), (0, 0)]
    even_second = [(2, rows), (1, 2 * rows), (1, 3 * rows), (0, rows)]
    result_odd = result_call(
        hiddens, tuple(zip(odd_place, odd_second)), packed, rows, width
    )
    result_even = result_call(
        hiddens, tuple(zip(even_place, even_second)), packed, rows, width
    )
    branch_stage, result_even, result_odd, term_near = tied(
        branch_stage, tuple(result_even), tuple(result_odd), term_near
    )
    branch_far = gather_far(grad_branch_own, branch_stage)
    result_crossed = cross(result_odd)
    term_all = grow(term_near, second_bit)
    branch_far, result_crossed, term_all = tied(branch_far, result_crossed, term_all)
    result_stage = scatter_first(joints(result_even, result_crossed))
    term_all = slot_rows(term_all)
    branch_even = (grad_branch_own, *branch_stage, *branch_far)
    branch_odd = cross(branch_even)

    mix_pairs = [(s * planes + w, w * groups + s) for s in range(groups) for w in range(planes)]
    down_pairs = []
    for s in range(groups):
        for w in range(planes):
            owner = (w - s) % planes * (groups // planes) + s // planes
            down_pairs.append((s * planes + w, owner * planes + w))

    scattered = [scatter_packed(grads) for grads in ff_grads]

    def owned(part, count, pairs):
        lines = count * width // (planes * LANES)
        tiles = part[:lines].reshape(groups, -1, LANES)
        tiles = lax.all_to_all(tiles, "seq", split_axis=0, concat_axis=0, tiled=True)
        tiles = tiles.reshape(groups, count // LANES, -1, LANES)
        moved = lax.ppermute(part[lines:], ("seq", "wshard"), pairs)
        return tiles, moved.reshape(width // LANES, -1, LANES)

    shape_one = (groups, seqs, seq_dev, 1)
    (
        grad_even,
        grad_odd,
        scaled_even,
        scaled_odd,
        sum_bias,
        sum_theta,
        sum_gain,
        *backs,
    ) = mix_backward(
        place_one,
        floor,
        rec_packed,
        pre_even,
        pre_odd,
        flags,
        bias_own,
        theta_own,
        gain_own,
        state,
        scale_all.reshape(shape_one),
        term_all.reshape(shape_one),
        branch_even,
        branch_odd,
    )
    grad_even = grad_even.reshape(half * rows, 5 * chan)
    grad_odd = grad_odd.reshape(half * rows, 5 * chan)
    scaled_even = scaled_even.reshape(half * rows, 2 * chan)
    scaled_odd = scaled_odd.reshape(half * rows, 2 * chan)
    backs = tuple(item.reshape(rows, width) for item in backs)
    grad_even, result_stage, scattered = tied(grad_even, result_stage, scattered)
    rec_grads = gradients(
        [
            (normed_even, branch_even, grad_even, scaled_even),
            (normed_odd, branch_odd, grad_odd, scaled_odd),
        ],
        jnp.zeros((1,), jnp.int32),
    )
    back_even, back_odd = backs[:half], backs[half:]
    back_crossed = cross(back_odd)
    back_crossed, rec_grads = tied(back_crossed, rec_grads)
    back_far = scatter_far(back_even[3], back_crossed[3])
    branch_ffn = scatter_last(result_even, result_crossed, after(result_stage, rec_grads))
    back_far, branch_ffn = tied(back_far, branch_ffn)
    back_near = scatter_near(back_even[1:3], back_crossed[1:3], back_far)
    grad_normed_in = scatter_sum(back_even[0], back_crossed[0], back_near)
    _, *scattered = tied(back_near, *scattered)
    second_tiles, second_lines = owned(scattered[1], cols[1], down_pairs)
    rec_part = after(scatter_packed(rec_grads), second_tiles)
    rec_tiles, rec_lines = owned(rec_part, 5 * chan, mix_pairs)
    first_tiles, first_lines = owned(after(scattered[0], rec_tiles), cols[0], down_pairs)
    result = (resid + branch_ffn).astype(BF)
    scaled_in = grad_normed_in * gain_mix
    grad_tokens = (
        grad_resid
        + scale_in * scaled_in
        - resid_in * scale_in**3 * jnp.mean(scaled_in * resid_in, axis=1, keepdims=True)
    ).astype(BF)
    grad_gain_mix = jnp.sum(grad_normed_in * resid_in * scale_in, axis=0)

    hidden_all = w_ffgate.shape[1]
    rec_widths = (w_in.shape[1], w_forget.shape[1], w_gate_out.shape[1])
    grad_w_ffgate, grad_w_ffup = assemble_tiles(
        [first_tiles, second_tiles], shares, planes, (hidden_all, hidden_all)
    )
    grad_w_down = assemble_rows([first_lines, second_lines])
    grad_w_in, grad_w_forget, grad_w_gate = assemble_tiles([rec_tiles], (mix_run,), 0, rec_widths)
    grad_w_out = assemble_rows([rec_lines])

    def spread(part):
        count = part.shape[1] // mix_run
        zero = jnp.zeros((count, groups, mix_run), F32)
        zero = lax.dynamic_update_slice(zero, part.reshape(count, 1, mix_run), (0, place, 0))
        return zero.reshape(-1)

    pieces = [
        spread(sum_bias),
        spread(sum_theta),
        spread(sum_gain),
        grad_gain_ffn,
        grad_gain_mix,
        jnp.stack(
            [
                jnp.sum(resid_in * resid_in),
                jnp.sum(branch_mix * branch_mix),
                jnp.sum(branch_ffn * branch_ffn),
            ]
        ),
    ]
    sums = sum_seq(jnp.concatenate(pieces))
    sums = tied(rec_part, sums, *others(sums))[1:]
    sums = sum_tree(list(sums))
    cuts = []
    offset = 0
    for piece in pieces:
        cuts.append(sums[offset : offset + piece.shape[0]])
        offset += piece.shape[0]
    grad_bias, grad_theta, grad_gain_out, grad_gain_ffn, grad_gain_mix, squares = cuts
    rms_values = jnp.sqrt(squares / (rows * width * devices))
    return (
        result.reshape(seqs, seq_dev, width),
        grad_tokens.reshape(seqs, seq_dev, width),
        grad_gain_mix,
        grad_w_in,
        grad_w_forget,
        grad_bias,
        grad_theta,
        grad_w_gate,
        grad_gain_out,
        grad_w_out,
        grad_gain_ffn,
        grad_w_ffgate,
        grad_w_ffup,
        grad_w_down,
        rms_values,
    )


def solution(mesh):
    whole = P()
    rowed = P("wshard", None)
    stream = P("wshard", "seq", None)
    owned = P(("seq", "wshard"), None)
    return jax.shard_map(
        body,
        mesh=mesh,
        in_specs=(
            stream,
            rowed,
            whole,
            whole,
            rowed,
            rowed,
            whole,
            whole,
            rowed,
            whole,
            rowed,
            whole,
            rowed,
            rowed,
            rowed,
            stream,
        ),
        out_specs=(
            stream,
            stream,
            whole,
            owned,
            owned,
            whole,
            whole,
            owned,
            whole,
            owned,
            whole,
            owned,
            owned,
            owned,
            whole,
        ),
        check_vma=False,
    )
```

```python
import functools

import jax
import jax.numpy as jnp
from jax import lax
from jax.experimental import pallas as pl
from jax.experimental.pallas import tpu as pltpu
from jax.sharding import PartitionSpec as P

LAYERS = 24
EPS = 1e-06
BF = jnp.bfloat16
F32 = jnp.float32


def dot(left, right, form):
    return jnp.einsum(form, left, right, preferred_element_type=F32)


def swap(value, bit):
    size = lax.axis_size("seq")
    return lax.ppermute(value, "seq", [(i, i ^ bit) for i in range(size)])


def chip_bits():
    size = lax.axis_size("seq")
    return [1 << i for i in range(1, size.bit_length() - 1)]


def plain_even(own):
    bits = chip_bits()
    if len(bits) == 2:
        first, second = bits
        half = own.shape[0] // 2
        from_first = swap(own, first)
        from_second = swap(own, second)
        top = swap(from_first[:half], second)
        low = swap(from_second[half:], first)
        return jnp.concatenate([own, from_first, from_second, top, low], axis=0)
    held = own
    for bit in bits:
        held = jnp.concatenate([held, swap(held, bit)], axis=0)
    return held


def plain_gather(own):
    even = plain_even(own)
    return even, swap(even, 1)


def plain_scatter(even, odd):
    bits = chip_bits()
    joint = even.astype(F32) + swap(odd, 1).astype(F32)
    if len(bits) == 2:
        first, second = bits
        rows = joint.shape[0] // 4
        half = rows // 2
        low_joint = joint.astype(BF)
        near_first, near_second, far = (
            low_joint[rows : 2 * rows],
            low_joint[2 * rows : 3 * rows],
            low_joint[3 * rows :],
        )
        far_top = swap(far[:half], first)
        far_low = swap(far[half:], second)
        first_top = swap(near_first[:half], first)
        second_low = swap(near_second[half:], second)
        first_low = swap((near_first[half:].astype(F32) + far_low.astype(F32)).astype(BF), first)
        second_top = swap(
            (near_second[:half].astype(F32) + far_top.astype(F32)).astype(BF), second
        )
        first_all = jnp.concatenate([first_top, first_low], axis=0).astype(F32)
        second_all = jnp.concatenate([second_top, second_low], axis=0).astype(F32)
        return joint[:rows] + first_all + second_all
    for bit in reversed(bits):
        half = joint.shape[0] // 2
        joint = joint[:half] + swap(joint[half:].astype(BF), bit).astype(F32)
    return joint


def gather_first(own):
    return tuple(swap(own, bit) for bit in chip_bits())


def gather_far(own, stage):
    first, second = chip_bits()
    half = own.shape[0] // 2
    return swap(stage[0][:half], second), swap(stage[1][half:], first)


def cross(pieces):
    return tuple(swap(piece, 1) for piece in pieces)


def scatter_far(even, crossed):
    half = even.shape[0] // 2
    bits = chip_bits()
    return tuple(
        swap((even[rows].astype(F32) + crossed[rows].astype(F32)).astype(BF), bit)
        for rows, bit in zip((slice(0, half), slice(half, None)), bits)
    )


def onward_kernel(first_even, first_cross, far_low, second_even, second_cross, far_top, *outs):
    half = far_low.shape[0]
    first_out, second_out = outs
    both = first_even[...].astype(F32) + first_cross[...].astype(F32)
    first_out[:half, :] = both[:half].astype(BF)
    first_out[half:, :] = (both[half:] + far_low[...].astype(F32)).astype(BF)
    both = second_even[...].astype(F32) + second_cross[...].astype(F32)
    second_out[:half, :] = (both[:half] + far_top[...].astype(F32)).astype(BF)
    second_out[half:, :] = both[half:].astype(BF)


def near_sums(even, crossed, far):
    rows, width = even[0].shape
    step = width // 4
    whole = pl.BlockSpec((rows, step), lambda i: (0, i))
    part = pl.BlockSpec((rows // 2, step), lambda i: (0, i))
    return pl.pallas_call(
        onward_kernel,
        grid=(width // step,),
        in_specs=[whole, whole, part] * 2,
        out_specs=[whole] * 2,
        out_shape=[jax.ShapeDtypeStruct((rows, width), BF)] * 2,
        cost_estimate=SMALL,
        name="onward_sums",
    )(even[0], crossed[0], far[1], even[1], crossed[1], far[0])


def to_neighbours(sums):
    return tuple(swap(item, bit) for item, bit in zip(sums, chip_bits()))


def scatter_near(even, crossed, far):
    return to_neighbours(near_sums(even, crossed, far))


def joint_kernel(*refs):
    count = len(refs) // 3
    for index in range(count):
        both = refs[index][...].astype(F32) + refs[count + index][...].astype(F32)
        refs[2 * count + index][...] = both.astype(BF)


FIRST_SUMS = ((3, 0), (3, 1), (1, 0), (2, 1))


def joints(even, crossed):
    rows, width = even[0].shape
    half = rows // 2
    step = width // 4

    def spec(part):
        return pl.BlockSpec((half, step), lambda i, part=part: (part, i))

    return pl.pallas_call(
        joint_kernel,
        grid=(width // step,),
        in_specs=[spec(part) for _, part in FIRST_SUMS] * 2,
        out_specs=[spec(0)] * len(FIRST_SUMS),
        out_shape=[jax.ShapeDtypeStruct((half, width), BF)] * len(FIRST_SUMS),
        cost_estimate=SMALL,
        name="chip_sums",
    )(*[even[index] for index, _ in FIRST_SUMS], *[crossed[index] for index, _ in FIRST_SUMS])


def scatter_first(sums):
    first, second = chip_bits()
    return tuple(swap(item, bit) for item, bit in zip(sums, (first, second, first, second)))


def scatter_last(even, crossed, stage):
    first, second = chip_bits()
    half = even[0].shape[0] // 2
    far_top, far_low, first_top, second_low = stage

    def onward(index, rows, far):
        both = even[index][rows].astype(F32) + crossed[index][rows].astype(F32)
        return (both + far.astype(F32)).astype(BF)

    first_low = swap(onward(1, slice(half, None), far_low), first)
    second_top = swap(onward(2, slice(0, half), far_top), second)
    first_all = jnp.concatenate([first_top, first_low], axis=0).astype(F32)
    second_all = jnp.concatenate([second_top, second_low], axis=0).astype(F32)
    return even[0].astype(F32) + crossed[0].astype(F32) + first_all + second_all


def scatter_sum(even, crossed, near):
    return (even.astype(F32) + crossed.astype(F32)) + (near[0].astype(F32) + near[1].astype(F32))


def tied(*values):
    return lax.optimization_barrier(values)


def grow(held, bit):
    return jnp.concatenate([held, swap(held, bit)], axis=0)


def shrink(blocks, bit):
    half = blocks.shape[0] // 2
    return blocks[:half] + swap(blocks[half:], bit)


def slot_rows(held):
    pairs = held.reshape(held.shape[0] // 2, 2, -1)
    return pairs.transpose(1, 0, 2).reshape(held.shape)


def gather_small(own):
    for bit in [1] + chip_bits():
        own = grow(own, bit)
    return slot_rows(own)


def scatter_small(blocks):
    for bit in [1] + list(reversed(chip_bits())):
        blocks = shrink(blocks, bit)
    return blocks


def sum_seq(value):
    for bit in [1] + chip_bits():
        value = value + swap(value, bit)
    return value


def others(value):
    planes = lax.axis_size("wshard")
    return [
        lax.ppermute(value, "wshard", [(i, i ^ key) for i in range(planes)])
        for key in range(1, planes)
    ]


def sum_tree(values):
    while len(values) > 1:
        values = [values[i] + values[i + 1] for i in range(0, len(values), 2)]
    return values[0]


LANES = 128
SMALL = pl.CostEstimate(flops=1024, transcendentals=0, bytes_accessed=1024)


def filler(flops):
    return pl.CostEstimate(flops=flops, transcendentals=0, bytes_accessed=1024)


def pack(arrays):
    lines = []
    for array in arrays:
        count, rows, cols = array.shape
        split = array.reshape(count, rows, cols // LANES, LANES).transpose(0, 2, 1, 3)
        lines.append(split.reshape(count, rows * cols // LANES, LANES))
    return jnp.concatenate(lines, axis=1)


def gather_packed(packed):
    return lax.all_gather(packed, "wshard", axis=0, tiled=True)


def scatter_packed(packed):
    return lax.psum_scatter(
        packed.reshape(-1, LANES), "wshard", scatter_dimension=0, tiled=True
    )


def after(value, *others):
    return lax.optimization_barrier((value, others))[0]


def slot_of(place, group, groups):
    key = place ^ group
    return (key >> 1) + (key & 1) * (groups // 2)


def group_of(place, half, index):
    return place ^ ((index << 1) | half)


def token_rows(slot, tokens):
    return pl.ds(pl.multiple_of(slot * tokens, tokens), tokens)


def keep_of(pre, flag, bias, floor, chan):
    logit = (pre[:, 2 * chan : 3 * chan] + bias).astype(BF).astype(F32)
    sig = jax.nn.sigmoid(logit)
    return (floor + (1.0 - floor) * sig) * (1.0 - flag), sig


def forward_kernel(
    place_ref,
    floor_ref,
    pre_even,
    pre_odd,
    flag_ref,
    bias_ref,
    theta_ref,
    gain_ref,
    state_ref,
    gated_even,
    gated_odd,
    square_ref,
    keep_s,
    val_re,
    val_im,
    prod_re,
    prod_im,
    carry_re,
    carry_im,
):
    groups, _, tokens, _ = flag_ref.shape
    chan = keep_s.shape[1]
    half_groups = groups // 2
    floor = floor_ref[0]
    place = place_ref[0]
    cosine = jnp.cos(theta_ref[...])
    sine = jnp.sin(theta_ref[...])

    for half, pre_ref in ((0, pre_even), (1, pre_odd)):

        @pl.loop(0, half_groups)
        def _(index, half=half, pre_ref=pre_ref):
            slot = index + half * half_groups
            rows = token_rows(slot, tokens)
            pre = pre_ref[index, 0]
            keep, _ = keep_of(pre, flag_ref[slot, 0], bias_ref[...], floor, chan)
            keep_s[rows, :] = keep
            fresh = 1.0 - keep
            value = pre[:, :chan]
            val_re[rows, :] = fresh * (value * jax.nn.sigmoid(value)).astype(BF).astype(F32)
            value = pre[:, chan : 2 * chan]
            val_im[rows, :] = fresh * (value * jax.nn.sigmoid(value)).astype(BF).astype(F32)

    def step(t, carry):
        h_re, h_im, p_re, p_im = carry
        rows = pl.ds(t, groups, stride=tokens)
        held = keep_s[rows, :]
        a_re = held * cosine
        a_im = held * sine
        n_re = a_re * h_re - a_im * h_im + val_re[rows, :]
        n_im = a_re * h_im + a_im * h_re + val_im[rows, :]
        q_re = a_re * p_re - a_im * p_im
        q_im = a_re * p_im + a_im * p_re
        val_re[rows, :] = n_re
        val_im[rows, :] = n_im
        prod_re[rows, :] = q_re
        prod_im[rows, :] = q_im
        return n_re, n_im, q_re, q_im

    zero = jnp.zeros((groups, chan), F32)
    lax.fori_loop(0, tokens, step, (zero, zero, zero + 1.0, zero), unroll=8)

    def link(group, carry):
        c_re, c_im = carry
        slot = slot_of(place, group, groups)
        carry_re[pl.ds(slot, 1), :] = c_re
        carry_im[pl.ds(slot, 1), :] = c_im
        last = pl.ds(slot * tokens + tokens - 1, 1)
        p_re = prod_re[last, :]
        p_im = prod_im[last, :]
        return (
            p_re * c_re - p_im * c_im + val_re[last, :],
            p_re * c_im + p_im * c_re + val_im[last, :],
        )

    nought = jnp.zeros((1, chan), F32)
    lax.fori_loop(0, groups, link, (nought, nought))

    for half, pre_ref, gated_ref in ((0, pre_even, gated_even), (1, pre_odd, gated_odd)):

        @pl.loop(0, half_groups)
        def _(index, half=half, pre_ref=pre_ref, gated_ref=gated_ref):
            slot = index + half * half_groups
            rows = token_rows(slot, tokens)
            c_re = carry_re[pl.ds(slot, 1), :]
            c_im = carry_im[pl.ds(slot, 1), :]
            p_re = prod_re[rows, :]
            p_im = prod_im[rows, :]
            h_re = val_re[rows, :] + p_re * c_re - p_im * c_im
            h_im = val_im[rows, :] + p_re * c_im + p_im * c_re
            state_ref[slot, 0, :, :chan] = h_re
            state_ref[slot, 0, :, chan:] = h_im
            m_re = h_re.astype(BF).astype(F32)
            m_im = h_im.astype(BF).astype(F32)
            gate = jax.nn.sigmoid(pre_ref[index, 0, :, 3 * chan :]) * gain_ref[...]
            gated_ref[index, 0, :, :chan] = (m_re * gate[:, :chan]).astype(BF)
            gated_ref[index, 0, :, chan:] = (m_im * gate[:, chan:]).astype(BF)
            square_ref[slot, 0] = jnp.sum(m_re * m_re + m_im * m_im, axis=1, keepdims=True)


def backward_kernel(
    place_ref,
    floor_ref,
    pre_even,
    pre_odd,
    flag_ref,
    bias_ref,
    theta_ref,
    gain_ref,
    state_ref,
    up_even,
    up_odd,
    scale_ref,
    term_ref,
    out_even,
    out_odd,
    scaled_even,
    scaled_odd,
    sum_bias,
    sum_theta,
    sum_gain,
    keep_s,
    adj_re,
    adj_im,
    prod_re,
    prod_im,
    carry_re,
    carry_im,
    next_s,
):
    groups, _, tokens, _ = flag_ref.shape
    chan = keep_s.shape[1]
    half_groups = groups // 2
    floor = floor_ref[0]
    place = place_ref[0]
    cosine = jnp.cos(theta_ref[...])
    sine = jnp.sin(theta_ref[...])

    @pl.when(pl.program_id(0) == 0)
    def _():
        sum_bias[...] = jnp.zeros_like(sum_bias)
        sum_theta[...] = jnp.zeros_like(sum_theta)
        sum_gain[...] = jnp.zeros_like(sum_gain)

    for half, pre_ref, up_ref, out_ref, scaled_ref in (
        (0, pre_even, up_even, out_even, scaled_even),
        (1, pre_odd, up_odd, out_odd, scaled_odd),
    ):

        @pl.loop(0, half_groups)
        def _(
            index, half=half, pre_ref=pre_ref, up_ref=up_ref, out_ref=out_ref, scaled_ref=scaled_ref
        ):
            slot = index + half * half_groups
            rows = token_rows(slot, tokens)
            pre = pre_ref[index, 0]
            keep, _ = keep_of(pre, flag_ref[slot, 0], bias_ref[...], floor, chan)
            keep_s[rows, :] = keep
            scale = scale_ref[slot, 0]
            mixed = state_ref[slot, 0].astype(BF).astype(F32)
            sig = jax.nn.sigmoid(pre[:, 3 * chan :])
            inner = up_ref[index, 0] * sig
            scaled_ref[index, 0] = (mixed * gain_ref[...] * sig * scale).astype(BF)
            normed = inner * mixed * scale
            sum_gain[...] += jnp.sum(normed, axis=0, keepdims=True)
            out_ref[index, 0, :, 3 * chan :] = (normed * gain_ref[...] * (1.0 - sig)).astype(BF)
            grad = (scale * (inner * gain_ref[...]) - mixed * term_ref[slot, 0]).astype(BF)
            adj_re[rows, :] = grad[:, :chan].astype(F32)
            adj_im[rows, :] = grad[:, chan:].astype(F32)

    @pl.loop(0, groups)
    def _(group):
        slot = slot_of(place, group, groups)
        after = slot_of(place, lax.min(group + 1, groups - 1), groups)
        row = keep_s[pl.ds(after * tokens, 1), :]
        next_s[pl.ds(slot, 1), :] = jnp.where(group == groups - 1, 0.0, row)

    def turn(t, held, carry):
        g_re, g_im, p_re, p_im = carry
        rows = pl.ds(t, groups, stride=tokens)
        a_re = held * cosine
        a_im = held * sine
        n_re = a_re * g_re + a_im * g_im + adj_re[rows, :]
        n_im = a_re * g_im - a_im * g_re + adj_im[rows, :]
        q_re = a_re * p_re + a_im * p_im
        q_im = a_re * p_im - a_im * p_re
        adj_re[rows, :] = n_re
        adj_im[rows, :] = n_im
        prod_re[rows, :] = q_re
        prod_im[rows, :] = q_im
        return n_re, n_im, q_re, q_im

    def step(index, carry):
        t = tokens - 2 - index
        return turn(t, keep_s[pl.ds(t + 1, groups, stride=tokens), :], carry)

    zero = jnp.zeros((groups, chan), F32)
    carry = turn(tokens - 1, next_s[...], (zero, zero, zero + 1.0, zero))
    lax.fori_loop(0, tokens - 1, step, carry, unroll=4)

    def link(index, carry):
        c_re, c_im = carry
        slot = slot_of(place, groups - 1 - index, groups)
        carry_re[pl.ds(slot, 1), :] = c_re
        carry_im[pl.ds(slot, 1), :] = c_im
        first = pl.ds(slot * tokens, 1)
        p_re = prod_re[first, :]
        p_im = prod_im[first, :]
        return (
            p_re * c_re - p_im * c_im + adj_re[first, :],
            p_re * c_im + p_im * c_re + adj_im[first, :],
        )

    nought = jnp.zeros((1, chan), F32)
    lax.fori_loop(0, groups, link, (nought, nought))
    head = lax.broadcasted_iota(jnp.int32, (tokens, 2 * chan), 0) == 0

    for half, pre_ref, out_ref in ((0, pre_even, out_even), (1, pre_odd, out_odd)):

        @pl.loop(0, half_groups)
        def _(index, half=half, pre_ref=pre_ref, out_ref=out_ref):
            slot = index + half * half_groups
            rows = token_rows(slot, tokens)
            group = group_of(place, half, index)
            before = slot_of(place, lax.max(group - 1, 0), groups)
            tail = jnp.where(group == 0, 0.0, state_ref[before, 0, tokens - 1 :, :])
            prev = jnp.where(head, tail, pltpu.roll(state_ref[slot, 0], 1, 0))
            prev_re = prev[:, :chan]
            prev_im = prev[:, chan:]
            c_re = carry_re[pl.ds(slot, 1), :]
            c_im = carry_im[pl.ds(slot, 1), :]
            p_re = prod_re[rows, :]
            p_im = prod_im[rows, :]
            g_re = adj_re[rows, :] + p_re * c_re - p_im * c_im
            g_im = adj_im[rows, :] + p_re * c_im + p_im * c_re
            turn_re = cosine * prev_re - sine * prev_im
            turn_im = sine * prev_re + cosine * prev_im
            flag = flag_ref[slot, 0]
            pre = pre_ref[index, 0]
            keep, sig = keep_of(pre, flag, bias_ref[...], floor, chan)
            fresh = 1.0 - keep
            x_re = pre[:, :chan]
            x_im = pre[:, chan : 2 * chan]
            s_re = jax.nn.sigmoid(x_re)
            s_im = jax.nn.sigmoid(x_im)
            cand_re = (x_re * s_re).astype(BF).astype(F32)
            cand_im = (x_im * s_im).astype(BF).astype(F32)
            grad_keep = g_re * (turn_re - cand_re) + g_im * (turn_im - cand_im)
            sum_theta[...] -= jnp.sum(
                keep * (g_re * turn_im - g_im * turn_re), axis=0, keepdims=True
            )
            grad_forget = (
                grad_keep * (1.0 - flag) * ((1.0 - floor) * (sig * (1.0 - sig)))
            ).astype(BF)
            sum_bias[...] += jnp.sum(grad_forget.astype(F32), axis=0, keepdims=True)
            out_ref[index, 0, :, 2 * chan : 3 * chan] = grad_forget
            cand_grad = (fresh * g_re).astype(BF).astype(F32)
            out_ref[index, 0, :, :chan] = (
                cand_grad * s_re * (1.0 + x_re * (1.0 - s_re))
            ).astype(BF)
            cand_grad = (fresh * g_im).astype(BF).astype(F32)
            out_ref[index, 0, :, chan : 2 * chan] = (
                cand_grad * s_im * (1.0 + x_im * (1.0 - s_im))
            ).astype(BF)


def block_spec(groups, tokens, width):
    mode = pl.Buffered(1) if groups > 4 and width % 128 and width > 1 else None
    return pl.BlockSpec((groups, 1, tokens, width), lambda b: (0, b, 0, 0), pipeline_mode=mode)


def row_spec(width):
    return pl.BlockSpec((1, width), lambda b: (0, 0))


def recur_forward(place, floor, pre_even, pre_odd, flags, bias, theta, gain):
    groups, seqs, tokens, _ = flags.shape
    chan = bias.shape[1]
    half = groups // 2
    scalar = pl.BlockSpec(memory_space=pltpu.SMEM)
    rows = groups * tokens
    pre_spec = block_spec(half, tokens, 5 * chan)
    one = block_spec(groups, tokens, 1)
    gated = block_spec(half, tokens, 2 * chan)
    gated_shape = jax.ShapeDtypeStruct((half, seqs, tokens, 2 * chan), BF)
    size = seqs * rows * chan
    return pl.pallas_call(
        forward_kernel,
        grid=(seqs,),
        in_specs=[
            scalar,
            scalar,
            pre_spec,
            pre_spec,
            one,
            row_spec(chan),
            row_spec(chan),
            row_spec(2 * chan),
        ],
        out_specs=[block_spec(groups, tokens, 2 * chan), gated, gated, one],
        out_shape=[
            jax.ShapeDtypeStruct((groups, seqs, tokens, 2 * chan), F32),
            gated_shape,
            gated_shape,
            jax.ShapeDtypeStruct((groups, seqs, tokens, 1), F32),
        ],
        scratch_shapes=[pltpu.VMEM((rows, chan), F32)] * 5
        + [pltpu.VMEM((groups, chan), F32)] * 2,
        compiler_params=pltpu.CompilerParams(vmem_limit_bytes=56 * 2**20),
        cost_estimate=SMALL,
        name="recur_forward",
    )(place, floor, pre_even, pre_odd, flags, bias, theta, gain)


def recur_backward(
    place, floor, pre_even, pre_odd, flags, bias, theta, gain, state, up_even, up_odd, scale, term
):
    groups, seqs, tokens, _ = flags.shape
    chan = bias.shape[1]
    half = groups // 2
    scalar = pl.BlockSpec(memory_space=pltpu.SMEM)
    rows = groups * tokens
    pre_spec = block_spec(half, tokens, 5 * chan)
    one = block_spec(groups, tokens, 1)
    up_spec = block_spec(half, tokens, 2 * chan)
    out_shape = jax.ShapeDtypeStruct((half, seqs, tokens, 5 * chan), BF)
    scaled_shape = jax.ShapeDtypeStruct((half, seqs, tokens, 2 * chan), BF)
    size = seqs * rows * chan
    return pl.pallas_call(
        backward_kernel,
        grid=(seqs,),
        in_specs=[
            scalar,
            scalar,
            pre_spec,
            pre_spec,
            one,
            row_spec(chan),
            row_spec(chan),
            row_spec(2 * chan),
            block_spec(groups, tokens, 2 * chan),
            up_spec,
            up_spec,
            one,
            one,
        ],
        out_specs=[
            pre_spec,
            pre_spec,
            up_spec,
            up_spec,
            row_spec(chan),
            row_spec(chan),
            row_spec(2 * chan),
        ],
        out_shape=[
            out_shape,
            out_shape,
            scaled_shape,
            scaled_shape,
            jax.ShapeDtypeStruct((1, chan), F32),
            jax.ShapeDtypeStruct((1, chan), F32),
            jax.ShapeDtypeStruct((1, 2 * chan), F32),
        ],
        scratch_shapes=[pltpu.VMEM((rows, chan), F32)] * 5
        + [pltpu.VMEM((groups, chan), F32)] * 3,
        compiler_params=pltpu.CompilerParams(vmem_limit_bytes=56 * 2**20),
        cost_estimate=SMALL,
        name="recur_backward",
    )(
        place, floor, pre_even, pre_odd, flags, bias, theta, gain, state, up_even, up_odd, scale, term
    )


def unpack_columns(packed, out):
    planes = packed.shape[0]
    rows = out.shape[0] // planes
    for plane in range(planes):
        for tile in range(out.shape[1] // LANES):
            out[plane * rows : (plane + 1) * rows, tile * LANES : (tile + 1) * LANES] = packed[
                plane, tile * rows : (tile + 1) * rows, :
            ]


def unpack_rows(packed, first, out):
    planes = packed.shape[0]
    rows = out.shape[0] // planes
    for plane in range(planes):
        for tile in range(out.shape[1] // LANES):
            base = first + tile * rows
            out[plane * rows : (plane + 1) * rows, tile * LANES : (tile + 1) * LANES] = packed[
                plane, base : base + rows, :
            ]


def dot_nn(left, right):
    return jnp.dot(left, right, preferred_element_type=F32)


def dot_nt(left, right):
    return lax.dot_general(left, right, (((1,), (1,)), ((), ())), preferred_element_type=F32)


def dot_tn(left, right):
    return lax.dot_general(left, right, (((0,), (0,)), ((), ())), preferred_element_type=F32)


def dot_nn(left, right):
    return jnp.dot(left, right, preferred_element_type=F32)


def dot_nt(left, right):
    return lax.dot_general(left, right, (((1,), (1,)), ((), ())), preferred_element_type=F32)


def dot_tn(left, right):
    return lax.dot_general(left, right, (((0,), (0,)), ((), ())), preferred_element_type=F32)


PIECES = 5
ANYWHERE = pl.BlockSpec(memory_space=pl.ANY)
SCALAR = pl.BlockSpec(memory_space=pltpu.SMEM)


def block_copies(pieces, held, sems):
    copies = []
    index = 0
    for block, parts in enumerate(pieces):
        copies.append([])
        rows = held.shape[1] // len(parts)
        for part, (ref, offset) in enumerate(parts):
            source = ref if offset is None else ref.at[offset : offset + rows]
            target = held.at[block, part * rows : (part + 1) * rows]
            copies[-1].append(pltpu.make_async_copy(source, target, sems.at[index]))
            index += 1
    return copies


def ffn_kernel(counts, offsets, last, *refs):
    refs = list(refs)

    def take(count):
        taken = refs[:count]
        del refs[:count]
        return taken

    (packed_ref,) = take(1)
    blocks = len(counts)
    normed = [[(ref, None) for ref in take(count)] for count in counts]
    up = [[(ref, None) for ref in take(count)] for count in counts]
    groups = [normed, up]
    if offsets:
        groups.append([[(ref, offset)] for ref, offset in zip(take(blocks), offsets)])
    hidden_ref, grad_ref = take(2)
    backs = take(blocks if last else 1)
    ff_s, down_s = take(2)
    helds = take(len(groups))
    sems = take(len(groups))
    copies = [block_copies(*item) for item in zip(groups, helds, sems)]
    hidden = down_s.shape[0]
    step = pl.program_id(0)

    @pl.when(step == 0)
    def _():
        for block in range(blocks):
            for group in copies:
                for copy in group[block]:
                    copy.start()
        first = ff_s.shape[0] // packed_ref.shape[0] * (ff_s.shape[1] // LANES)
        unpack_columns(packed_ref, ff_s)
        unpack_rows(packed_ref, first, down_s)

    for block in range(blocks):

        @pl.when(step == block)
        def _(block=block):
            for group in copies:
                for copy in group[block]:
                    copy.wait()

    ff = dot_nn(helds[0][step], ff_s[...])
    gate, value = ff[:, :hidden], ff[:, hidden:]
    sig = jax.nn.sigmoid(gate)
    silu = gate * sig
    hidden_ref[...] = (silu * value).astype(BF)
    grad = dot_nt(helds[1][step], down_s[...])
    grad_ref[:, :hidden] = (grad * value * sig * (1.0 + gate * (1.0 - sig))).astype(BF)
    grad_ref[:, hidden:] = (grad * silu).astype(BF)
    back = dot_nt(grad_ref[...], ff_s[...])
    if offsets:
        back = back + helds[2][step]
    if last:
        for block in range(blocks):

            @pl.when(step == block)
            def _(block=block):
                backs[block][...] = back.astype(BF)
    else:
        backs[0][...] = back


def ffn_call(blocks, packed, ff_cols, bases=None, fills=False):
    rows = sum(piece.shape[0] for piece in blocks[0][0])
    width = blocks[0][0][0].shape[1]
    count = len(blocks)
    tokens = count * rows
    hidden = ff_cols // 2
    last = bases is not None
    counts = tuple(len(block[0]) for block in blocks)
    pieces = sum(counts)
    operands = [packed]
    for index in range(2):
        for block in blocks:
            operands += block[index]
    held = pltpu.VMEM((count, rows, width), BF)
    helds = [held, held]
    sems = [pltpu.SemaphoreType.DMA((pieces,))] * 2
    if last:
        operands += [array for array, _ in bases]
        helds.append(pltpu.VMEM((count, rows, width), F32))
        sems.append(pltpu.SemaphoreType.DMA((count,)))
    backs = [jax.ShapeDtypeStruct((tokens, width), F32)]
    back_specs = [pl.BlockSpec((rows, width), lambda i: (i, 0))]
    if last:
        backs = [jax.ShapeDtypeStruct((rows, width), BF)] * count
        back_specs = [pl.BlockSpec((rows, width), lambda i: (0, 0))] * count
    offsets = tuple(offset for _, offset in bases) if last else ()
    return pl.pallas_call(
        functools.partial(ffn_kernel, counts, offsets, last),
        grid=(count,),
        in_specs=[pl.BlockSpec(packed.shape, lambda i: (0, 0, 0), pipeline_mode=pl.Buffered(1))]
        + [ANYWHERE] * (len(operands) - 1),
        out_specs=[
            pl.BlockSpec((rows, hidden), lambda i: (i, 0)),
            pl.BlockSpec((rows, ff_cols), lambda i: (i, 0)),
        ]
        + back_specs,
        out_shape=[
            jax.ShapeDtypeStruct((tokens, hidden), BF),
            jax.ShapeDtypeStruct((tokens, ff_cols), BF),
            *backs,
        ],
        scratch_shapes=[pltpu.VMEM((width, ff_cols), BF), pltpu.VMEM((hidden, width), BF)]
        + helds
        + sems,
        compiler_params=pltpu.CompilerParams(vmem_limit_bytes=60 * 2**20),
        cost_estimate=filler(5 * tokens * width * ff_cols if fills else 1024),
        name="ffn",
    )(*operands)


def grads_kernel(planes, owners, counts, turn_ref, *refs):
    refs = list(refs)
    out_ref = refs.pop()

    def take(count):
        taken = refs[:count]
        del refs[:count]
        return taken

    groups = [(take(count), take(count), *take(2)) for count in counts]
    step = pl.program_id(0)
    steps = pl.num_programs(0)
    block = groups[0][0][0].shape[1]
    subs = owners // steps
    run = block // subs // planes
    tiles = groups[0][2].shape[1] // LANES
    count = groups[0][3].shape[1] // planes

    def joined(pieces):
        return jnp.concatenate([piece[...] for piece in pieces], axis=0)

    grad = sum(dot_tn(joined(left), cols[...]) for left, _, cols, _ in groups).astype(BF)
    for sub in range(subs):
        for plane in range(planes):
            first = (sub * planes + plane) * run
            for tile in range(tiles):
                base = ((step * subs + sub) * tiles + tile) * run
                lines = pl.ds(pl.multiple_of(base, 16), run)
                out_ref[plane, lines, :] = grad[
                    first : first + run, tile * LANES : (tile + 1) * LANES
                ]
    grad = sum(dot_tn(rows[...], joined(up)) for _, up, _, rows in groups).astype(BF)
    first = run * tiles * owners
    for index in range(planes):
        plane = lax.rem(turn_ref[0] + index, planes)
        for tile in range(block // LANES):
            base = first + (step * (block // LANES) + tile) * count
            lines = pl.ds(pl.multiple_of(base, 16), count)
            out_ref[plane, lines, :] = grad[
                index * count : (index + 1) * count, tile * LANES : (tile + 1) * LANES
            ]


def grads_call(owners, planes, turn, groups):
    width = groups[0][0][0].shape[1]
    steps = owners // 2
    block = width // steps
    col_count = groups[0][2].shape[1]
    row_count = groups[0][3].shape[1]
    tokens = sum(group[2].shape[0] for group in groups)
    lines = (col_count * width + row_count * width) // (planes * LANES)
    operands, specs = [turn], [SCALAR]
    for left, up, cols, rows in groups:
        for piece in (*left, *up):
            operands.append(piece)
            specs.append(pl.BlockSpec((piece.shape[0], block), lambda i: (0, i)))
        for array in (cols, rows):
            operands.append(array)
            specs.append(
                pl.BlockSpec(array.shape, lambda i: (0, 0), pipeline_mode=pl.Buffered(1))
            )
    return pl.pallas_call(
        functools.partial(
            grads_kernel, planes, owners, tuple(len(group[0]) for group in groups)
        ),
        grid=(steps,),
        in_specs=specs,
        out_specs=pl.BlockSpec((planes, lines, LANES), lambda i: (0, 0, 0)),
        out_shape=jax.ShapeDtypeStruct((planes, lines, LANES), BF),
        compiler_params=pltpu.CompilerParams(vmem_limit_bytes=60 * 2**20),
        cost_estimate=filler(4 * tokens * width * (col_count + row_count)),
        name="weight_grads",
    )(*operands)


def result_kernel(firsts, places, counts, *refs):
    hiddens = (refs[: counts[0]], refs[counts[0] : sum(counts)])
    refs = refs[sum(counts) :]
    outs, down_s = refs[2:-1], refs[-1]
    step = pl.program_id(0)
    first_rows = hiddens[0][0].shape[1]

    @pl.when(step == 0)
    def _():
        unpack_rows(refs[0], firsts[0], down_s.at[:first_rows])
        unpack_rows(refs[1], firsts[1], down_s.at[first_rows:])

    for slot, out in enumerate(outs):

        @pl.when(step == slot)
        def _(slot=slot, out=out):
            rows = out.shape[0]
            parts = []
            for arrays, (index, offset) in zip(hiddens, places[slot]):
                parts.append(arrays[index][offset : offset + rows, :])
            total = dot_nn(parts[0], down_s[:first_rows, :])
            total = total + dot_nn(parts[1], down_s[first_rows:, :])
            out[...] = total.astype(BF)


def result_call(hiddens, places, packed, rows, width):
    slots = len(places)
    total = hiddens[0][0].shape[1] + hiddens[1][0].shape[1]
    firsts = tuple(
        part.shape[1] - arrays[0].shape[1] // part.shape[0] * width // LANES
        for part, arrays in zip(packed, hiddens)
    )
    arrays = [*hiddens[0], *hiddens[1]]

    def whole(array):
        zeros = (0,) * array.ndim
        return pl.BlockSpec(array.shape, lambda i: zeros, pipeline_mode=pl.Buffered(1))

    return pl.pallas_call(
        functools.partial(
            result_kernel, firsts, places, (len(hiddens[0]), len(hiddens[1]))
        ),
        grid=(slots,),
        in_specs=[whole(array) for array in arrays] + [whole(part) for part in packed],
        out_specs=[pl.BlockSpec((rows, width), lambda i: (0, 0))] * slots,
        out_shape=[jax.ShapeDtypeStruct((rows, width), BF)] * slots,
        scratch_shapes=[pltpu.VMEM((total, width), BF)],
        compiler_params=pltpu.CompilerParams(vmem_limit_bytes=48 * 2**20),
        cost_estimate=filler(2 * slots * rows * width * total),
        name="ffn_result",
    )(*arrays, *packed)


def seq_copies(pieces, held, sems, seq):
    tokens = held.shape[2]
    rows = slice(seq * tokens, (seq + 1) * tokens)
    copies = [
        pltpu.make_async_copy(pieces[slot].at[rows], held.at[seq, slot], sems.at[seq, slot])
        for slot in range(3)
    ]
    copies.append(pltpu.make_async_copy(pieces[3 + seq], held.at[seq, 3], sems.at[seq, 3]))
    return copies


def fetch(groups):
    seqs = groups[0][1].shape[0]

    @pl.when(pl.program_id(0) == 0)
    def _():
        for seq in range(seqs):
            for pieces, held, sems in groups:
                for copy in seq_copies(pieces, held, sems, seq):
                    copy.start()


def arrive(groups):
    for seq in range(groups[0][1].shape[0]):

        @pl.when(pl.program_id(0) == seq)
        def _(seq=seq):
            for pieces, held, sems in groups:
                for copy in seq_copies(pieces, held, sems, seq):
                    copy.wait()


def unpack_mix(packed_ref, rec_s, out_s):
    @pl.when(pl.program_id(0) == 0)
    def _():
        lines = rec_s.shape[0] // packed_ref.shape[0] * (rec_s.shape[1] // LANES)
        unpack_columns(packed_ref, rec_s)
        unpack_rows(packed_ref, lines, out_s)


def mix_forward_kernel(*refs):
    place_ref, floor_ref, packed_ref, flag_ref, bias_ref, theta_ref, gain_ref = refs[:7]
    refs = refs[7:]
    even, odd = refs[:PIECES], refs[PIECES : 2 * PIECES]
    refs = refs[2 * PIECES :]
    pre_even, pre_odd, state_ref, square_ref = refs[:4]
    mix_even, mix_odd = refs[4:8], refs[8:12]
    rec_s, out_s, gated_even, gated_odd, x_even, x_odd, sems_even, sems_odd = refs[12:20]
    scratch = refs[20:]
    half, _, tokens, _ = pre_even.shape
    seq = pl.program_id(0)
    groups = ((even, x_even, sems_even), (odd, x_odd, sems_odd))
    fetch(groups)
    unpack_mix(packed_ref, rec_s, out_s)
    arrive(groups)
    for x_ref, pre_ref in ((x_even, pre_even), (x_odd, pre_odd)):

        @pl.loop(0, half, step=2)
        def _(index, x_ref=x_ref, pre_ref=pre_ref):
            pair = pl.ds(index, 2)
            x = x_ref[seq, pair].reshape(2 * tokens, -1)
            pre_ref[pair, 0] = dot_nn(x, rec_s[...]).reshape(2, tokens, -1)

    forward_kernel(
        place_ref,
        floor_ref,
        pre_even,
        pre_odd,
        flag_ref,
        bias_ref,
        theta_ref,
        gain_ref,
        state_ref,
        gated_even,
        gated_odd,
        square_ref,
        *scratch,
    )
    for gated_ref, mixes in ((gated_odd, mix_odd), (gated_even, mix_even)):
        for index in range(0, half, 2):
            gated = gated_ref[index : index + 2, 0].reshape(2 * tokens, -1)
            mix = dot_nn(gated, out_s[...]).astype(BF)
            mixes[index][0] = mix[:tokens]
            mixes[index + 1][0] = mix[tokens:]


def mix_forward(place, floor, even, odd, packed, flags, bias, theta, gain):
    groups, seqs, tokens, _ = flags.shape
    chan = bias.shape[1]
    half = groups // 2
    width = even[0].shape[-1]
    rows = groups * tokens
    pre_spec = block_spec(half, tokens, 5 * chan)
    one = block_spec(groups, tokens, 1)
    pre_shape = jax.ShapeDtypeStruct((half, seqs, tokens, 5 * chan), F32)
    mix_spec = pl.BlockSpec((1, tokens, width), lambda b: (b, 0, 0))
    mix_shape = jax.ShapeDtypeStruct((seqs, tokens, width), BF)
    gated = pltpu.VMEM((half, 1, tokens, 2 * chan), BF)
    held = pltpu.VMEM((seqs, half, tokens, width), BF)
    sems = pltpu.SemaphoreType.DMA((seqs, half))
    return pl.pallas_call(
        mix_forward_kernel,
        grid=(seqs,),
        in_specs=[
            SCALAR,
            SCALAR,
            pl.BlockSpec(packed.shape, lambda b: (0, 0, 0), pipeline_mode=pl.Buffered(1)),
            one,
            row_spec(chan),
            row_spec(chan),
            row_spec(2 * chan),
        ]
        + [ANYWHERE] * (2 * PIECES),
        out_specs=[pre_spec, pre_spec, block_spec(groups, tokens, 2 * chan), one]
        + [mix_spec] * (2 * half),
        out_shape=[
            pre_shape,
            pre_shape,
            jax.ShapeDtypeStruct((groups, seqs, tokens, 2 * chan), F32),
            jax.ShapeDtypeStruct((groups, seqs, tokens, 1), F32),
        ]
        + [mix_shape] * (2 * half),
        scratch_shapes=[
            pltpu.VMEM((width, 5 * chan), BF),
            pltpu.VMEM((2 * chan, width), BF),
            gated,
            gated,
            held,
            held,
            sems,
            sems,
        ]
        + [pltpu.VMEM((rows, chan), F32)] * 5
        + [pltpu.VMEM((groups, chan), F32)] * 2,
        compiler_params=pltpu.CompilerParams(vmem_limit_bytes=60 * 2**20),
        cost_estimate=SMALL,
        name="mix_forward",
    )(place, floor, packed, flags, bias, theta, gain, *even, *odd)


def mix_backward_kernel(*refs):
    place_ref, floor_ref, packed_ref = refs[:3]
    pre_even, pre_odd, flag_ref, bias_ref, theta_ref, gain_ref, state_ref = refs[3:10]
    scale_ref, term_ref = refs[10:12]
    refs = refs[12:]
    even, odd = refs[:PIECES], refs[PIECES : 2 * PIECES]
    refs = refs[2 * PIECES :]
    out_even, out_odd, scaled_even, scaled_odd, sum_bias, sum_theta, sum_gain = refs[:7]
    back_even, back_odd = refs[7:11], refs[11:15]
    rec_s, out_s, up_even, up_odd, x_even, x_odd, sems_even, sems_odd = refs[15:23]
    scratch = refs[23:]
    half, _, tokens, _ = pre_even.shape
    seq = pl.program_id(0)
    groups = ((even, x_even, sems_even), (odd, x_odd, sems_odd))
    fetch(groups)
    unpack_mix(packed_ref, rec_s, out_s)
    arrive(groups)
    for x_ref, up_ref in ((x_even, up_even), (x_odd, up_odd)):

        @pl.loop(0, half, step=2)
        def _(index, x_ref=x_ref, up_ref=up_ref):
            pair = pl.ds(index, 2)
            branch = x_ref[seq, pair].reshape(2 * tokens, -1)
            up_ref[pair, 0] = dot_nt(branch, out_s[...]).reshape(2, tokens, -1)

    backward_kernel(
        place_ref,
        floor_ref,
        pre_even,
        pre_odd,
        flag_ref,
        bias_ref,
        theta_ref,
        gain_ref,
        state_ref,
        up_even,
        up_odd,
        scale_ref,
        term_ref,
        out_even,
        out_odd,
        scaled_even,
        scaled_odd,
        sum_bias,
        sum_theta,
        sum_gain,
        *scratch,
    )
    for out_ref, backs in ((out_odd, back_odd), (out_even, back_even)):
        for index in range(0, half, 2):
            grad = out_ref[index : index + 2, 0].reshape(2 * tokens, -1)
            back = dot_nt(grad, rec_s[...]).astype(BF)
            backs[index][0] = back[:tokens]
            backs[index + 1][0] = back[tokens:]


def mix_backward(
    place, floor, packed, pre_even, pre_odd, flags, bias, theta, gain, state, scale, term,
    even, odd,
):
    groups, seqs, tokens, _ = flags.shape
    chan = bias.shape[1]
    half = groups // 2
    width = even[0].shape[-1]
    rows = groups * tokens
    pre_spec = block_spec(half, tokens, 5 * chan)
    one = block_spec(groups, tokens, 1)
    pair_spec = block_spec(half, tokens, 2 * chan)
    back_spec = pl.BlockSpec((1, tokens, width), lambda b: (b, 0, 0))
    pre_shape = jax.ShapeDtypeStruct((half, seqs, tokens, 5 * chan), BF)
    pair_shape = jax.ShapeDtypeStruct((half, seqs, tokens, 2 * chan), BF)
    up = pltpu.VMEM((half, 1, tokens, 2 * chan), F32)
    held = pltpu.VMEM((seqs, half, tokens, width), BF)
    sems = pltpu.SemaphoreType.DMA((seqs, half))
    return pl.pallas_call(
        mix_backward_kernel,
        grid=(seqs,),
        in_specs=[
            SCALAR,
            SCALAR,
            pl.BlockSpec(packed.shape, lambda b: (0, 0, 0), pipeline_mode=pl.Buffered(1)),
            pre_spec,
            pre_spec,
            one,
            row_spec(chan),
            row_spec(chan),
            row_spec(2 * chan),
            block_spec(groups, tokens, 2 * chan),
            one,
            one,
        ]
        + [ANYWHERE] * (2 * PIECES),
        out_specs=[
            pre_spec,
            pre_spec,
            pair_spec,
            pair_spec,
            row_spec(chan),
            row_spec(chan),
            row_spec(2 * chan),
        ]
        + [back_spec] * (2 * half),
        out_shape=[
            pre_shape,
            pre_shape,
            pair_shape,
            pair_shape,
            jax.ShapeDtypeStruct((1, chan), F32),
            jax.ShapeDtypeStruct((1, chan), F32),
            jax.ShapeDtypeStruct((1, 2 * chan), F32),
        ]
        + [jax.ShapeDtypeStruct((seqs, tokens, width), BF)] * (2 * half),
        scratch_shapes=[
            pltpu.VMEM((width, 5 * chan), BF),
            pltpu.VMEM((2 * chan, width), BF),
            up,
            up,
            held,
            held,
            sems,
            sems,
        ]
        + [pltpu.VMEM((rows, chan), F32)] * 5
        + [pltpu.VMEM((groups, chan), F32)] * 3,
        compiler_params=pltpu.CompilerParams(vmem_limit_bytes=60 * 2**20),
        cost_estimate=SMALL,
        name="mix_backward",
    )(
        place, floor, packed, pre_even, pre_odd, flags, bias, theta, gain, state, scale,
        term, *even, *odd,
    )


def assemble_tiles_kernel(shares, planes, *refs):
    sources, outs = refs[: len(shares)], refs[len(shares) :]
    groups = sources[0].shape[0]
    run = sum(shares)
    for group in range(groups):
        wides = [
            jnp.concatenate(
                [source[group, tile].astype(F32) for tile in range(source.shape[1])], axis=1
            )
            for source in sources
        ]
        firsts = [0] * len(shares)
        for out in outs:
            for block in range(out.shape[1] // (groups * run)):
                where = group
                if planes:
                    where = (block + group) % planes + planes * (group // planes)
                base = (block * groups + where) * run
                for index, share in enumerate(shares):
                    first = firsts[index]
                    out[:, base : base + share] = wides[index][:, first : first + share]
                    firsts[index] += share
                    base += share


def assemble_tiles(parts, shares, planes, widths):
    rows = parts[0].shape[2]
    return pl.pallas_call(
        functools.partial(assemble_tiles_kernel, shares, planes),
        out_shape=[jax.ShapeDtypeStruct((rows, width), F32) for width in widths],
        compiler_params=pltpu.CompilerParams(vmem_limit_bytes=48 * 2**20),
        cost_estimate=SMALL,
        name="assemble_columns",
    )(*parts)


def assemble_rows_kernel(*refs):
    out = refs[-1]
    base = 0
    for source in refs[:-1]:
        tiles, rows, _ = source.shape
        for tile in range(tiles):
            out[base : base + rows, tile * LANES : (tile + 1) * LANES] = source[tile].astype(F32)
        base += rows


def assemble_rows(parts):
    rows = sum(part.shape[1] for part in parts)
    width = parts[0].shape[0] * LANES
    return pl.pallas_call(
        assemble_rows_kernel,
        out_shape=jax.ShapeDtypeStruct((rows, width), F32),
        compiler_params=pltpu.CompilerParams(vmem_limit_bytes=48 * 2**20),
        cost_estimate=SMALL,
        name="assemble_rows",
    )(*parts)


def shard_gather(value):
    return lax.all_gather(value, "wshard", axis=0, tiled=True)


def shard_scatter(value):
    return lax.psum_scatter(value, "wshard", scatter_dimension=0, tiled=True)


def plain_body(
    tokens,
    starts,
    layer_index,
    gain_mix,
    w_in,
    w_forget,
    bias_forget,
    theta,
    w_gate_out,
    gain_out,
    w_out,
    gain_ffn,
    w_ffgate,
    w_ffup,
    w_down,
    out_grad,
):
    seqs, seq_dev, width = tokens.shape
    rows = seqs * seq_dev
    groups = lax.axis_size("seq")
    planes = lax.axis_size("wshard")
    half = groups // 2
    devices = groups * planes
    place = lax.axis_index("seq")
    floor = layer_index.astype(F32) / LAYERS
    mix_run = w_out.shape[0] // groups
    ffn_run = w_down.shape[0] // groups
    chan = mix_run * planes // 2
    hidden = ffn_run * planes

    def own_columns(array, run):
        count = array.shape[1] // (run * groups)
        column = lax.broadcasted_iota(jnp.int32, (array.shape[1], count * run), 0)
        index = lax.broadcasted_iota(jnp.int32, (array.shape[1], count * run), 1)
        block = index // run
        chosen = column == block * (run * groups) + place * run + (index - block * run)
        return dot(array, chosen.astype(BF), "rc,cj->rj").astype(BF)

    def own_parts(vector):
        count = vector.shape[0] // (mix_run * groups)
        split = vector.reshape(count, groups, mix_run)
        return lax.dynamic_slice_in_dim(split, place, 1, 1).reshape(1, count * mix_run)

    def own_rows(array):
        run = array.shape[0] // groups
        return lax.dynamic_slice_in_dim(array, place * run, run, 0)

    resid_in = tokens.reshape(rows, width).astype(F32)
    scale_in = lax.rsqrt(jnp.mean(resid_in * resid_in, axis=1, keepdims=True) + EPS)
    normed_own = (resid_in * scale_in * gain_mix).astype(BF)
    normed_even, normed_odd = plain_gather(normed_own)
    upstream_own = out_grad.reshape(rows, width)

    rec_w = shard_gather(
        jnp.concatenate(
            [
                own_columns(w_in, mix_run),
                own_columns(w_forget, mix_run),
                own_columns(w_gate_out, mix_run),
            ],
            axis=1,
        )
    )
    out_w = shard_gather(own_rows(w_out))
    ff_w = shard_gather(
        jnp.concatenate([own_columns(w_ffgate, ffn_run), own_columns(w_ffup, ffn_run)], axis=1)
    )
    down_w = shard_gather(own_rows(w_down))

    slots = lax.broadcasted_iota(jnp.int32, (groups, groups), 0)
    sources = lax.broadcasted_iota(jnp.int32, (groups, groups), 1)
    keys = jnp.where(slots < half, 2 * slots, 2 * (slots - half) + 1)
    chosen = ((place ^ keys) == sources).astype(F32)
    marks = starts.astype(F32).reshape(seqs, groups, seq_dev).transpose(1, 0, 2)
    flags = jnp.sum(chosen[:, :, None, None] * marks[None], axis=1)[..., None]
    bias_own = own_parts(bias_forget)
    theta_own = own_parts(theta)
    gain_own = own_parts(gain_out)
    place_one = place.reshape(1)

    def blocks(array):
        return array.reshape(half, seqs, seq_dev, -1)

    pre_even = blocks(dot(normed_even, rec_w, "td,dc->tc"))
    pre_odd = blocks(dot(normed_odd, rec_w, "td,dc->tc"))
    state, gated_even, gated_odd, square = recur_forward(
        place_one, floor, pre_even, pre_odd, flags, bias_own, theta_own, gain_own
    )
    gated_even = gated_even.reshape(half * rows, 2 * chan)
    gated_odd = gated_odd.reshape(half * rows, 2 * chan)

    def mix(gated):
        return dot(gated, out_w, "tc,cd->td").astype(BF)

    square_own = scatter_small(square.reshape(groups, rows))
    scale_own = lax.rsqrt(square_own / width + EPS)
    scale_out = scale_own.reshape(rows, 1)
    branch_mix = scale_out * plain_scatter(mix(gated_even), mix(gated_odd))
    resid = resid_in + branch_mix
    scale_ffn = lax.rsqrt(jnp.mean(resid * resid, axis=1, keepdims=True) + EPS)
    ffn_even, ffn_odd = plain_gather((resid * scale_ffn * gain_ffn).astype(BF))
    scale_all = gather_small(scale_own)
    up_even, up_odd = plain_gather(upstream_own)

    def ffn(normed, upstream):
        ff = dot(normed, ff_w, "td,df->tf")
        ffn_gate, ffn_up = ff[:, :hidden], ff[:, hidden:]
        sig_ffn = jax.nn.sigmoid(ffn_gate)
        silu_ffn = ffn_gate * sig_ffn
        ffn_hidden = (silu_ffn * ffn_up).astype(BF)
        grad_hidden = dot(upstream, down_w, "td,fd->tf")
        grad_gate = grad_hidden * ffn_up * sig_ffn * (1.0 + ffn_gate * (1.0 - sig_ffn))
        grad_up = grad_hidden * silu_ffn
        grad_ff = jnp.concatenate([grad_gate.astype(BF), grad_up.astype(BF)], axis=1)
        return ffn_hidden, grad_ff

    hidden_odd, grad_ff_odd = ffn(ffn_odd, up_odd)
    hidden_even, grad_ff_even = ffn(ffn_even, up_even)
    grad_normed_ffn = plain_scatter(
        dot(grad_ff_even, ff_w, "tf,df->td").astype(BF),
        dot(grad_ff_odd, ff_w, "tf,df->td").astype(BF),
    )
    branch_ffn = plain_scatter(
        dot(hidden_even, down_w, "tf,fd->td").astype(BF),
        dot(hidden_odd, down_w, "tf,fd->td").astype(BF),
    )
    result = (resid + branch_ffn).astype(BF)

    scaled_ffn = grad_normed_ffn * gain_ffn
    grad_resid = (
        upstream_own.astype(F32)
        + scale_ffn * scaled_ffn
        - resid * scale_ffn**3 * jnp.mean(scaled_ffn * resid, axis=1, keepdims=True)
    )
    grad_gain_ffn = jnp.sum(grad_normed_ffn * resid * scale_ffn, axis=0)
    grad_branch_own = grad_resid.astype(BF)
    overlap = jnp.sum(grad_branch_own.astype(F32) * branch_mix, axis=1)
    term_all = gather_small((scale_out[:, 0] ** 2 * overlap / width)[None])
    branch_even, branch_odd = plain_gather(grad_branch_own)
    grad_gated_even = blocks(dot(branch_even, out_w, "td,cd->tc"))
    grad_gated_odd = blocks(dot(branch_odd, out_w, "td,cd->tc"))

    shape_one = (groups, seqs, seq_dev, 1)
    grad_even, grad_odd, scaled_even, scaled_odd, sum_bias, sum_theta, sum_gain = recur_backward(
        place_one,
        floor,
        pre_even,
        pre_odd,
        flags,
        bias_own,
        theta_own,
        gain_own,
        state,
        grad_gated_even,
        grad_gated_odd,
        scale_all.reshape(shape_one),
        term_all.reshape(shape_one),
    )
    grad_even = grad_even.reshape(half * rows, 5 * chan)
    grad_odd = grad_odd.reshape(half * rows, 5 * chan)
    grad_normed_in = plain_scatter(
        dot(grad_even, rec_w, "tc,dc->td").astype(BF),
        dot(grad_odd, rec_w, "tc,dc->td").astype(BF),
    )
    scaled_in = grad_normed_in * gain_mix
    grad_tokens = (
        grad_resid
        + scale_in * scaled_in
        - resid_in * scale_in**3 * jnp.mean(scaled_in * resid_in, axis=1, keepdims=True)
    ).astype(BF)
    grad_gain_mix = jnp.sum(grad_normed_in * resid_in * scale_in, axis=0)

    def pair_dot(left, right, form):
        return dot(left[0], right[0], form) + dot(left[1], right[1], form)

    def to_owner(grad):
        run = grad.shape[0] // devices
        part = grad.astype(BF).reshape(groups, planes, run, -1).transpose(1, 0, 2, 3)
        part = shard_scatter(part.reshape(grad.shape)).reshape(groups, run, -1)
        return lax.all_to_all(part, "seq", split_axis=0, concat_axis=0, tiled=True)

    def columns(part, run):
        source, count, cols = part.shape
        split = part.reshape(source, count, cols // run, run)
        return split.transpose(1, 2, 0, 3).reshape(count, -1).astype(F32)

    scaled_even = scaled_even.reshape(half * rows, 2 * chan)
    scaled_odd = scaled_odd.reshape(half * rows, 2 * chan)
    ff_grad = to_owner(
        pair_dot((ffn_even, ffn_odd), (grad_ff_even, grad_ff_odd), "td,tf->df")
    )
    grad_w_ffgate = columns(ff_grad[..., :hidden], ffn_run)
    grad_w_ffup = columns(ff_grad[..., hidden:], ffn_run)
    rec_grad = to_owner(pair_dot((normed_even, normed_odd), (grad_even, grad_odd), "td,tc->dc"))
    grad_w_in = columns(rec_grad[..., : 2 * chan], mix_run)
    grad_w_forget = columns(rec_grad[..., 2 * chan : 3 * chan], mix_run)
    grad_w_gate = columns(rec_grad[..., 3 * chan :], mix_run)

    pairs = [
        (s * planes + w, w * groups + s) for s in range(groups) for w in range(planes)
    ]

    def rows_to_owner(grad):
        part = shard_scatter(grad.astype(BF))
        return lax.ppermute(part, ("seq", "wshard"), pairs).astype(F32)

    grad_w_down = rows_to_owner(
        pair_dot((hidden_even, hidden_odd), (up_even, up_odd), "tf,td->fd")
    )
    grad_w_out = rows_to_owner(
        pair_dot((scaled_even, scaled_odd), (branch_even, branch_odd), "tc,td->cd")
    )

    def spread(part):
        count = part.shape[1] // mix_run
        zero = jnp.zeros((count, groups, mix_run), F32)
        zero = lax.dynamic_update_slice(zero, part.reshape(count, 1, mix_run), (0, place, 0))
        return zero.reshape(-1)

    pieces = [
        spread(sum_bias),
        spread(sum_theta),
        spread(sum_gain),
        grad_gain_ffn,
        grad_gain_mix,
        jnp.stack(
            [
                jnp.sum(resid_in * resid_in),
                jnp.sum(branch_mix * branch_mix),
                jnp.sum(branch_ffn * branch_ffn),
            ]
        ),
    ]
    sums = sum_seq(jnp.concatenate(pieces))
    sums = sum_tree([sums, *others(sums)])
    cuts = []
    offset = 0
    for piece in pieces:
        cuts.append(sums[offset : offset + piece.shape[0]])
        offset += piece.shape[0]
    grad_bias, grad_theta, grad_gain_out, grad_gain_ffn, grad_gain_mix, squares = cuts
    rms_values = jnp.sqrt(squares / (rows * width * devices))
    return (
        result.reshape(seqs, seq_dev, width),
        grad_tokens.reshape(seqs, seq_dev, width),
        grad_gain_mix,
        grad_w_in,
        grad_w_forget,
        grad_bias,
        grad_theta,
        grad_w_gate,
        grad_gain_out,
        grad_w_out,
        grad_gain_ffn,
        grad_w_ffgate,
        grad_w_ffup,
        grad_w_down,
        rms_values,
    )


def body(
    tokens,
    starts,
    layer_index,
    gain_mix,
    w_in,
    w_forget,
    bias_forget,
    theta,
    w_gate_out,
    gain_out,
    w_out,
    gain_ffn,
    w_ffgate,
    w_ffup,
    w_down,
    out_grad,
):
    seqs, seq_dev, width = tokens.shape
    rows = seqs * seq_dev
    groups = lax.axis_size("seq")
    planes = lax.axis_size("wshard")
    half = groups // 2
    devices = groups * planes
    mix_run = w_out.shape[0] // groups
    ffn_run = w_down.shape[0] // groups
    chan = mix_run * planes // 2
    shares = (ffn_run * 6 // 11, ffn_run - ffn_run * 6 // 11)
    if not (
        groups == 8
        and groups % planes == 0
        and seqs == 2
        and chan % LANES == 0
        and all(2 * planes * share % LANES == 0 and share % 16 == 0 for share in shares)
    ):
        return plain_body(
            tokens,
            starts,
            layer_index,
            gain_mix,
            w_in,
            w_forget,
            bias_forget,
            theta,
            w_gate_out,
            gain_out,
            w_out,
            gain_ffn,
            w_ffgate,
            w_ffup,
            w_down,
            out_grad,
        )
    place = lax.axis_index("seq")
    floor = layer_index.astype(F32) / LAYERS
    place_one = place.reshape(1)

    first_bit, second_bit = chip_bits()

    def turned(block):
        return lax.rem(block + place, planes) + planes * (place // planes)

    def own_columns(array, run, first, count, where):
        blocks = array.shape[1] // (run * groups)
        column = lax.broadcasted_iota(jnp.int32, (array.shape[1], blocks * count), 0)
        index = lax.broadcasted_iota(jnp.int32, (array.shape[1], blocks * count), 1)
        block = index // count
        wanted = (block * groups + where(block)) * run + first + (index - block * count)
        return dot(array, (column == wanted).astype(BF), "rc,cj->rj").astype(BF)

    def own_parts(vector):
        count = vector.shape[0] // (mix_run * groups)
        split = vector.reshape(count, groups, mix_run)
        return lax.dynamic_slice_in_dim(split, place, 1, 1).reshape(1, count * mix_run)

    def own_rows(array, first, count, where):
        run = array.shape[0] // groups
        return lax.dynamic_slice_in_dim(array, where * run + first, count, 0)

    rec_own = jnp.concatenate(
        [
            own_columns(array, mix_run, 0, mix_run, lambda block: place)
            for array in (w_in, w_forget, w_gate_out)
        ],
        axis=1,
    )
    packs = [pack([rec_own[None], own_rows(w_out, 0, mix_run, place)[None]])]
    first = 0
    for share in shares:
        ff_own = jnp.concatenate(
            [own_columns(array, ffn_run, first, share, turned) for array in (w_ffgate, w_ffup)], axis=1
        )
        packs.append(pack([ff_own[None], own_rows(w_down, first, share, turned(lax.axis_index("wshard")))[None]]))
        first += share
    rec_packed = gather_packed(packs[0])

    upstream_own = out_grad.reshape(rows, width)
    up_stage = gather_first(upstream_own)
    tokens_, up_stage = tied(after(tokens, packs[0]), up_stage)
    resid_in = tokens_.reshape(rows, width).astype(F32)
    scale_in = lax.rsqrt(jnp.mean(resid_in * resid_in, axis=1, keepdims=True) + EPS)
    normed_own = (resid_in * scale_in * gain_mix).astype(BF)
    normed_stage = gather_first(normed_own)
    normed_stage, packs[1], packs[2] = tied(normed_stage, packs[1], packs[2])
    normed_far = gather_far(normed_own, normed_stage)
    normed_even = (normed_own, *normed_stage, *normed_far)
    normed_odd = cross(normed_even)
    up_far = gather_far(upstream_own, up_stage)
    packed = [gather_packed(item) for item in packs[1:]]

    slots = lax.broadcasted_iota(jnp.int32, (groups, groups), 0)
    sources = lax.broadcasted_iota(jnp.int32, (groups, groups), 1)
    keys = jnp.where(slots < half, 2 * slots, 2 * (slots - half) + 1)
    chosen = ((place ^ keys) == sources).astype(F32)
    marks = starts.astype(F32).reshape(seqs, groups, seq_dev).transpose(1, 0, 2)
    flags = jnp.sum(chosen[:, :, None, None] * marks[None], axis=1)[..., None]
    bias_own = own_parts(bias_forget)
    theta_own = own_parts(theta)
    gain_own = own_parts(gain_out)

    pre_even, pre_odd, state, square, *mixes = mix_forward(
        place_one,
        floor,
        normed_even,
        normed_odd,
        rec_packed,
        flags,
        bias_own,
        theta_own,
        gain_own,
    )
    mixes = tuple(item.reshape(rows, width) for item in mixes)
    mix_even, mix_odd = mixes[:half], mixes[half:]
    mix_odd, up_far = tied(mix_odd, up_far)
    up_even = (upstream_own, *up_stage, *up_far)
    square = shrink(square.reshape(groups, rows), 1)
    mix_crossed = cross(mix_odd)
    mix_far = scatter_far(mix_even[3], mix_crossed[3])
    square_next = shrink(square, second_bit)
    mix_far, square_next = tied(mix_far, square_next)
    mix_near = scatter_near(mix_even[1:3], mix_crossed[1:3], mix_far)
    up_odd = cross(up_even)
    square_own = shrink(square_next, first_bit)
    scale_own = lax.rsqrt(square_own / width + EPS)
    scale_out = scale_own.reshape(rows, 1)
    branch_mix = scale_out * scatter_sum(mix_even[0], mix_crossed[0], mix_near)
    resid = resid_in + branch_mix
    scale_ffn = lax.rsqrt(jnp.mean(resid * resid, axis=1, keepdims=True) + EPS)
    ffn_own = (resid * scale_ffn * gain_ffn).astype(BF)
    ffn_stage = gather_first(ffn_own)
    ffn_far = gather_far(ffn_own, ffn_stage)
    scale_all = gather_small(scale_own)

    cols = [2 * planes * share for share in shares]

    def block(normed, up, slot):
        cut = slice(slot, slot + 1) if slot < 3 else slice(3, None)
        return normed[cut], up[cut]

    def grouped(blocks, out):
        return (
            [piece for item in blocks for piece in item[0]],
            [piece for item in blocks for piece in item[1]],
            out[1],
            out[0],
        )

    def gradients(groups_, turn):
        return grads_call(groups, planes, turn, groups_)

    ffn_near = (ffn_own, *ffn_stage)
    even_blocks = [block(ffn_near, up_even, slot) for slot in range(3)]
    even_out = ffn_call(even_blocks, packed[0], cols[0], fills=True)
    odd_near = cross(ffn_near)
    odd_blocks = [block(odd_near, up_odd, slot) for slot in range(3)]
    odd_out = ffn_call(odd_blocks, packed[0], cols[0], fills=True)
    ffn_far, odd_out = tied(ffn_far, odd_out)
    odd_far = cross(ffn_far)
    ffn_even = (*ffn_near, *ffn_far)
    ffn_odd = (*odd_near, *odd_far)
    far_blocks = [block(ffn_even, up_even, 3), block(ffn_odd, up_odd, 3)]
    far_out = ffn_call(far_blocks, packed[0], cols[0])
    firsts = [
        (even_blocks, even_out),
        (odd_blocks, odd_out),
        (far_blocks, far_out),
    ]
    ff_grads = [gradients([grouped(*item) for item in firsts], place_one)]
    even_place = [(0, 0), (0, rows), (0, 2 * rows), (2, 0)]
    odd_place = [(1, 0), (1, rows), (1, 2 * rows), (2, rows)]

    def base(place_):
        return firsts[place_[0]][1][2], place_[1]

    packed[1], ff_grads[0], scale_all, _ = tied(packed[1], ff_grads[0], scale_all, far_out)
    far_blocks = [block(ffn_odd, up_odd, 3), block(ffn_even, up_even, 3)]
    far_out = ffn_call(far_blocks, packed[1], cols[1], [base(odd_place[3]), base(even_place[3])])
    (far_crossed,) = cross([far_out[2]])
    back_far = scatter_far(far_out[3], far_crossed)
    near_packed, _ = tied(packed[1], far_crossed)
    near_blocks = [block(ffn_odd, up_odd, slot) for slot in (1, 2)]
    near_blocks += [block(ffn_even, up_even, slot) for slot in (1, 2)]
    near_out = ffn_call(
        near_blocks,
        near_packed,
        cols[1],
        [base(odd_place[1]), base(odd_place[2]), base(even_place[1]), base(even_place[2])],
        True,
    )
    back_far, near_out = tied(back_far, near_out)
    near_crossed = cross(near_out[2:4])
    back_sums = near_sums(near_out[4:6], near_crossed, back_far)
    back_near = to_neighbours(back_sums)
    own_packed, _ = tied(packed[1], back_sums)
    own_blocks = [block(ffn_odd, up_odd, 0), block(ffn_even, up_even, 0)]
    own_out = ffn_call(
        own_blocks, own_packed, cols[1], [base(odd_place[0]), base(even_place[0])], True
    )
    (own_crossed,) = cross([own_out[2]])
    seconds = [(far_blocks, far_out), (near_blocks, near_out), (own_blocks, own_out)]
    ff_grads.append(gradients([grouped(*item) for item in seconds], place_one))
    back_near, ff_grads[1], own_crossed = tied(back_near, ff_grads[1], own_crossed)
    grad_normed_ffn = scatter_sum(own_out[3], own_crossed, back_near)

    scaled_ffn = grad_normed_ffn * gain_ffn
    grad_resid = (
        upstream_own.astype(F32)
        + scale_ffn * scaled_ffn
        - resid * scale_ffn**3 * jnp.mean(scaled_ffn * resid, axis=1, keepdims=True)
    )
    grad_gain_ffn = jnp.sum(grad_normed_ffn * resid * scale_ffn, axis=0)
    grad_branch_own = grad_resid.astype(BF)
    overlap = jnp.sum(grad_branch_own.astype(F32) * branch_mix, axis=1)
    term_own = (scale_out[:, 0] ** 2 * overlap / width)[None]
    branch_stage = gather_first(grad_branch_own)
    term_near = grow(grow(term_own, 1), first_bit)
    hiddens = [[item[1][0] for item in firsts], [item[1][0] for item in seconds]]
    hiddens[1][2] = after(hiddens[1][2], grad_branch_own)
    odd_second = [(2, 0), (1, 0), (1, rows), (0, 0)]
    even_second = [(2, rows), (1, 2 * rows), (1, 3 * rows), (0, rows)]
    result_odd = result_call(
        hiddens, tuple(zip(odd_place, odd_second)), packed, rows, width
    )
    result_even = result_call(
        hiddens, tuple(zip(even_place, even_second)), packed, rows, width
    )
    branch_stage, result_even, result_odd, term_near = tied(
        branch_stage, tuple(result_even), tuple(result_odd), term_near
    )
    branch_far = gather_far(grad_branch_own, branch_stage)
    result_crossed = cross(result_odd)
    term_all = grow(term_near, second_bit)
    branch_far, result_crossed, term_all = tied(branch_far, result_crossed, term_all)
    result_stage = scatter_first(joints(result_even, result_crossed))
    term_all = slot_rows(term_all)
    branch_even = (grad_branch_own, *branch_stage, *branch_far)
    branch_odd = cross(branch_even)

    mix_pairs = [(s * planes + w, w * groups + s) for s in range(groups) for w in range(planes)]
    down_pairs = []
    for s in range(groups):
        for w in range(planes):
            owner = (w - s) % planes * (groups // planes) + s // planes
            down_pairs.append((s * planes + w, owner * planes + w))

    scattered = [scatter_packed(grads) for grads in ff_grads]

    def owned(part, count, pairs):
        lines = count * width // (planes * LANES)
        tiles = part[:lines].reshape(groups, -1, LANES)
        tiles = lax.all_to_all(tiles, "seq", split_axis=0, concat_axis=0, tiled=True)
        tiles = tiles.reshape(groups, count // LANES, -1, LANES)
        moved = lax.ppermute(part[lines:], ("seq", "wshard"), pairs)
        return tiles, moved.reshape(width // LANES, -1, LANES)

    shape_one = (groups, seqs, seq_dev, 1)
    (
        grad_even,
        grad_odd,
        scaled_even,
        scaled_odd,
        sum_bias,
        sum_theta,
        sum_gain,
        *backs,
    ) = mix_backward(
        place_one,
        floor,
        rec_packed,
        pre_even,
        pre_odd,
        flags,
        bias_own,
        theta_own,
        gain_own,
        state,
        scale_all.reshape(shape_one),
        term_all.reshape(shape_one),
        branch_even,
        branch_odd,
    )
    grad_even = grad_even.reshape(half * rows, 5 * chan)
    grad_odd = grad_odd.reshape(half * rows, 5 * chan)
    scaled_even = scaled_even.reshape(half * rows, 2 * chan)
    scaled_odd = scaled_odd.reshape(half * rows, 2 * chan)
    backs = tuple(item.reshape(rows, width) for item in backs)
    grad_even, result_stage, scattered = tied(grad_even, result_stage, scattered)
    rec_grads = gradients(
        [
            (normed_even, branch_even, grad_even, scaled_even),
            (normed_odd, branch_odd, grad_odd, scaled_odd),
        ],
        jnp.zeros((1,), jnp.int32),
    )
    back_even, back_odd = backs[:half], backs[half:]
    back_crossed = cross(back_odd)
    back_crossed, rec_grads = tied(back_crossed, rec_grads)
    back_far = scatter_far(back_even[3], back_crossed[3])
    branch_ffn = scatter_last(result_even, result_crossed, after(result_stage, rec_grads))
    first_tiles, first_lines = owned(scattered[0], cols[0], down_pairs)
    second_tiles, second_lines = owned(scattered[1], cols[1], down_pairs)
    back_far, branch_ffn, first_tiles, second_tiles = tied(
        back_far, branch_ffn, first_tiles, second_tiles
    )
    back_near = scatter_near(back_even[1:3], back_crossed[1:3], back_far)
    back_near, rec_part = tied(back_near, scatter_packed(rec_grads))
    grad_normed_in = scatter_sum(back_even[0], back_crossed[0], back_near)
    rec_tiles, rec_lines = owned(rec_part, 5 * chan, mix_pairs)
    result = (resid + branch_ffn).astype(BF)
    scaled_in = grad_normed_in * gain_mix
    grad_tokens = (
        grad_resid
        + scale_in * scaled_in
        - resid_in * scale_in**3 * jnp.mean(scaled_in * resid_in, axis=1, keepdims=True)
    ).astype(BF)
    grad_gain_mix = jnp.sum(grad_normed_in * resid_in * scale_in, axis=0)

    hidden_all = w_ffgate.shape[1]
    rec_widths = (w_in.shape[1], w_forget.shape[1], w_gate_out.shape[1])
    grad_w_ffgate, grad_w_ffup = assemble_tiles(
        [first_tiles, second_tiles], shares, planes, (hidden_all, hidden_all)
    )
    grad_w_down = assemble_rows([first_lines, second_lines])
    grad_w_out = assemble_rows([rec_lines])

    def spread(part):
        count = part.shape[1] // mix_run
        zero = jnp.zeros((count, groups, mix_run), F32)
        zero = lax.dynamic_update_slice(zero, part.reshape(count, 1, mix_run), (0, place, 0))
        return zero.reshape(-1)

    pieces = [
        spread(sum_bias),
        spread(sum_theta),
        spread(sum_gain),
        grad_gain_ffn,
        grad_gain_mix,
        jnp.stack(
            [
                jnp.sum(resid_in * resid_in),
                jnp.sum(branch_mix * branch_mix),
                jnp.sum(branch_ffn * branch_ffn),
            ]
        ),
    ]
    sums, rec_tiles = tied(sum_seq(jnp.concatenate(pieces)), rec_tiles)
    sums = sum_tree([sums, *others(sums)])
    grad_w_in, grad_w_forget, grad_w_gate = assemble_tiles([rec_tiles], (mix_run,), 0, rec_widths)
    cuts = []
    offset = 0
    for piece in pieces:
        cuts.append(sums[offset : offset + piece.shape[0]])
        offset += piece.shape[0]
    grad_bias, grad_theta, grad_gain_out, grad_gain_ffn, grad_gain_mix, squares = cuts
    rms_values = jnp.sqrt(squares / (rows * width * devices))
    return (
        result.reshape(seqs, seq_dev, width),
        grad_tokens.reshape(seqs, seq_dev, width),
        grad_gain_mix,
        grad_w_in,
        grad_w_forget,
        grad_bias,
        grad_theta,
        grad_w_gate,
        grad_gain_out,
        grad_w_out,
        grad_gain_ffn,
        grad_w_ffgate,
        grad_w_ffup,
        grad_w_down,
        rms_values,
    )


def solution(mesh):
    whole = P()
    rowed = P("wshard", None)
    stream = P("wshard", "seq", None)
    owned = P(("seq", "wshard"), None)
    return jax.shard_map(
        body,
        mesh=mesh,
        in_specs=(
            stream,
            rowed,
            whole,
            whole,
            rowed,
            rowed,
            whole,
            whole,
            rowed,
            whole,
            rowed,
            whole,
            rowed,
            rowed,
            rowed,
            stream,
        ),
        out_specs=(
            stream,
            stream,
            whole,
            owned,
            owned,
            whole,
            whole,
            owned,
            whole,
            owned,
            whole,
            owned,
            owned,
            owned,
            whole,
        ),
        check_vma=False,
    )
```

```python
import functools

import jax
import jax.numpy as jnp
from jax import lax
from jax.experimental import pallas as pl
from jax.experimental.pallas import tpu as pltpu
from jax.sharding import PartitionSpec as P

LAYERS = 24
EPS = 1e-06
BF = jnp.bfloat16
F32 = jnp.float32


def dot(left, right, form):
    return jnp.einsum(form, left, right, preferred_element_type=F32)


def swap(value, bit):
    size = lax.axis_size("seq")
    return lax.ppermute(value, "seq", [(i, i ^ bit) for i in range(size)])


def chip_bits():
    size = lax.axis_size("seq")
    return [1 << i for i in range(1, size.bit_length() - 1)]


def plain_even(own):
    bits = chip_bits()
    if len(bits) == 2:
        first, second = bits
        half = own.shape[0] // 2
        from_first = swap(own, first)
        from_second = swap(own, second)
        top = swap(from_first[:half], second)
        low = swap(from_second[half:], first)
        return jnp.concatenate([own, from_first, from_second, top, low], axis=0)
    held = own
    for bit in bits:
        held = jnp.concatenate([held, swap(held, bit)], axis=0)
    return held


def plain_gather(own):
    even = plain_even(own)
    return even, swap(even, 1)


def plain_scatter(even, odd):
    bits = chip_bits()
    joint = even.astype(F32) + swap(odd, 1).astype(F32)
    if len(bits) == 2:
        first, second = bits
        rows = joint.shape[0] // 4
        half = rows // 2
        low_joint = joint.astype(BF)
        near_first, near_second, far = (
            low_joint[rows : 2 * rows],
            low_joint[2 * rows : 3 * rows],
            low_joint[3 * rows :],
        )
        far_top = swap(far[:half], first)
        far_low = swap(far[half:], second)
        first_top = swap(near_first[:half], first)
        second_low = swap(near_second[half:], second)
        first_low = swap((near_first[half:].astype(F32) + far_low.astype(F32)).astype(BF), first)
        second_top = swap(
            (near_second[:half].astype(F32) + far_top.astype(F32)).astype(BF), second
        )
        first_all = jnp.concatenate([first_top, first_low], axis=0).astype(F32)
        second_all = jnp.concatenate([second_top, second_low], axis=0).astype(F32)
        return joint[:rows] + first_all + second_all
    for bit in reversed(bits):
        half = joint.shape[0] // 2
        joint = joint[:half] + swap(joint[half:].astype(BF), bit).astype(F32)
    return joint


def gather_first(own):
    return tuple(swap(own, bit) for bit in chip_bits())


def gather_far(own, stage):
    first, second = chip_bits()
    half = own.shape[0] // 2
    return swap(stage[0][:half], second), swap(stage[1][half:], first)


def cross(pieces):
    return tuple(swap(piece, 1) for piece in pieces)


def scatter_far(even, crossed):
    half = even.shape[0] // 2
    bits = chip_bits()
    return tuple(
        swap((even[rows].astype(F32) + crossed[rows].astype(F32)).astype(BF), bit)
        for rows, bit in zip((slice(0, half), slice(half, None)), bits)
    )


def onward_kernel(first_even, first_cross, far_low, second_even, second_cross, far_top, *outs):
    half = far_low.shape[0]
    first_out, second_out = outs
    both = first_even[...].astype(F32) + first_cross[...].astype(F32)
    first_out[:half, :] = both[:half].astype(BF)
    first_out[half:, :] = (both[half:] + far_low[...].astype(F32)).astype(BF)
    both = second_even[...].astype(F32) + second_cross[...].astype(F32)
    second_out[:half, :] = (both[:half] + far_top[...].astype(F32)).astype(BF)
    second_out[half:, :] = both[half:].astype(BF)


def near_sums(even, crossed, far):
    rows, width = even[0].shape
    step = width // 4
    whole = pl.BlockSpec((rows, step), lambda i: (0, i))
    part = pl.BlockSpec((rows // 2, step), lambda i: (0, i))
    return pl.pallas_call(
        onward_kernel,
        grid=(width // step,),
        in_specs=[whole, whole, part] * 2,
        out_specs=[whole] * 2,
        out_shape=[jax.ShapeDtypeStruct((rows, width), BF)] * 2,
        cost_estimate=SMALL,
        name="onward_sums",
    )(even[0], crossed[0], far[1], even[1], crossed[1], far[0])


def to_neighbours(sums):
    return tuple(swap(item, bit) for item, bit in zip(sums, chip_bits()))


def scatter_near(even, crossed, far):
    return to_neighbours(near_sums(even, crossed, far))


def joint_kernel(*refs):
    count = len(refs) // 3
    for index in range(count):
        both = refs[index][...].astype(F32) + refs[count + index][...].astype(F32)
        refs[2 * count + index][...] = both.astype(BF)


FIRST_SUMS = ((3, 0), (3, 1), (1, 0), (2, 1))


def joints(even, crossed):
    rows, width = even[0].shape
    half = rows // 2
    step = width // 4

    def spec(part):
        return pl.BlockSpec((half, step), lambda i, part=part: (part, i))

    return pl.pallas_call(
        joint_kernel,
        grid=(width // step,),
        in_specs=[spec(part) for _, part in FIRST_SUMS] * 2,
        out_specs=[spec(0)] * len(FIRST_SUMS),
        out_shape=[jax.ShapeDtypeStruct((half, width), BF)] * len(FIRST_SUMS),
        cost_estimate=SMALL,
        name="chip_sums",
    )(*[even[index] for index, _ in FIRST_SUMS], *[crossed[index] for index, _ in FIRST_SUMS])


def scatter_first(sums):
    first, second = chip_bits()
    return tuple(swap(item, bit) for item, bit in zip(sums, (first, second, first, second)))


def scatter_last(even, crossed, stage):
    first, second = chip_bits()
    half = even[0].shape[0] // 2
    far_top, far_low, first_top, second_low = stage

    def onward(index, rows, far):
        both = even[index][rows].astype(F32) + crossed[index][rows].astype(F32)
        return (both + far.astype(F32)).astype(BF)

    first_low = swap(onward(1, slice(half, None), far_low), first)
    second_top = swap(onward(2, slice(0, half), far_top), second)
    first_all = jnp.concatenate([first_top, first_low], axis=0).astype(F32)
    second_all = jnp.concatenate([second_top, second_low], axis=0).astype(F32)
    return even[0].astype(F32) + crossed[0].astype(F32) + first_all + second_all


def scatter_sum(even, crossed, near):
    return (even.astype(F32) + crossed.astype(F32)) + (near[0].astype(F32) + near[1].astype(F32))


def tied(*values):
    return lax.optimization_barrier(values)


def grow(held, bit):
    return jnp.concatenate([held, swap(held, bit)], axis=0)


def shrink(blocks, bit):
    half = blocks.shape[0] // 2
    return blocks[:half] + swap(blocks[half:], bit)


def slot_rows(held):
    pairs = held.reshape(held.shape[0] // 2, 2, -1)
    return pairs.transpose(1, 0, 2).reshape(held.shape)


def gather_small(own):
    for bit in [1] + chip_bits():
        own = grow(own, bit)
    return slot_rows(own)


def scatter_small(blocks):
    for bit in [1] + list(reversed(chip_bits())):
        blocks = shrink(blocks, bit)
    return blocks


def sum_seq(value):
    for bit in [1] + chip_bits():
        value = value + swap(value, bit)
    return value


def others(value):
    planes = lax.axis_size("wshard")
    return [
        lax.ppermute(value, "wshard", [(i, i ^ key) for i in range(planes)])
        for key in range(1, planes)
    ]


def sum_tree(values):
    while len(values) > 1:
        values = [values[i] + values[i + 1] for i in range(0, len(values), 2)]
    return values[0]


LANES = 128
SMALL = pl.CostEstimate(flops=1024, transcendentals=0, bytes_accessed=1024)


def filler(flops):
    return pl.CostEstimate(flops=flops, transcendentals=0, bytes_accessed=1024)


def pack(arrays):
    lines = []
    for array in arrays:
        count, rows, cols = array.shape
        split = array.reshape(count, rows, cols // LANES, LANES).transpose(0, 2, 1, 3)
        lines.append(split.reshape(count, rows * cols // LANES, LANES))
    return jnp.concatenate(lines, axis=1)


def gather_packed(packed):
    return lax.all_gather(packed, "wshard", axis=0, tiled=True)


def scatter_packed(packed):
    return lax.psum_scatter(
        packed.reshape(-1, LANES), "wshard", scatter_dimension=0, tiled=True
    )


def after(value, *others):
    return lax.optimization_barrier((value, others))[0]


def slot_of(place, group, groups):
    key = place ^ group
    return (key >> 1) + (key & 1) * (groups // 2)


def group_of(place, half, index):
    return place ^ ((index << 1) | half)


def token_rows(slot, tokens):
    return pl.ds(pl.multiple_of(slot * tokens, tokens), tokens)


def keep_of(pre, flag, bias, floor, chan):
    logit = (pre[:, 2 * chan : 3 * chan] + bias).astype(BF).astype(F32)
    sig = jax.nn.sigmoid(logit)
    return (floor + (1.0 - floor) * sig) * (1.0 - flag), sig


def forward_kernel(
    place_ref,
    floor_ref,
    pre_even,
    pre_odd,
    flag_ref,
    bias_ref,
    theta_ref,
    gain_ref,
    state_ref,
    gated_even,
    gated_odd,
    square_ref,
    keep_s,
    val_re,
    val_im,
    prod_re,
    prod_im,
    carry_re,
    carry_im,
):
    groups, _, tokens, _ = flag_ref.shape
    chan = keep_s.shape[1]
    half_groups = groups // 2
    floor = floor_ref[0]
    place = place_ref[0]
    cosine = jnp.cos(theta_ref[...])
    sine = jnp.sin(theta_ref[...])

    for half, pre_ref in ((0, pre_even), (1, pre_odd)):

        @pl.loop(0, half_groups)
        def _(index, half=half, pre_ref=pre_ref):
            slot = index + half * half_groups
            rows = token_rows(slot, tokens)
            pre = pre_ref[index, 0]
            keep, _ = keep_of(pre, flag_ref[slot, 0], bias_ref[...], floor, chan)
            keep_s[rows, :] = keep
            fresh = 1.0 - keep
            value = pre[:, :chan]
            val_re[rows, :] = fresh * (value * jax.nn.sigmoid(value)).astype(BF).astype(F32)
            value = pre[:, chan : 2 * chan]
            val_im[rows, :] = fresh * (value * jax.nn.sigmoid(value)).astype(BF).astype(F32)

    def step(t, carry):
        h_re, h_im, p_re, p_im = carry
        rows = pl.ds(t, groups, stride=tokens)
        held = keep_s[rows, :]
        a_re = held * cosine
        a_im = held * sine
        n_re = a_re * h_re - a_im * h_im + val_re[rows, :]
        n_im = a_re * h_im + a_im * h_re + val_im[rows, :]
        q_re = a_re * p_re - a_im * p_im
        q_im = a_re * p_im + a_im * p_re
        val_re[rows, :] = n_re
        val_im[rows, :] = n_im
        prod_re[rows, :] = q_re
        prod_im[rows, :] = q_im
        return n_re, n_im, q_re, q_im

    zero = jnp.zeros((groups, chan), F32)
    lax.fori_loop(0, tokens, step, (zero, zero, zero + 1.0, zero), unroll=8)

    def link(group, carry):
        c_re, c_im = carry
        slot = slot_of(place, group, groups)
        carry_re[pl.ds(slot, 1), :] = c_re
        carry_im[pl.ds(slot, 1), :] = c_im
        last = pl.ds(slot * tokens + tokens - 1, 1)
        p_re = prod_re[last, :]
        p_im = prod_im[last, :]
        return (
            p_re * c_re - p_im * c_im + val_re[last, :],
            p_re * c_im + p_im * c_re + val_im[last, :],
        )

    nought = jnp.zeros((1, chan), F32)
    lax.fori_loop(0, groups, link, (nought, nought))

    for half, pre_ref, gated_ref in ((0, pre_even, gated_even), (1, pre_odd, gated_odd)):

        @pl.loop(0, half_groups)
        def _(index, half=half, pre_ref=pre_ref, gated_ref=gated_ref):
            slot = index + half * half_groups
            rows = token_rows(slot, tokens)
            c_re = carry_re[pl.ds(slot, 1), :]
            c_im = carry_im[pl.ds(slot, 1), :]
            p_re = prod_re[rows, :]
            p_im = prod_im[rows, :]
            h_re = val_re[rows, :] + p_re * c_re - p_im * c_im
            h_im = val_im[rows, :] + p_re * c_im + p_im * c_re
            state_ref[slot, 0, :, :chan] = h_re
            state_ref[slot, 0, :, chan:] = h_im
            m_re = h_re.astype(BF).astype(F32)
            m_im = h_im.astype(BF).astype(F32)
            gate = jax.nn.sigmoid(pre_ref[index, 0, :, 3 * chan :]) * gain_ref[...]
            gated_ref[index, 0, :, :chan] = (m_re * gate[:, :chan]).astype(BF)
            gated_ref[index, 0, :, chan:] = (m_im * gate[:, chan:]).astype(BF)
            square_ref[slot, 0] = jnp.sum(m_re * m_re + m_im * m_im, axis=1, keepdims=True)


def backward_kernel(
    place_ref,
    floor_ref,
    pre_even,
    pre_odd,
    flag_ref,
    bias_ref,
    theta_ref,
    gain_ref,
    state_ref,
    up_even,
    up_odd,
    scale_ref,
    term_ref,
    out_even,
    out_odd,
    scaled_even,
    scaled_odd,
    sum_bias,
    sum_theta,
    sum_gain,
    keep_s,
    adj_re,
    adj_im,
    prod_re,
    prod_im,
    carry_re,
    carry_im,
    next_s,
):
    groups, _, tokens, _ = flag_ref.shape
    chan = keep_s.shape[1]
    half_groups = groups // 2
    floor = floor_ref[0]
    place = place_ref[0]
    cosine = jnp.cos(theta_ref[...])
    sine = jnp.sin(theta_ref[...])

    @pl.when(pl.program_id(0) == 0)
    def _():
        sum_bias[...] = jnp.zeros_like(sum_bias)
        sum_theta[...] = jnp.zeros_like(sum_theta)
        sum_gain[...] = jnp.zeros_like(sum_gain)

    for half, pre_ref, up_ref, out_ref, scaled_ref in (
        (0, pre_even, up_even, out_even, scaled_even),
        (1, pre_odd, up_odd, out_odd, scaled_odd),
    ):

        @pl.loop(0, half_groups)
        def _(
            index, half=half, pre_ref=pre_ref, up_ref=up_ref, out_ref=out_ref, scaled_ref=scaled_ref
        ):
            slot = index + half * half_groups
            rows = token_rows(slot, tokens)
            pre = pre_ref[index, 0]
            keep, _ = keep_of(pre, flag_ref[slot, 0], bias_ref[...], floor, chan)
            keep_s[rows, :] = keep
            scale = scale_ref[slot, 0]
            mixed = state_ref[slot, 0].astype(BF).astype(F32)
            sig = jax.nn.sigmoid(pre[:, 3 * chan :])
            inner = up_ref[index, 0] * sig
            scaled_ref[index, 0] = (mixed * gain_ref[...] * sig * scale).astype(BF)
            normed = inner * mixed * scale
            sum_gain[...] += jnp.sum(normed, axis=0, keepdims=True)
            out_ref[index, 0, :, 3 * chan :] = (normed * gain_ref[...] * (1.0 - sig)).astype(BF)
            grad = (scale * (inner * gain_ref[...]) - mixed * term_ref[slot, 0]).astype(BF)
            adj_re[rows, :] = grad[:, :chan].astype(F32)
            adj_im[rows, :] = grad[:, chan:].astype(F32)

    @pl.loop(0, groups)
    def _(group):
        slot = slot_of(place, group, groups)
        after = slot_of(place, lax.min(group + 1, groups - 1), groups)
        row = keep_s[pl.ds(after * tokens, 1), :]
        next_s[pl.ds(slot, 1), :] = jnp.where(group == groups - 1, 0.0, row)

    def turn(t, held, carry):
        g_re, g_im, p_re, p_im = carry
        rows = pl.ds(t, groups, stride=tokens)
        a_re = held * cosine
        a_im = held * sine
        n_re = a_re * g_re + a_im * g_im + adj_re[rows, :]
        n_im = a_re * g_im - a_im * g_re + adj_im[rows, :]
        q_re = a_re * p_re + a_im * p_im
        q_im = a_re * p_im - a_im * p_re
        adj_re[rows, :] = n_re
        adj_im[rows, :] = n_im
        prod_re[rows, :] = q_re
        prod_im[rows, :] = q_im
        return n_re, n_im, q_re, q_im

    def step(index, carry):
        t = tokens - 2 - index
        return turn(t, keep_s[pl.ds(t + 1, groups, stride=tokens), :], carry)

    zero = jnp.zeros((groups, chan), F32)
    carry = turn(tokens - 1, next_s[...], (zero, zero, zero + 1.0, zero))
    lax.fori_loop(0, tokens - 1, step, carry, unroll=4)

    def link(index, carry):
        c_re, c_im = carry
        slot = slot_of(place, groups - 1 - index, groups)
        carry_re[pl.ds(slot, 1), :] = c_re
        carry_im[pl.ds(slot, 1), :] = c_im
        first = pl.ds(slot * tokens, 1)
        p_re = prod_re[first, :]
        p_im = prod_im[first, :]
        return (
            p_re * c_re - p_im * c_im + adj_re[first, :],
            p_re * c_im + p_im * c_re + adj_im[first, :],
        )

    nought = jnp.zeros((1, chan), F32)
    lax.fori_loop(0, groups, link, (nought, nought))
    head = lax.broadcasted_iota(jnp.int32, (tokens, 2 * chan), 0) == 0

    for half, pre_ref, out_ref in ((0, pre_even, out_even), (1, pre_odd, out_odd)):

        @pl.loop(0, half_groups)
        def _(index, half=half, pre_ref=pre_ref, out_ref=out_ref):
            slot = index + half * half_groups
            rows = token_rows(slot, tokens)
            group = group_of(place, half, index)
            before = slot_of(place, lax.max(group - 1, 0), groups)
            tail = jnp.where(group == 0, 0.0, state_ref[before, 0, tokens - 1 :, :])
            prev = jnp.where(head, tail, pltpu.roll(state_ref[slot, 0], 1, 0))
            prev_re = prev[:, :chan]
            prev_im = prev[:, chan:]
            c_re = carry_re[pl.ds(slot, 1), :]
            c_im = carry_im[pl.ds(slot, 1), :]
            p_re = prod_re[rows, :]
            p_im = prod_im[rows, :]
            g_re = adj_re[rows, :] + p_re * c_re - p_im * c_im
            g_im = adj_im[rows, :] + p_re * c_im + p_im * c_re
            turn_re = cosine * prev_re - sine * prev_im
            turn_im = sine * prev_re + cosine * prev_im
            flag = flag_ref[slot, 0]
            pre = pre_ref[index, 0]
            keep, sig = keep_of(pre, flag, bias_ref[...], floor, chan)
            fresh = 1.0 - keep
            x_re = pre[:, :chan]
            x_im = pre[:, chan : 2 * chan]
            s_re = jax.nn.sigmoid(x_re)
            s_im = jax.nn.sigmoid(x_im)
            cand_re = (x_re * s_re).astype(BF).astype(F32)
            cand_im = (x_im * s_im).astype(BF).astype(F32)
            grad_keep = g_re * (turn_re - cand_re) + g_im * (turn_im - cand_im)
            sum_theta[...] -= jnp.sum(
                keep * (g_re * turn_im - g_im * turn_re), axis=0, keepdims=True
            )
            grad_forget = (
                grad_keep * (1.0 - flag) * ((1.0 - floor) * (sig * (1.0 - sig)))
            ).astype(BF)
            sum_bias[...] += jnp.sum(grad_forget.astype(F32), axis=0, keepdims=True)
            out_ref[index, 0, :, 2 * chan : 3 * chan] = grad_forget
            cand_grad = (fresh * g_re).astype(BF).astype(F32)
            out_ref[index, 0, :, :chan] = (
                cand_grad * s_re * (1.0 + x_re * (1.0 - s_re))
            ).astype(BF)
            cand_grad = (fresh * g_im).astype(BF).astype(F32)
            out_ref[index, 0, :, chan : 2 * chan] = (
                cand_grad * s_im * (1.0 + x_im * (1.0 - s_im))
            ).astype(BF)


def block_spec(groups, tokens, width):
    mode = pl.Buffered(1) if groups > 4 and width % 128 and width > 1 else None
    return pl.BlockSpec((groups, 1, tokens, width), lambda b: (0, b, 0, 0), pipeline_mode=mode)


def row_spec(width):
    return pl.BlockSpec((1, width), lambda b: (0, 0))


def recur_forward(place, floor, pre_even, pre_odd, flags, bias, theta, gain):
    groups, seqs, tokens, _ = flags.shape
    chan = bias.shape[1]
    half = groups // 2
    scalar = pl.BlockSpec(memory_space=pltpu.SMEM)
    rows = groups * tokens
    pre_spec = block_spec(half, tokens, 5 * chan)
    one = block_spec(groups, tokens, 1)
    gated = block_spec(half, tokens, 2 * chan)
    gated_shape = jax.ShapeDtypeStruct((half, seqs, tokens, 2 * chan), BF)
    size = seqs * rows * chan
    return pl.pallas_call(
        forward_kernel,
        grid=(seqs,),
        in_specs=[
            scalar,
            scalar,
            pre_spec,
            pre_spec,
            one,
            row_spec(chan),
            row_spec(chan),
            row_spec(2 * chan),
        ],
        out_specs=[block_spec(groups, tokens, 2 * chan), gated, gated, one],
        out_shape=[
            jax.ShapeDtypeStruct((groups, seqs, tokens, 2 * chan), F32),
            gated_shape,
            gated_shape,
            jax.ShapeDtypeStruct((groups, seqs, tokens, 1), F32),
        ],
        scratch_shapes=[pltpu.VMEM((rows, chan), F32)] * 5
        + [pltpu.VMEM((groups, chan), F32)] * 2,
        compiler_params=pltpu.CompilerParams(vmem_limit_bytes=56 * 2**20),
        cost_estimate=SMALL,
        name="recur_forward",
    )(place, floor, pre_even, pre_odd, flags, bias, theta, gain)


def recur_backward(
    place, floor, pre_even, pre_odd, flags, bias, theta, gain, state, up_even, up_odd, scale, term
):
    groups, seqs, tokens, _ = flags.shape
    chan = bias.shape[1]
    half = groups // 2
    scalar = pl.BlockSpec(memory_space=pltpu.SMEM)
    rows = groups * tokens
    pre_spec = block_spec(half, tokens, 5 * chan)
    one = block_spec(groups, tokens, 1)
    up_spec = block_spec(half, tokens, 2 * chan)
    out_shape = jax.ShapeDtypeStruct((half, seqs, tokens, 5 * chan), BF)
    scaled_shape = jax.ShapeDtypeStruct((half, seqs, tokens, 2 * chan), BF)
    size = seqs * rows * chan
    return pl.pallas_call(
        backward_kernel,
        grid=(seqs,),
        in_specs=[
            scalar,
            scalar,
            pre_spec,
            pre_spec,
            one,
            row_spec(chan),
            row_spec(chan),
            row_spec(2 * chan),
            block_spec(groups, tokens, 2 * chan),
            up_spec,
            up_spec,
            one,
            one,
        ],
        out_specs=[
            pre_spec,
            pre_spec,
            up_spec,
            up_spec,
            row_spec(chan),
            row_spec(chan),
            row_spec(2 * chan),
        ],
        out_shape=[
            out_shape,
            out_shape,
            scaled_shape,
            scaled_shape,
            jax.ShapeDtypeStruct((1, chan), F32),
            jax.ShapeDtypeStruct((1, chan), F32),
            jax.ShapeDtypeStruct((1, 2 * chan), F32),
        ],
        scratch_shapes=[pltpu.VMEM((rows, chan), F32)] * 5
        + [pltpu.VMEM((groups, chan), F32)] * 3,
        compiler_params=pltpu.CompilerParams(vmem_limit_bytes=56 * 2**20),
        cost_estimate=SMALL,
        name="recur_backward",
    )(
        place, floor, pre_even, pre_odd, flags, bias, theta, gain, state, up_even, up_odd, scale, term
    )


def unpack_columns(packed, out):
    planes = packed.shape[0]
    rows = out.shape[0] // planes
    for plane in range(planes):
        for tile in range(out.shape[1] // LANES):
            out[plane * rows : (plane + 1) * rows, tile * LANES : (tile + 1) * LANES] = packed[
                plane, tile * rows : (tile + 1) * rows, :
            ]


def unpack_rows(packed, first, out):
    planes = packed.shape[0]
    rows = out.shape[0] // planes
    for plane in range(planes):
        for tile in range(out.shape[1] // LANES):
            base = first + tile * rows
            out[plane * rows : (plane + 1) * rows, tile * LANES : (tile + 1) * LANES] = packed[
                plane, base : base + rows, :
            ]


def dot_nn(left, right):
    return jnp.dot(left, right, preferred_element_type=F32)


def dot_nt(left, right):
    return lax.dot_general(left, right, (((1,), (1,)), ((), ())), preferred_element_type=F32)


def dot_tn(left, right):
    return lax.dot_general(left, right, (((0,), (0,)), ((), ())), preferred_element_type=F32)


def dot_nn(left, right):
    return jnp.dot(left, right, preferred_element_type=F32)


def dot_nt(left, right):
    return lax.dot_general(left, right, (((1,), (1,)), ((), ())), preferred_element_type=F32)


def dot_tn(left, right):
    return lax.dot_general(left, right, (((0,), (0,)), ((), ())), preferred_element_type=F32)


PIECES = 5
ANYWHERE = pl.BlockSpec(memory_space=pl.ANY)
SCALAR = pl.BlockSpec(memory_space=pltpu.SMEM)


def block_copies(pieces, held, sems):
    copies = []
    index = 0
    for block, parts in enumerate(pieces):
        copies.append([])
        rows = held.shape[1] // len(parts)
        for part, (ref, offset) in enumerate(parts):
            source = ref if offset is None else ref.at[offset : offset + rows]
            target = held.at[block, part * rows : (part + 1) * rows]
            copies[-1].append(pltpu.make_async_copy(source, target, sems.at[index]))
            index += 1
    return copies


def ffn_kernel(counts, offsets, last, *refs):
    refs = list(refs)

    def take(count):
        taken = refs[:count]
        del refs[:count]
        return taken

    (packed_ref,) = take(1)
    blocks = len(counts)
    normed = [[(ref, None) for ref in take(count)] for count in counts]
    up = [[(ref, None) for ref in take(count)] for count in counts]
    groups = [normed, up]
    if offsets:
        groups.append([[(ref, offset)] for ref, offset in zip(take(blocks), offsets)])
    hidden_ref, grad_ref = take(2)
    backs = take(blocks if last else 1)
    ff_s, down_s = take(2)
    helds = take(len(groups))
    sems = take(len(groups))
    copies = [block_copies(*item) for item in zip(groups, helds, sems)]
    hidden = down_s.shape[0]
    step = pl.program_id(0)

    @pl.when(step == 0)
    def _():
        for block in range(blocks):
            for group in copies:
                for copy in group[block]:
                    copy.start()
        first = ff_s.shape[0] // packed_ref.shape[0] * (ff_s.shape[1] // LANES)
        unpack_columns(packed_ref, ff_s)
        unpack_rows(packed_ref, first, down_s)

    for block in range(blocks):

        @pl.when(step == block)
        def _(block=block):
            for group in copies:
                for copy in group[block]:
                    copy.wait()

    ff = dot_nn(helds[0][step], ff_s[...])
    gate, value = ff[:, :hidden], ff[:, hidden:]
    sig = jax.nn.sigmoid(gate)
    silu = gate * sig
    hidden_ref[...] = (silu * value).astype(BF)
    grad = dot_nt(helds[1][step], down_s[...])
    grad_ref[:, :hidden] = (grad * value * sig * (1.0 + gate * (1.0 - sig))).astype(BF)
    grad_ref[:, hidden:] = (grad * silu).astype(BF)
    back = dot_nt(grad_ref[...], ff_s[...])
    if offsets:
        back = back + helds[2][step]
    if last:
        for block in range(blocks):

            @pl.when(step == block)
            def _(block=block):
                backs[block][...] = back.astype(BF)
    else:
        backs[0][...] = back


def ffn_call(blocks, packed, ff_cols, bases=None, fills=False):
    rows = sum(piece.shape[0] for piece in blocks[0][0])
    width = blocks[0][0][0].shape[1]
    count = len(blocks)
    tokens = count * rows
    hidden = ff_cols // 2
    last = bases is not None
    counts = tuple(len(block[0]) for block in blocks)
    pieces = sum(counts)
    operands = [packed]
    for index in range(2):
        for block in blocks:
            operands += block[index]
    held = pltpu.VMEM((count, rows, width), BF)
    helds = [held, held]
    sems = [pltpu.SemaphoreType.DMA((pieces,))] * 2
    if last:
        operands += [array for array, _ in bases]
        helds.append(pltpu.VMEM((count, rows, width), F32))
        sems.append(pltpu.SemaphoreType.DMA((count,)))
    backs = [jax.ShapeDtypeStruct((tokens, width), F32)]
    back_specs = [pl.BlockSpec((rows, width), lambda i: (i, 0))]
    if last:
        backs = [jax.ShapeDtypeStruct((rows, width), BF)] * count
        back_specs = [pl.BlockSpec((rows, width), lambda i: (0, 0))] * count
    offsets = tuple(offset for _, offset in bases) if last else ()
    return pl.pallas_call(
        functools.partial(ffn_kernel, counts, offsets, last),
        grid=(count,),
        in_specs=[pl.BlockSpec(packed.shape, lambda i: (0, 0, 0), pipeline_mode=pl.Buffered(1))]
        + [ANYWHERE] * (len(operands) - 1),
        out_specs=[
            pl.BlockSpec((rows, hidden), lambda i: (i, 0)),
            pl.BlockSpec((rows, ff_cols), lambda i: (i, 0)),
        ]
        + back_specs,
        out_shape=[
            jax.ShapeDtypeStruct((tokens, hidden), BF),
            jax.ShapeDtypeStruct((tokens, ff_cols), BF),
            *backs,
        ],
        scratch_shapes=[pltpu.VMEM((width, ff_cols), BF), pltpu.VMEM((hidden, width), BF)]
        + helds
        + sems,
        compiler_params=pltpu.CompilerParams(vmem_limit_bytes=60 * 2**20),
        cost_estimate=filler(5 * tokens * width * ff_cols if fills else 1024),
        name="ffn",
    )(*operands)


def grads_kernel(planes, owners, counts, turn_ref, *refs):
    refs = list(refs)
    out_ref = refs.pop()

    def take(count):
        taken = refs[:count]
        del refs[:count]
        return taken

    groups = [(take(count), take(count), *take(2)) for count in counts]
    step = pl.program_id(0)
    steps = pl.num_programs(0)
    block = groups[0][0][0].shape[1]
    subs = owners // steps
    run = block // subs // planes
    tiles = groups[0][2].shape[1] // LANES
    count = groups[0][3].shape[1] // planes

    def joined(pieces):
        return jnp.concatenate([piece[...] for piece in pieces], axis=0)

    grad = sum(dot_tn(joined(left), cols[...]) for left, _, cols, _ in groups).astype(BF)
    for sub in range(subs):
        for plane in range(planes):
            first = (sub * planes + plane) * run
            for tile in range(tiles):
                base = ((step * subs + sub) * tiles + tile) * run
                lines = pl.ds(pl.multiple_of(base, 16), run)
                out_ref[plane, lines, :] = grad[
                    first : first + run, tile * LANES : (tile + 1) * LANES
                ]
    grad = sum(dot_tn(rows[...], joined(up)) for _, up, _, rows in groups).astype(BF)
    first = run * tiles * owners
    for index in range(planes):
        plane = lax.rem(turn_ref[0] + index, planes)
        for tile in range(block // LANES):
            base = first + (step * (block // LANES) + tile) * count
            lines = pl.ds(pl.multiple_of(base, 16), count)
            out_ref[plane, lines, :] = grad[
                index * count : (index + 1) * count, tile * LANES : (tile + 1) * LANES
            ]


def grads_call(owners, planes, turn, groups):
    width = groups[0][0][0].shape[1]
    steps = owners // 2
    block = width // steps
    col_count = groups[0][2].shape[1]
    row_count = groups[0][3].shape[1]
    tokens = sum(group[2].shape[0] for group in groups)
    lines = (col_count * width + row_count * width) // (planes * LANES)
    operands, specs = [turn], [SCALAR]
    for left, up, cols, rows in groups:
        for piece in (*left, *up):
            operands.append(piece)
            specs.append(pl.BlockSpec((piece.shape[0], block), lambda i: (0, i)))
        for array in (cols, rows):
            operands.append(array)
            specs.append(
                pl.BlockSpec(array.shape, lambda i: (0, 0), pipeline_mode=pl.Buffered(1))
            )
    return pl.pallas_call(
        functools.partial(
            grads_kernel, planes, owners, tuple(len(group[0]) for group in groups)
        ),
        grid=(steps,),
        in_specs=specs,
        out_specs=pl.BlockSpec((planes, lines, LANES), lambda i: (0, 0, 0)),
        out_shape=jax.ShapeDtypeStruct((planes, lines, LANES), BF),
        compiler_params=pltpu.CompilerParams(vmem_limit_bytes=60 * 2**20),
        cost_estimate=filler(4 * tokens * width * (col_count + row_count)),
        name="weight_grads",
    )(*operands)


def result_kernel(firsts, places, counts, *refs):
    hiddens = (refs[: counts[0]], refs[counts[0] : sum(counts)])
    refs = refs[sum(counts) :]
    outs, down_s = refs[2:-1], refs[-1]
    step = pl.program_id(0)
    first_rows = hiddens[0][0].shape[1]

    @pl.when(step == 0)
    def _():
        unpack_rows(refs[0], firsts[0], down_s.at[:first_rows])
        unpack_rows(refs[1], firsts[1], down_s.at[first_rows:])

    for slot, out in enumerate(outs):

        @pl.when(step == slot)
        def _(slot=slot, out=out):
            rows = out.shape[0]
            parts = []
            for arrays, (index, offset) in zip(hiddens, places[slot]):
                parts.append(arrays[index][offset : offset + rows, :])
            total = dot_nn(parts[0], down_s[:first_rows, :])
            total = total + dot_nn(parts[1], down_s[first_rows:, :])
            out[...] = total.astype(BF)


def result_call(hiddens, places, packed, rows, width):
    slots = len(places)
    total = hiddens[0][0].shape[1] + hiddens[1][0].shape[1]
    firsts = tuple(
        part.shape[1] - arrays[0].shape[1] // part.shape[0] * width // LANES
        for part, arrays in zip(packed, hiddens)
    )
    arrays = [*hiddens[0], *hiddens[1]]

    def whole(array):
        zeros = (0,) * array.ndim
        return pl.BlockSpec(array.shape, lambda i: zeros, pipeline_mode=pl.Buffered(1))

    return pl.pallas_call(
        functools.partial(
            result_kernel, firsts, places, (len(hiddens[0]), len(hiddens[1]))
        ),
        grid=(slots,),
        in_specs=[whole(array) for array in arrays] + [whole(part) for part in packed],
        out_specs=[pl.BlockSpec((rows, width), lambda i: (0, 0))] * slots,
        out_shape=[jax.ShapeDtypeStruct((rows, width), BF)] * slots,
        scratch_shapes=[pltpu.VMEM((total, width), BF)],
        compiler_params=pltpu.CompilerParams(vmem_limit_bytes=48 * 2**20),
        cost_estimate=filler(2 * slots * rows * width * total),
        name="ffn_result",
    )(*arrays, *packed)


def seq_copies(pieces, held, sems, seq):
    tokens = held.shape[2]
    rows = slice(seq * tokens, (seq + 1) * tokens)
    copies = [
        pltpu.make_async_copy(pieces[slot].at[rows], held.at[seq, slot], sems.at[seq, slot])
        for slot in range(3)
    ]
    copies.append(pltpu.make_async_copy(pieces[3 + seq], held.at[seq, 3], sems.at[seq, 3]))
    return copies


def fetch(groups):
    seqs = groups[0][1].shape[0]

    @pl.when(pl.program_id(0) == 0)
    def _():
        for seq in range(seqs):
            for pieces, held, sems in groups:
                for copy in seq_copies(pieces, held, sems, seq):
                    copy.start()


def arrive(groups):
    for seq in range(groups[0][1].shape[0]):

        @pl.when(pl.program_id(0) == seq)
        def _(seq=seq):
            for pieces, held, sems in groups:
                for copy in seq_copies(pieces, held, sems, seq):
                    copy.wait()


def unpack_mix(packed_ref, rec_s, out_s):
    @pl.when(pl.program_id(0) == 0)
    def _():
        lines = rec_s.shape[0] // packed_ref.shape[0] * (rec_s.shape[1] // LANES)
        unpack_columns(packed_ref, rec_s)
        unpack_rows(packed_ref, lines, out_s)


def mix_forward_kernel(*refs):
    place_ref, floor_ref, packed_ref, flag_ref, bias_ref, theta_ref, gain_ref = refs[:7]
    refs = refs[7:]
    even, odd = refs[:PIECES], refs[PIECES : 2 * PIECES]
    refs = refs[2 * PIECES :]
    pre_even, pre_odd, state_ref, square_ref = refs[:4]
    mix_even, mix_odd = refs[4:8], refs[8:12]
    rec_s, out_s, gated_even, gated_odd, x_even, x_odd, sems_even, sems_odd = refs[12:20]
    scratch = refs[20:]
    half, _, tokens, _ = pre_even.shape
    seq = pl.program_id(0)
    groups = ((even, x_even, sems_even), (odd, x_odd, sems_odd))
    fetch(groups)
    unpack_mix(packed_ref, rec_s, out_s)
    arrive(groups)
    for x_ref, pre_ref in ((x_even, pre_even), (x_odd, pre_odd)):

        @pl.loop(0, half, step=2)
        def _(index, x_ref=x_ref, pre_ref=pre_ref):
            pair = pl.ds(index, 2)
            x = x_ref[seq, pair].reshape(2 * tokens, -1)
            pre_ref[pair, 0] = dot_nn(x, rec_s[...]).reshape(2, tokens, -1)

    forward_kernel(
        place_ref,
        floor_ref,
        pre_even,
        pre_odd,
        flag_ref,
        bias_ref,
        theta_ref,
        gain_ref,
        state_ref,
        gated_even,
        gated_odd,
        square_ref,
        *scratch,
    )
    for gated_ref, mixes in ((gated_odd, mix_odd), (gated_even, mix_even)):
        for index in range(0, half, 2):
            gated = gated_ref[index : index + 2, 0].reshape(2 * tokens, -1)
            mix = dot_nn(gated, out_s[...]).astype(BF)
            mixes[index][0] = mix[:tokens]
            mixes[index + 1][0] = mix[tokens:]


def mix_forward(place, floor, even, odd, packed, flags, bias, theta, gain):
    groups, seqs, tokens, _ = flags.shape
    chan = bias.shape[1]
    half = groups // 2
    width = even[0].shape[-1]
    rows = groups * tokens
    pre_spec = block_spec(half, tokens, 5 * chan)
    one = block_spec(groups, tokens, 1)
    pre_shape = jax.ShapeDtypeStruct((half, seqs, tokens, 5 * chan), F32)
    mix_spec = pl.BlockSpec((1, tokens, width), lambda b: (b, 0, 0))
    mix_shape = jax.ShapeDtypeStruct((seqs, tokens, width), BF)
    gated = pltpu.VMEM((half, 1, tokens, 2 * chan), BF)
    held = pltpu.VMEM((seqs, half, tokens, width), BF)
    sems = pltpu.SemaphoreType.DMA((seqs, half))
    return pl.pallas_call(
        mix_forward_kernel,
        grid=(seqs,),
        in_specs=[
            SCALAR,
            SCALAR,
            pl.BlockSpec(packed.shape, lambda b: (0, 0, 0), pipeline_mode=pl.Buffered(1)),
            one,
            row_spec(chan),
            row_spec(chan),
            row_spec(2 * chan),
        ]
        + [ANYWHERE] * (2 * PIECES),
        out_specs=[pre_spec, pre_spec, block_spec(groups, tokens, 2 * chan), one]
        + [mix_spec] * (2 * half),
        out_shape=[
            pre_shape,
            pre_shape,
            jax.ShapeDtypeStruct((groups, seqs, tokens, 2 * chan), F32),
            jax.ShapeDtypeStruct((groups, seqs, tokens, 1), F32),
        ]
        + [mix_shape] * (2 * half),
        scratch_shapes=[
            pltpu.VMEM((width, 5 * chan), BF),
            pltpu.VMEM((2 * chan, width), BF),
            gated,
            gated,
            held,
            held,
            sems,
            sems,
        ]
        + [pltpu.VMEM((rows, chan), F32)] * 5
        + [pltpu.VMEM((groups, chan), F32)] * 2,
        compiler_params=pltpu.CompilerParams(vmem_limit_bytes=60 * 2**20),
        cost_estimate=SMALL,
        name="mix_forward",
    )(place, floor, packed, flags, bias, theta, gain, *even, *odd)


def mix_backward_kernel(*refs):
    place_ref, floor_ref, packed_ref = refs[:3]
    pre_even, pre_odd, flag_ref, bias_ref, theta_ref, gain_ref, state_ref = refs[3:10]
    scale_ref, term_ref = refs[10:12]
    refs = refs[12:]
    even, odd = refs[:PIECES], refs[PIECES : 2 * PIECES]
    refs = refs[2 * PIECES :]
    out_even, out_odd, scaled_even, scaled_odd, sum_bias, sum_theta, sum_gain = refs[:7]
    back_even, back_odd = refs[7:11], refs[11:15]
    rec_s, out_s, up_even, up_odd, x_even, x_odd, sems_even, sems_odd = refs[15:23]
    scratch = refs[23:]
    half, _, tokens, _ = pre_even.shape
    seq = pl.program_id(0)
    groups = ((even, x_even, sems_even), (odd, x_odd, sems_odd))
    fetch(groups)
    unpack_mix(packed_ref, rec_s, out_s)
    arrive(groups)
    for x_ref, up_ref in ((x_even, up_even), (x_odd, up_odd)):

        @pl.loop(0, half, step=2)
        def _(index, x_ref=x_ref, up_ref=up_ref):
            pair = pl.ds(index, 2)
            branch = x_ref[seq, pair].reshape(2 * tokens, -1)
            up_ref[pair, 0] = dot_nt(branch, out_s[...]).reshape(2, tokens, -1)

    backward_kernel(
        place_ref,
        floor_ref,
        pre_even,
        pre_odd,
        flag_ref,
        bias_ref,
        theta_ref,
        gain_ref,
        state_ref,
        up_even,
        up_odd,
        scale_ref,
        term_ref,
        out_even,
        out_odd,
        scaled_even,
        scaled_odd,
        sum_bias,
        sum_theta,
        sum_gain,
        *scratch,
    )
    for out_ref, backs in ((out_odd, back_odd), (out_even, back_even)):
        for index in range(0, half, 2):
            grad = out_ref[index : index + 2, 0].reshape(2 * tokens, -1)
            back = dot_nt(grad, rec_s[...]).astype(BF)
            backs[index][0] = back[:tokens]
            backs[index + 1][0] = back[tokens:]


def mix_backward(
    place, floor, packed, pre_even, pre_odd, flags, bias, theta, gain, state, scale, term,
    even, odd,
):
    groups, seqs, tokens, _ = flags.shape
    chan = bias.shape[1]
    half = groups // 2
    width = even[0].shape[-1]
    rows = groups * tokens
    pre_spec = block_spec(half, tokens, 5 * chan)
    one = block_spec(groups, tokens, 1)
    pair_spec = block_spec(half, tokens, 2 * chan)
    back_spec = pl.BlockSpec((1, tokens, width), lambda b: (b, 0, 0))
    pre_shape = jax.ShapeDtypeStruct((half, seqs, tokens, 5 * chan), BF)
    pair_shape = jax.ShapeDtypeStruct((half, seqs, tokens, 2 * chan), BF)
    up = pltpu.VMEM((half, 1, tokens, 2 * chan), F32)
    held = pltpu.VMEM((seqs, half, tokens, width), BF)
    sems = pltpu.SemaphoreType.DMA((seqs, half))
    return pl.pallas_call(
        mix_backward_kernel,
        grid=(seqs,),
        in_specs=[
            SCALAR,
            SCALAR,
            pl.BlockSpec(packed.shape, lambda b: (0, 0, 0), pipeline_mode=pl.Buffered(1)),
            pre_spec,
            pre_spec,
            one,
            row_spec(chan),
            row_spec(chan),
            row_spec(2 * chan),
            block_spec(groups, tokens, 2 * chan),
            one,
            one,
        ]
        + [ANYWHERE] * (2 * PIECES),
        out_specs=[
            pre_spec,
            pre_spec,
            pair_spec,
            pair_spec,
            row_spec(chan),
            row_spec(chan),
            row_spec(2 * chan),
        ]
        + [back_spec] * (2 * half),
        out_shape=[
            pre_shape,
            pre_shape,
            pair_shape,
            pair_shape,
            jax.ShapeDtypeStruct((1, chan), F32),
            jax.ShapeDtypeStruct((1, chan), F32),
            jax.ShapeDtypeStruct((1, 2 * chan), F32),
        ]
        + [jax.ShapeDtypeStruct((seqs, tokens, width), BF)] * (2 * half),
        scratch_shapes=[
            pltpu.VMEM((width, 5 * chan), BF),
            pltpu.VMEM((2 * chan, width), BF),
            up,
            up,
            held,
            held,
            sems,
            sems,
        ]
        + [pltpu.VMEM((rows, chan), F32)] * 5
        + [pltpu.VMEM((groups, chan), F32)] * 3,
        compiler_params=pltpu.CompilerParams(vmem_limit_bytes=60 * 2**20),
        cost_estimate=SMALL,
        name="mix_backward",
    )(
        place, floor, packed, pre_even, pre_odd, flags, bias, theta, gain, state, scale,
        term, *even, *odd,
    )


def assemble_tiles_kernel(shares, planes, *refs):
    sources, outs = refs[: len(shares)], refs[len(shares) :]
    groups = sources[0].shape[0]
    run = sum(shares)
    for group in range(groups):
        wides = [
            jnp.concatenate(
                [source[group, tile].astype(F32) for tile in range(source.shape[1])], axis=1
            )
            for source in sources
        ]
        firsts = [0] * len(shares)
        for out in outs:
            for block in range(out.shape[1] // (groups * run)):
                where = group
                if planes:
                    where = (block + group) % planes + planes * (group // planes)
                base = (block * groups + where) * run
                for index, share in enumerate(shares):
                    first = firsts[index]
                    out[:, base : base + share] = wides[index][:, first : first + share]
                    firsts[index] += share
                    base += share


def assemble_tiles(parts, shares, planes, widths):
    rows = parts[0].shape[2]
    return pl.pallas_call(
        functools.partial(assemble_tiles_kernel, shares, planes),
        out_shape=[jax.ShapeDtypeStruct((rows, width), F32) for width in widths],
        compiler_params=pltpu.CompilerParams(vmem_limit_bytes=48 * 2**20),
        cost_estimate=SMALL,
        name="assemble_columns",
    )(*parts)


def assemble_rows_kernel(*refs):
    out = refs[-1]
    base = 0
    for source in refs[:-1]:
        tiles, rows, _ = source.shape
        for tile in range(tiles):
            out[base : base + rows, tile * LANES : (tile + 1) * LANES] = source[tile].astype(F32)
        base += rows


def assemble_rows(parts):
    rows = sum(part.shape[1] for part in parts)
    width = parts[0].shape[0] * LANES
    return pl.pallas_call(
        assemble_rows_kernel,
        out_shape=jax.ShapeDtypeStruct((rows, width), F32),
        compiler_params=pltpu.CompilerParams(vmem_limit_bytes=48 * 2**20),
        cost_estimate=SMALL,
        name="assemble_rows",
    )(*parts)


def shard_gather(value):
    return lax.all_gather(value, "wshard", axis=0, tiled=True)


def shard_scatter(value):
    return lax.psum_scatter(value, "wshard", scatter_dimension=0, tiled=True)


def plain_body(
    tokens,
    starts,
    layer_index,
    gain_mix,
    w_in,
    w_forget,
    bias_forget,
    theta,
    w_gate_out,
    gain_out,
    w_out,
    gain_ffn,
    w_ffgate,
    w_ffup,
    w_down,
    out_grad,
):
    seqs, seq_dev, width = tokens.shape
    rows = seqs * seq_dev
    groups = lax.axis_size("seq")
    planes = lax.axis_size("wshard")
    half = groups // 2
    devices = groups * planes
    place = lax.axis_index("seq")
    floor = layer_index.astype(F32) / LAYERS
    mix_run = w_out.shape[0] // groups
    ffn_run = w_down.shape[0] // groups
    chan = mix_run * planes // 2
    hidden = ffn_run * planes

    def own_columns(array, run):
        count = array.shape[1] // (run * groups)
        column = lax.broadcasted_iota(jnp.int32, (array.shape[1], count * run), 0)
        index = lax.broadcasted_iota(jnp.int32, (array.shape[1], count * run), 1)
        block = index // run
        chosen = column == block * (run * groups) + place * run + (index - block * run)
        return dot(array, chosen.astype(BF), "rc,cj->rj").astype(BF)

    def own_parts(vector):
        count = vector.shape[0] // (mix_run * groups)
        split = vector.reshape(count, groups, mix_run)
        return lax.dynamic_slice_in_dim(split, place, 1, 1).reshape(1, count * mix_run)

    def own_rows(array):
        run = array.shape[0] // groups
        return lax.dynamic_slice_in_dim(array, place * run, run, 0)

    resid_in = tokens.reshape(rows, width).astype(F32)
    scale_in = lax.rsqrt(jnp.mean(resid_in * resid_in, axis=1, keepdims=True) + EPS)
    normed_own = (resid_in * scale_in * gain_mix).astype(BF)
    normed_even, normed_odd = plain_gather(normed_own)
    upstream_own = out_grad.reshape(rows, width)

    rec_w = shard_gather(
        jnp.concatenate(
            [
                own_columns(w_in, mix_run),
                own_columns(w_forget, mix_run),
                own_columns(w_gate_out, mix_run),
            ],
            axis=1,
        )
    )
    out_w = shard_gather(own_rows(w_out))
    ff_w = shard_gather(
        jnp.concatenate([own_columns(w_ffgate, ffn_run), own_columns(w_ffup, ffn_run)], axis=1)
    )
    down_w = shard_gather(own_rows(w_down))

    slots = lax.broadcasted_iota(jnp.int32, (groups, groups), 0)
    sources = lax.broadcasted_iota(jnp.int32, (groups, groups), 1)
    keys = jnp.where(slots < half, 2 * slots, 2 * (slots - half) + 1)
    chosen = ((place ^ keys) == sources).astype(F32)
    marks = starts.astype(F32).reshape(seqs, groups, seq_dev).transpose(1, 0, 2)
    flags = jnp.sum(chosen[:, :, None, None] * marks[None], axis=1)[..., None]
    bias_own = own_parts(bias_forget)
    theta_own = own_parts(theta)
    gain_own = own_parts(gain_out)
    place_one = place.reshape(1)

    def blocks(array):
        return array.reshape(half, seqs, seq_dev, -1)

    pre_even = blocks(dot(normed_even, rec_w, "td,dc->tc"))
    pre_odd = blocks(dot(normed_odd, rec_w, "td,dc->tc"))
    state, gated_even, gated_odd, square = recur_forward(
        place_one, floor, pre_even, pre_odd, flags, bias_own, theta_own, gain_own
    )
    gated_even = gated_even.reshape(half * rows, 2 * chan)
    gated_odd = gated_odd.reshape(half * rows, 2 * chan)

    def mix(gated):
        return dot(gated, out_w, "tc,cd->td").astype(BF)

    square_own = scatter_small(square.reshape(groups, rows))
    scale_own = lax.rsqrt(square_own / width + EPS)
    scale_out = scale_own.reshape(rows, 1)
    branch_mix = scale_out * plain_scatter(mix(gated_even), mix(gated_odd))
    resid = resid_in + branch_mix
    scale_ffn = lax.rsqrt(jnp.mean(resid * resid, axis=1, keepdims=True) + EPS)
    ffn_even, ffn_odd = plain_gather((resid * scale_ffn * gain_ffn).astype(BF))
    scale_all = gather_small(scale_own)
    up_even, up_odd = plain_gather(upstream_own)

    def ffn(normed, upstream):
        ff = dot(normed, ff_w, "td,df->tf")
        ffn_gate, ffn_up = ff[:, :hidden], ff[:, hidden:]
        sig_ffn = jax.nn.sigmoid(ffn_gate)
        silu_ffn = ffn_gate * sig_ffn
        ffn_hidden = (silu_ffn * ffn_up).astype(BF)
        grad_hidden = dot(upstream, down_w, "td,fd->tf")
        grad_gate = grad_hidden * ffn_up * sig_ffn * (1.0 + ffn_gate * (1.0 - sig_ffn))
        grad_up = grad_hidden * silu_ffn
        grad_ff = jnp.concatenate([grad_gate.astype(BF), grad_up.astype(BF)], axis=1)
        return ffn_hidden, grad_ff

    hidden_odd, grad_ff_odd = ffn(ffn_odd, up_odd)
    hidden_even, grad_ff_even = ffn(ffn_even, up_even)
    grad_normed_ffn = plain_scatter(
        dot(grad_ff_even, ff_w, "tf,df->td").astype(BF),
        dot(grad_ff_odd, ff_w, "tf,df->td").astype(BF),
    )
    branch_ffn = plain_scatter(
        dot(hidden_even, down_w, "tf,fd->td").astype(BF),
        dot(hidden_odd, down_w, "tf,fd->td").astype(BF),
    )
    result = (resid + branch_ffn).astype(BF)

    scaled_ffn = grad_normed_ffn * gain_ffn
    grad_resid = (
        upstream_own.astype(F32)
        + scale_ffn * scaled_ffn
        - resid * scale_ffn**3 * jnp.mean(scaled_ffn * resid, axis=1, keepdims=True)
    )
    grad_gain_ffn = jnp.sum(grad_normed_ffn * resid * scale_ffn, axis=0)
    grad_branch_own = grad_resid.astype(BF)
    overlap = jnp.sum(grad_branch_own.astype(F32) * branch_mix, axis=1)
    term_all = gather_small((scale_out[:, 0] ** 2 * overlap / width)[None])
    branch_even, branch_odd = plain_gather(grad_branch_own)
    grad_gated_even = blocks(dot(branch_even, out_w, "td,cd->tc"))
    grad_gated_odd = blocks(dot(branch_odd, out_w, "td,cd->tc"))

    shape_one = (groups, seqs, seq_dev, 1)
    grad_even, grad_odd, scaled_even, scaled_odd, sum_bias, sum_theta, sum_gain = recur_backward(
        place_one,
        floor,
        pre_even,
        pre_odd,
        flags,
        bias_own,
        theta_own,
        gain_own,
        state,
        grad_gated_even,
        grad_gated_odd,
        scale_all.reshape(shape_one),
        term_all.reshape(shape_one),
    )
    grad_even = grad_even.reshape(half * rows, 5 * chan)
    grad_odd = grad_odd.reshape(half * rows, 5 * chan)
    grad_normed_in = plain_scatter(
        dot(grad_even, rec_w, "tc,dc->td").astype(BF),
        dot(grad_odd, rec_w, "tc,dc->td").astype(BF),
    )
    scaled_in = grad_normed_in * gain_mix
    grad_tokens = (
        grad_resid
        + scale_in * scaled_in
        - resid_in * scale_in**3 * jnp.mean(scaled_in * resid_in, axis=1, keepdims=True)
    ).astype(BF)
    grad_gain_mix = jnp.sum(grad_normed_in * resid_in * scale_in, axis=0)

    def pair_dot(left, right, form):
        return dot(left[0], right[0], form) + dot(left[1], right[1], form)

    def to_owner(grad):
        run = grad.shape[0] // devices
        part = grad.astype(BF).reshape(groups, planes, run, -1).transpose(1, 0, 2, 3)
        part = shard_scatter(part.reshape(grad.shape)).reshape(groups, run, -1)
        return lax.all_to_all(part, "seq", split_axis=0, concat_axis=0, tiled=True)

    def columns(part, run):
        source, count, cols = part.shape
        split = part.reshape(source, count, cols // run, run)
        return split.transpose(1, 2, 0, 3).reshape(count, -1).astype(F32)

    scaled_even = scaled_even.reshape(half * rows, 2 * chan)
    scaled_odd = scaled_odd.reshape(half * rows, 2 * chan)
    ff_grad = to_owner(
        pair_dot((ffn_even, ffn_odd), (grad_ff_even, grad_ff_odd), "td,tf->df")
    )
    grad_w_ffgate = columns(ff_grad[..., :hidden], ffn_run)
    grad_w_ffup = columns(ff_grad[..., hidden:], ffn_run)
    rec_grad = to_owner(pair_dot((normed_even, normed_odd), (grad_even, grad_odd), "td,tc->dc"))
    grad_w_in = columns(rec_grad[..., : 2 * chan], mix_run)
    grad_w_forget = columns(rec_grad[..., 2 * chan : 3 * chan], mix_run)
    grad_w_gate = columns(rec_grad[..., 3 * chan :], mix_run)

    pairs = [
        (s * planes + w, w * groups + s) for s in range(groups) for w in range(planes)
    ]

    def rows_to_owner(grad):
        part = shard_scatter(grad.astype(BF))
        return lax.ppermute(part, ("seq", "wshard"), pairs).astype(F32)

    grad_w_down = rows_to_owner(
        pair_dot((hidden_even, hidden_odd), (up_even, up_odd), "tf,td->fd")
    )
    grad_w_out = rows_to_owner(
        pair_dot((scaled_even, scaled_odd), (branch_even, branch_odd), "tc,td->cd")
    )

    def spread(part):
        count = part.shape[1] // mix_run
        zero = jnp.zeros((count, groups, mix_run), F32)
        zero = lax.dynamic_update_slice(zero, part.reshape(count, 1, mix_run), (0, place, 0))
        return zero.reshape(-1)

    pieces = [
        spread(sum_bias),
        spread(sum_theta),
        spread(sum_gain),
        grad_gain_ffn,
        grad_gain_mix,
        jnp.stack(
            [
                jnp.sum(resid_in * resid_in),
                jnp.sum(branch_mix * branch_mix),
                jnp.sum(branch_ffn * branch_ffn),
            ]
        ),
    ]
    sums = sum_seq(jnp.concatenate(pieces))
    sums = sum_tree([sums, *others(sums)])
    cuts = []
    offset = 0
    for piece in pieces:
        cuts.append(sums[offset : offset + piece.shape[0]])
        offset += piece.shape[0]
    grad_bias, grad_theta, grad_gain_out, grad_gain_ffn, grad_gain_mix, squares = cuts
    rms_values = jnp.sqrt(squares / (rows * width * devices))
    return (
        result.reshape(seqs, seq_dev, width),
        grad_tokens.reshape(seqs, seq_dev, width),
        grad_gain_mix,
        grad_w_in,
        grad_w_forget,
        grad_bias,
        grad_theta,
        grad_w_gate,
        grad_gain_out,
        grad_w_out,
        grad_gain_ffn,
        grad_w_ffgate,
        grad_w_ffup,
        grad_w_down,
        rms_values,
    )


def body(
    tokens,
    starts,
    layer_index,
    gain_mix,
    w_in,
    w_forget,
    bias_forget,
    theta,
    w_gate_out,
    gain_out,
    w_out,
    gain_ffn,
    w_ffgate,
    w_ffup,
    w_down,
    out_grad,
):
    seqs, seq_dev, width = tokens.shape
    rows = seqs * seq_dev
    groups = lax.axis_size("seq")
    planes = lax.axis_size("wshard")
    half = groups // 2
    devices = groups * planes
    mix_run = w_out.shape[0] // groups
    ffn_run = w_down.shape[0] // groups
    chan = mix_run * planes // 2
    shares = (ffn_run * 5 // 11, ffn_run - ffn_run * 5 // 11)
    if not (
        groups == 8
        and groups % planes == 0
        and seqs == 2
        and chan % LANES == 0
        and all(2 * planes * share % LANES == 0 and share % 16 == 0 for share in shares)
    ):
        return plain_body(
            tokens,
            starts,
            layer_index,
            gain_mix,
            w_in,
            w_forget,
            bias_forget,
            theta,
            w_gate_out,
            gain_out,
            w_out,
            gain_ffn,
            w_ffgate,
            w_ffup,
            w_down,
            out_grad,
        )
    place = lax.axis_index("seq")
    floor = layer_index.astype(F32) / LAYERS
    place_one = place.reshape(1)

    first_bit, second_bit = chip_bits()

    def turned(block):
        return lax.rem(block + place, planes) + planes * (place // planes)

    def own_columns(array, run, first, count, where):
        blocks = array.shape[1] // (run * groups)
        column = lax.broadcasted_iota(jnp.int32, (array.shape[1], blocks * count), 0)
        index = lax.broadcasted_iota(jnp.int32, (array.shape[1], blocks * count), 1)
        block = index // count
        wanted = (block * groups + where(block)) * run + first + (index - block * count)
        return dot(array, (column == wanted).astype(BF), "rc,cj->rj").astype(BF)

    def own_parts(vector):
        count = vector.shape[0] // (mix_run * groups)
        split = vector.reshape(count, groups, mix_run)
        return lax.dynamic_slice_in_dim(split, place, 1, 1).reshape(1, count * mix_run)

    def own_rows(array, first, count, where):
        run = array.shape[0] // groups
        return lax.dynamic_slice_in_dim(array, where * run + first, count, 0)

    rec_own = jnp.concatenate(
        [
            own_columns(array, mix_run, 0, mix_run, lambda block: place)
            for array in (w_in, w_forget, w_gate_out)
        ],
        axis=1,
    )
    packs = [pack([rec_own[None], own_rows(w_out, 0, mix_run, place)[None]])]
    first = 0
    for share in shares:
        ff_own = jnp.concatenate(
            [own_columns(array, ffn_run, first, share, turned) for array in (w_ffgate, w_ffup)], axis=1
        )
        packs.append(pack([ff_own[None], own_rows(w_down, first, share, turned(lax.axis_index("wshard")))[None]]))
        first += share
    rec_packed = gather_packed(packs[0])

    upstream_own = out_grad.reshape(rows, width)
    up_stage = gather_first(upstream_own)
    tokens_, up_stage = tied(after(tokens, packs[0]), up_stage)
    resid_in = tokens_.reshape(rows, width).astype(F32)
    scale_in = lax.rsqrt(jnp.mean(resid_in * resid_in, axis=1, keepdims=True) + EPS)
    normed_own = (resid_in * scale_in * gain_mix).astype(BF)
    normed_stage = gather_first(normed_own)
    normed_stage, packs[1], packs[2] = tied(normed_stage, packs[1], packs[2])
    normed_far = gather_far(normed_own, normed_stage)
    normed_even = (normed_own, *normed_stage, *normed_far)
    normed_odd = cross(normed_even)
    up_far = gather_far(upstream_own, up_stage)
    packed = [gather_packed(item) for item in packs[1:]]

    slots = lax.broadcasted_iota(jnp.int32, (groups, groups), 0)
    sources = lax.broadcasted_iota(jnp.int32, (groups, groups), 1)
    keys = jnp.where(slots < half, 2 * slots, 2 * (slots - half) + 1)
    chosen = ((place ^ keys) == sources).astype(F32)
    marks = starts.astype(F32).reshape(seqs, groups, seq_dev).transpose(1, 0, 2)
    flags = jnp.sum(chosen[:, :, None, None] * marks[None], axis=1)[..., None]
    bias_own = own_parts(bias_forget)
    theta_own = own_parts(theta)
    gain_own = own_parts(gain_out)

    pre_even, pre_odd, state, square, *mixes = mix_forward(
        place_one,
        floor,
        normed_even,
        normed_odd,
        rec_packed,
        flags,
        bias_own,
        theta_own,
        gain_own,
    )
    mixes = tuple(item.reshape(rows, width) for item in mixes)
    mix_even, mix_odd = mixes[:half], mixes[half:]
    mix_odd, up_far = tied(mix_odd, up_far)
    up_even = (upstream_own, *up_stage, *up_far)
    square = shrink(square.reshape(groups, rows), 1)
    mix_crossed = cross(mix_odd)
    mix_far = scatter_far(mix_even[3], mix_crossed[3])
    square_next = shrink(square, second_bit)
    mix_far, square_next = tied(mix_far, square_next)
    mix_near = scatter_near(mix_even[1:3], mix_crossed[1:3], mix_far)
    up_odd = cross(up_even)
    square_own = shrink(square_next, first_bit)
    scale_own = lax.rsqrt(square_own / width + EPS)
    scale_out = scale_own.reshape(rows, 1)
    branch_mix = scale_out * scatter_sum(mix_even[0], mix_crossed[0], mix_near)
    resid = resid_in + branch_mix
    scale_ffn = lax.rsqrt(jnp.mean(resid * resid, axis=1, keepdims=True) + EPS)
    ffn_own = (resid * scale_ffn * gain_ffn).astype(BF)
    ffn_stage = gather_first(ffn_own)
    ffn_far = gather_far(ffn_own, ffn_stage)
    scale_all = gather_small(scale_own)

    cols = [2 * planes * share for share in shares]

    def block(normed, up, slot):
        cut = slice(slot, slot + 1) if slot < 3 else slice(3, None)
        return normed[cut], up[cut]

    def grouped(blocks, out):
        return (
            [piece for item in blocks for piece in item[0]],
            [piece for item in blocks for piece in item[1]],
            out[1],
            out[0],
        )

    def gradients(groups_, turn):
        return grads_call(groups, planes, turn, groups_)

    ffn_near = (ffn_own, *ffn_stage)
    even_blocks = [block(ffn_near, up_even, slot) for slot in range(3)]
    even_out = ffn_call(even_blocks, packed[0], cols[0], fills=True)
    odd_near = cross(ffn_near)
    odd_blocks = [block(odd_near, up_odd, slot) for slot in range(3)]
    odd_out = ffn_call(odd_blocks, packed[0], cols[0], fills=True)
    ffn_far, odd_out = tied(ffn_far, odd_out)
    odd_far = cross(ffn_far)
    ffn_even = (*ffn_near, *ffn_far)
    ffn_odd = (*odd_near, *odd_far)
    far_blocks = [block(ffn_even, up_even, 3), block(ffn_odd, up_odd, 3)]
    far_out = ffn_call(far_blocks, packed[0], cols[0])
    firsts = [
        (even_blocks, even_out),
        (odd_blocks, odd_out),
        (far_blocks, far_out),
    ]
    ff_grads = [gradients([grouped(*item) for item in firsts], place_one)]
    even_place = [(0, 0), (0, rows), (0, 2 * rows), (2, 0)]
    odd_place = [(1, 0), (1, rows), (1, 2 * rows), (2, rows)]

    def base(place_):
        return firsts[place_[0]][1][2], place_[1]

    packed[1], ff_grads[0], scale_all, _ = tied(packed[1], ff_grads[0], scale_all, far_out)
    far_blocks = [block(ffn_odd, up_odd, 3), block(ffn_even, up_even, 3)]
    far_out = ffn_call(far_blocks, packed[1], cols[1], [base(odd_place[3]), base(even_place[3])])
    (far_crossed,) = cross([far_out[2]])
    back_far = scatter_far(far_out[3], far_crossed)
    near_packed, _ = tied(packed[1], far_crossed)
    near_blocks = [block(ffn_odd, up_odd, slot) for slot in (1, 2)]
    near_blocks += [block(ffn_even, up_even, slot) for slot in (1, 2)]
    near_out = ffn_call(
        near_blocks,
        near_packed,
        cols[1],
        [base(odd_place[1]), base(odd_place[2]), base(even_place[1]), base(even_place[2])],
        True,
    )
    back_far, near_out = tied(back_far, near_out)
    near_crossed = cross(near_out[2:4])
    back_sums = near_sums(near_out[4:6], near_crossed, back_far)
    back_near = to_neighbours(back_sums)
    own_packed, _ = tied(packed[1], back_sums)
    own_blocks = [block(ffn_odd, up_odd, 0), block(ffn_even, up_even, 0)]
    own_out = ffn_call(
        own_blocks, own_packed, cols[1], [base(odd_place[0]), base(even_place[0])], True
    )
    (own_crossed,) = cross([own_out[2]])
    seconds = [(far_blocks, far_out), (near_blocks, near_out), (own_blocks, own_out)]
    ff_grads.append(gradients([grouped(*item) for item in seconds], place_one))
    back_near, ff_grads[1], own_crossed = tied(back_near, ff_grads[1], own_crossed)
    grad_normed_ffn = scatter_sum(own_out[3], own_crossed, back_near)

    scaled_ffn = grad_normed_ffn * gain_ffn
    grad_resid = (
        upstream_own.astype(F32)
        + scale_ffn * scaled_ffn
        - resid * scale_ffn**3 * jnp.mean(scaled_ffn * resid, axis=1, keepdims=True)
    )
    grad_gain_ffn = jnp.sum(grad_normed_ffn * resid * scale_ffn, axis=0)
    grad_branch_own = grad_resid.astype(BF)
    overlap = jnp.sum(grad_branch_own.astype(F32) * branch_mix, axis=1)
    term_own = (scale_out[:, 0] ** 2 * overlap / width)[None]
    branch_stage = gather_first(grad_branch_own)
    term_near = grow(grow(term_own, 1), first_bit)
    hiddens = [[item[1][0] for item in firsts], [item[1][0] for item in seconds]]
    hiddens[1][2] = after(hiddens[1][2], grad_branch_own)
    odd_second = [(2, 0), (1, 0), (1, rows), (0, 0)]
    even_second = [(2, rows), (1, 2 * rows), (1, 3 * rows), (0, rows)]
    result_odd = result_call(
        hiddens, tuple(zip(odd_place, odd_second)), packed, rows, width
    )
    result_even = result_call(
        hiddens, tuple(zip(even_place, even_second)), packed, rows, width
    )
    branch_stage, result_even, result_odd, term_near = tied(
        branch_stage, tuple(result_even), tuple(result_odd), term_near
    )
    branch_far = gather_far(grad_branch_own, branch_stage)
    result_crossed = cross(result_odd)
    term_all = grow(term_near, second_bit)
    branch_far, result_crossed, term_all = tied(branch_far, result_crossed, term_all)
    result_stage = scatter_first(joints(result_even, result_crossed))
    term_all = slot_rows(term_all)
    branch_even = (grad_branch_own, *branch_stage, *branch_far)
    branch_odd = cross(branch_even)

    mix_pairs = [(s * planes + w, w * groups + s) for s in range(groups) for w in range(planes)]
    down_pairs = []
    for s in range(groups):
        for w in range(planes):
            owner = (w - s) % planes * (groups // planes) + s // planes
            down_pairs.append((s * planes + w, owner * planes + w))

    scattered = [scatter_packed(grads) for grads in ff_grads]

    def owned(part, count, pairs):
        lines = count * width // (planes * LANES)
        tiles = part[:lines].reshape(groups, -1, LANES)
        tiles = lax.all_to_all(tiles, "seq", split_axis=0, concat_axis=0, tiled=True)
        tiles = tiles.reshape(groups, count // LANES, -1, LANES)
        moved = lax.ppermute(part[lines:], ("seq", "wshard"), pairs)
        return tiles, moved.reshape(width // LANES, -1, LANES)

    shape_one = (groups, seqs, seq_dev, 1)
    (
        grad_even,
        grad_odd,
        scaled_even,
        scaled_odd,
        sum_bias,
        sum_theta,
        sum_gain,
        *backs,
    ) = mix_backward(
        place_one,
        floor,
        rec_packed,
        pre_even,
        pre_odd,
        flags,
        bias_own,
        theta_own,
        gain_own,
        state,
        scale_all.reshape(shape_one),
        term_all.reshape(shape_one),
        branch_even,
        branch_odd,
    )
    grad_even = grad_even.reshape(half * rows, 5 * chan)
    grad_odd = grad_odd.reshape(half * rows, 5 * chan)
    scaled_even = scaled_even.reshape(half * rows, 2 * chan)
    scaled_odd = scaled_odd.reshape(half * rows, 2 * chan)
    backs = tuple(item.reshape(rows, width) for item in backs)
    grad_even, result_stage, scattered = tied(grad_even, result_stage, scattered)
    rec_grads = gradients(
        [
            (normed_even, branch_even, grad_even, scaled_even),
            (normed_odd, branch_odd, grad_odd, scaled_odd),
        ],
        jnp.zeros((1,), jnp.int32),
    )
    back_even, back_odd = backs[:half], backs[half:]
    back_crossed = cross(back_odd)
    back_crossed, rec_grads = tied(back_crossed, rec_grads)
    back_far = scatter_far(back_even[3], back_crossed[3])
    branch_ffn = scatter_last(result_even, result_crossed, after(result_stage, rec_grads))
    first_tiles, first_lines = owned(scattered[0], cols[0], down_pairs)
    second_tiles, second_lines = owned(scattered[1], cols[1], down_pairs)
    back_far, branch_ffn, first_tiles, second_tiles = tied(
        back_far, branch_ffn, first_tiles, second_tiles
    )
    back_near = scatter_near(back_even[1:3], back_crossed[1:3], back_far)
    back_near, rec_part = tied(back_near, scatter_packed(rec_grads))
    grad_normed_in = scatter_sum(back_even[0], back_crossed[0], back_near)
    rec_tiles, rec_lines = owned(rec_part, 5 * chan, mix_pairs)
    result = (resid + branch_ffn).astype(BF)
    scaled_in = grad_normed_in * gain_mix
    grad_tokens = (
        grad_resid
        + scale_in * scaled_in
        - resid_in * scale_in**3 * jnp.mean(scaled_in * resid_in, axis=1, keepdims=True)
    ).astype(BF)
    grad_gain_mix = jnp.sum(grad_normed_in * resid_in * scale_in, axis=0)

    hidden_all = w_ffgate.shape[1]
    rec_widths = (w_in.shape[1], w_forget.shape[1], w_gate_out.shape[1])
    grad_w_ffgate, grad_w_ffup = assemble_tiles(
        [first_tiles, second_tiles], shares, planes, (hidden_all, hidden_all)
    )
    grad_w_down = assemble_rows([first_lines, second_lines])

    def spread(part):
        count = part.shape[1] // mix_run
        zero = jnp.zeros((count, groups, mix_run), F32)
        zero = lax.dynamic_update_slice(zero, part.reshape(count, 1, mix_run), (0, place, 0))
        return zero.reshape(-1)

    pieces = [
        spread(sum_bias),
        spread(sum_theta),
        spread(sum_gain),
        grad_gain_ffn,
        grad_gain_mix,
        jnp.stack(
            [
                jnp.sum(resid_in * resid_in),
                jnp.sum(branch_mix * branch_mix),
                jnp.sum(branch_ffn * branch_ffn),
            ]
        ),
    ]
    sums, rec_tiles, rec_lines = tied(sum_seq(jnp.concatenate(pieces)), rec_tiles, rec_lines)
    sums = sum_tree([sums, *others(sums)])
    grad_w_out = assemble_rows([rec_lines])
    grad_w_in, grad_w_forget, grad_w_gate = assemble_tiles([rec_tiles], (mix_run,), 0, rec_widths)
    cuts = []
    offset = 0
    for piece in pieces:
        cuts.append(sums[offset : offset + piece.shape[0]])
        offset += piece.shape[0]
    grad_bias, grad_theta, grad_gain_out, grad_gain_ffn, grad_gain_mix, squares = cuts
    rms_values = jnp.sqrt(squares / (rows * width * devices))
    return (
        result.reshape(seqs, seq_dev, width),
        grad_tokens.reshape(seqs, seq_dev, width),
        grad_gain_mix,
        grad_w_in,
        grad_w_forget,
        grad_bias,
        grad_theta,
        grad_w_gate,
        grad_gain_out,
        grad_w_out,
        grad_gain_ffn,
        grad_w_ffgate,
        grad_w_ffup,
        grad_w_down,
        rms_values,
    )


def solution(mesh):
    whole = P()
    rowed = P("wshard", None)
    stream = P("wshard", "seq", None)
    owned = P(("seq", "wshard"), None)
    return jax.shard_map(
        body,
        mesh=mesh,
        in_specs=(
            stream,
            rowed,
            whole,
            whole,
            rowed,
            rowed,
            whole,
            whole,
            rowed,
            whole,
            rowed,
            whole,
            rowed,
            rowed,
            rowed,
            stream,
        ),
        out_specs=(
            stream,
            stream,
            whole,
            owned,
            owned,
            whole,
            whole,
            owned,
            whole,
            owned,
            whole,
            owned,
            owned,
            owned,
            whole,
        ),
        check_vma=False,
    )
```
